512 devices in a mesh: tile: 64 (over x, z_lo, core), depth: 8 (over y, z_hi).
Axes of the slice: x: 4, y: 4, z: 16 (z_hi: 2, z_lo: 8; z = z_hi * 8 + z_lo), core: 2. Of those that a mesh axis runs over, the one named last changes fastest.
Arguments:
- displacement: float32 [128, 1024, 1024], P('depth', 'tile'), may hold values from -6 to 6
- damage: float32 [128, 1024, 1024], P('depth', 'tile'), may hold values from 0 to 0.6
- modulus: float32 [128, 1024, 1024], P('depth', 'tile'), may hold values from 0.5 to 2
- toughness: float32 [128, 1024, 1024], P('depth', 'tile'), may hold values from 0.5 to 2
- pressure: float32 [1024, 1024], P('tile'), may hold values from -6 to 6
- crack_mask: int32 [1024, 1024], P('tile'), may hold values 0 or 1
- wells: int32 [16], replicated, may hold values from 0 to 1048575
- rates: float32 [16], replicated, may hold values from 0.5 to 2
Outputs:
- new_pressure: float32 [1024, 1024], P('tile')
The draws below stay inside these ranges and needn't reach their ends.
All inputs are finite; a program needn't handle non-finite values. No bound on the sum of `crack_mask` on one device may be relied on, other than what follows from the above.
Results may differ from the reference program's by a relative error of at most 0.00002.
Values sent between devices are 32-bit elements; how exact they have to be, the bound alone decides.
No kernel may reach another device: no remote copies, remote signals or barrier semaphores. Data moves between devices by JAX's collectives and lax.ppermute only.
A program may use at most 64 MiB of HBM per device.

```python
import math
import jax
import jax.numpy as jnp

NY = 1024
WELLS = 16
NX = 1024
NZ = 128


def set_ends(result, own_key, least, top_value):
    longest = result.shape.index(max(result.shape))
    spots = []
    for shift in (0, 1):
        where = [jax.random.randint(jax.random.fold_in(own_key, axis), (), 0, length) for axis, length in enumerate(result.shape)]
        where[longest] = (where[longest] + shift) % result.shape[longest]
        spots.append(tuple(where))
    return result.at[spots[0]].set(least).at[spots[1]].set(top_value)


def block_scale(stream_key, extent, cuts, least, high):
    level = 1.0
    for axis_at, shards_of in cuts:
        steps = jax.random.uniform(jax.random.fold_in(jax.random.fold_in(stream_key, 6), axis_at), (shards_of,), jnp.float32, least / len(cuts), high / len(cuts))
        level = level * jnp.repeat(jnp.exp(steps), extent[axis_at] // shards_of).reshape((-1,) + (1,) * (len(extent) - 1 - axis_at))
    return level


def scatter_about(own_key, extent, deviation, bound, pieces=(), dtype=jnp.bfloat16):
    result = deviation * jax.random.normal(own_key, extent, jnp.float32)
    if pieces:
        result = result * block_scale(own_key, extent, pieces, -0.22, 0.18)
    return jnp.clip(result, -bound, bound).astype(dtype)


def setup_inputs(seed: int = 0) -> dict:
    key_list = jax.random.split(jax.random.key(seed), 9)
    return {
        "displacement": scatter_about(key_list[0], (NZ, NX, NY), 1.0, 6.0, ((0, 8), (1, 64)), jnp.float32),
        "damage": jnp.clip(0.6 * jax.random.uniform(key_list[1], (NZ, NX, NY), jnp.float32) ** block_scale(key_list[1], (NZ, NX, NY), ((0, 8), (1, 64)), -0.2, 0.2), 0.0, 0.6),
        "modulus": jnp.clip(jnp.exp(math.log(2.0) - 1.3862944 * jax.random.uniform(key_list[2], (NZ, NX, NY), jnp.float32) ** block_scale(key_list[2], (NZ, NX, NY), ((0, 8), (1, 64)), -0.2, 0.2)), 0.5, 2.0),
        "toughness": jnp.clip(jnp.exp(math.log(2.0) - 1.3862944 * jax.random.uniform(key_list[3], (NZ, NX, NY), jnp.float32) ** block_scale(key_list[3], (NZ, NX, NY), ((0, 8), (1, 64)), -0.2, 0.2)), 0.5, 2.0),
        "pressure": scatter_about(key_list[4], (NX, NY), 1.0, 6.0, ((0, 64),), jnp.float32),
        "crack_mask": set_ends((jax.random.randint(key_list[5], (NX, NY), 0, 4) < 3).astype(jnp.int32), jax.random.fold_in(key_list[5], 1), 0, 1),
        "wells": set_ends(jax.random.randint(key_list[6], (WELLS,), 0, NX * NY), jax.random.fold_in(key_list[6], 1), 0, (NX * NY) - 1).astype(jnp.int32),
        "rates": jnp.clip(jnp.exp(jax.random.uniform(key_list[7], (WELLS,), jnp.float32, math.log(0.5), math.log(2.0))), 0.5, 2.0),
    }


def sides(padded):
    return [padded[2:, 1:-1, 1:-1], padded[:-2, 1:-1, 1:-1], padded[1:-1, 2:, 1:-1],
            padded[1:-1, :-2, 1:-1], padded[1:-1, 1:-1, 2:], padded[1:-1, 1:-1, :-2]]


def flat_sides(padded):
    return [padded[2:, 1:-1], padded[:-2, 1:-1], padded[1:-1, 2:], padded[1:-1, :-2]]


def plane_sweep(p_pad, k_pad, anchor, source, trans):
    coef = jnp.zeros_like(trans)
    flow = jnp.zeros_like(trans)
    for k_side, p_side in zip(flat_sides(k_pad), flat_sides(p_pad)):
        face = 0.5 * (trans + k_side)
        coef = coef + face
        flow = flow + face * p_side
    return (anchor + source + flow) / (1.0 + coef)


def reference(displacement, damage, modulus, toughness, pressure, crack_mask, wells, rates):
    stiff = ((1.0 - damage) ** 2 + 0.001) * modulus
    mask_f = crack_mask.astype(jnp.float32)
    layer = jnp.arange(NZ) == NZ // 2
    load = 4.0 * mask_f * pressure
    force = jnp.where(layer[:, None, None], load[None, :, :], jnp.float32(0.0))
    u_pad = jnp.pad(displacement, 1)
    c_pad = jnp.pad(stiff, 1)
    coef = jnp.zeros_like(stiff)
    flux = jnp.zeros_like(stiff)
    for c_side, u_side in zip(sides(c_pad), sides(u_pad)):
        face = 0.5 * (stiff + c_side)
        coef = coef + face
        flux = flux + face * (u_side - displacement)
    moved = displacement + 0.8 * (force + flux) / coef
    m_pad = jnp.pad(moved, 1)
    energy = jnp.zeros_like(moved)
    for m_side in sides(m_pad):
        energy = energy + (m_side - moved) ** 2
    energy = 0.25 * modulus * energy
    d_pad = jnp.pad(damage, 1)
    beside_all = jnp.zeros_like(damage)
    for d_side in sides(d_pad):
        beside_all = beside_all + d_side
    trial = (2.0 * energy + toughness * beside_all) / (7.0 * toughness + 2.0 * energy)
    new_damage = jnp.maximum(damage, trial)
    aperture = 0.5 + (4.0 / NZ) * jnp.sum(new_damage * moved * moved, axis=0)
    trans = mask_f * aperture ** 3
    source = 4.0 * jnp.zeros((NX * NY,), jnp.float32).at[wells].add(rates).reshape(NX, NY)
    k_pad = jnp.pad(trans, 1)
    level = pressure
    for sweep_step in range(2):
        level = plane_sweep(jnp.pad(level, 1), k_pad, pressure, source, trans)
    return level
```

```python
import jax
import jax.numpy as jnp
from jax import lax
from jax.sharding import PartitionSpec as P


def padded_2(cells, sides, width):
    for axis, dim in sides:
        count = lax.axis_size(axis)
        ends = count - 1
        head = lax.slice_in_dim(cells, 0, width, axis=dim)
        tail = lax.slice_in_dim(cells, cells.shape[dim] - width, cells.shape[dim], axis=dim)
        cells = jnp.concatenate(
            [
                lax.ppermute(tail, axis, [(i, (i + 1) % count) for i in range(ends)]),
                cells,
                lax.ppermute(head, axis, [((i + 1) % count, i) for i in range(ends)]),
            ],
            axis=dim,
        )
    return cells


def sides(padded):
    return [
        padded[2:, 1:-1, 1:-1],
        padded[:-2, 1:-1, 1:-1],
        padded[1:-1, 2:, 1:-1],
        padded[1:-1, :-2, 1:-1],
        padded[1:-1, 1:-1, 2:],
        padded[1:-1, 1:-1, :-2],
    ]


def flat_sides(padded):
    return [padded[2:, 1:-1], padded[:-2, 1:-1], padded[1:-1, 2:], padded[1:-1, :-2]]


def pad_last(stacked):
    widths = [(0, 0)] * (stacked.ndim - 1) + [(1, 1)]
    return jnp.pad(stacked, widths)


def plane_sweep(p_pad, k_pad, anchor, source, trans):
    coef = jnp.zeros_like(trans)
    flow = jnp.zeros_like(trans)
    for k_side, p_side in zip(flat_sides(k_pad), flat_sides(p_pad)):
        face = 0.5 * (trans + k_side)
        coef = coef + face
        flow = flow + face * p_side
    return (anchor + source + flow) / (1.0 + coef)


def well_source(wells, rates, row_start, rows, cols, width):
    row_ids = row_start + jnp.arange(rows, dtype=jnp.int32)
    col_ids = jnp.arange(cols, dtype=jnp.int32)
    flat = row_ids[:, None] * width + col_ids[None, :]
    hit = flat[:, :, None] == wells[None, None, :]
    return 4.0 * jnp.sum(jnp.where(hit, rates[None, None, :], jnp.float32(0.0)), axis=-1)


def butterfly_sum(part, axis):
    count = lax.axis_size(axis)
    step = 1
    while step < count:
        pairs = [(i, i ^ step) for i in range(count)]
        part = part + lax.ppermute(part, axis, pairs)
        step *= 2
    return part


def relax_step(u_pad, c_pad, center_u, center_c):
    coef = jnp.zeros_like(center_c)
    flux = jnp.zeros_like(center_c)
    for c_side, u_side in zip(sides(c_pad), sides(u_pad)):
        face = 0.5 * (center_c + c_side)
        coef = coef + face
        flux = flux + face * (u_side - center_u)
    return (coef, flux)


def on_device(displacement, damage, modulus, toughness, pressure, crack_mask, wells, rates):
    depth_cells, tile_cells, width = displacement.shape
    total_depth = depth_cells * lax.axis_size("depth")
    depth_start = lax.axis_index("depth") * depth_cells
    tile_start = lax.axis_index("tile") * tile_cells
    stiff = ((1.0 - damage) ** 2 + 0.001) * modulus
    mask_f = crack_mask.astype(jnp.float32)
    layer = depth_start + jnp.arange(depth_cells, dtype=jnp.int32) == total_depth // 2
    load = 4.0 * mask_f * pressure
    force = jnp.where(layer[:, None, None], load[None, :, :], jnp.float32(0.0))
    framed = pad_last(
        padded_2(jnp.stack([displacement, stiff, damage]), (("depth", 1), ("tile", 2)), 1)
    )
    u_pad, c_pad, d_pad = (framed[0], framed[1], framed[2])
    coef, flux = relax_step(u_pad, c_pad, displacement, stiff)
    moved = displacement + 0.8 * (force + flux) / coef
    m_pad = pad_last(padded_2(moved, (("depth", 0), ("tile", 1)), 1))
    energy = jnp.zeros_like(moved)
    for m_side in sides(m_pad):
        energy = energy + (m_side - moved) ** 2
    energy = 0.25 * modulus * energy
    beside_all = jnp.zeros_like(damage)
    for d_side in sides(d_pad):
        beside_all = beside_all + d_side
    trial = (2.0 * energy + toughness * beside_all) / (7.0 * toughness + 2.0 * energy)
    new_damage = jnp.maximum(damage, trial)
    partial_open = 4.0 / total_depth * jnp.sum(new_damage * moved * moved, axis=0)
    aperture = 0.5 + butterfly_sum(partial_open, "depth")
    trans = mask_f * aperture**3
    source = well_source(wells, rates, tile_start, tile_cells, width, width)
    rimmed = pad_last(padded_2(jnp.stack([trans, pressure]), (("tile", 1),), 1))
    k_pad = rimmed[0]
    level = plane_sweep(rimmed[1], k_pad, pressure, source, trans)
    level_pad = pad_last(padded_2(level, (("tile", 0),), 1))
    return plane_sweep(level_pad, k_pad, pressure, source, trans)


def solution(mesh):
    return jax.shard_map(
        on_device,
        mesh=mesh,
        in_specs=(
            P("depth", "tile", None),
            P("depth", "tile", None),
            P("depth", "tile", None),
            P("depth", "tile", None),
            P("tile", None),
            P("tile", None),
            P(),
            P(),
        ),
        out_specs=P("tile", None),
        check_vma=False,
    )
```

```python
import jax
import jax.numpy as jnp
from jax import lax
from jax.sharding import PartitionSpec as P


def halo_swap(lo_face, hi_face, axis):
    count = lax.axis_size(axis)
    even = lax.axis_index(axis) % 2 == 0
    pairs_a = [(i, i ^ 1) for i in range(count)]
    pairs_b = [(i, i + 1) for i in range(1, count - 1, 2)] + [(i + 1, i) for i in range(1, count - 1, 2)]
    got_a = lax.ppermute(jnp.where(even, hi_face, lo_face), axis, pairs_a)
    got_b = lax.ppermute(jnp.where(even, lo_face, hi_face), axis, pairs_b)
    return jnp.where(even, got_b, got_a), jnp.where(even, got_a, got_b)


def butterfly_sum(part, axis):
    count = lax.axis_size(axis)
    order = [1 << k for k in range(1, count.bit_length() - 1)] + [1]
    for step in order:
        pairs = [(i, i ^ step) for i in range(lax.axis_size(axis))]
        part = part + lax.ppermute(part, axis, pairs)
    return part


def pad_last(stacked):
    widths = [(0, 0)] * (stacked.ndim - 1) + [(1, 1)]
    return jnp.pad(stacked, widths)


def flat_sides(padded):
    return [padded[2:, 1:-1], padded[:-2, 1:-1], padded[1:-1, 2:], padded[1:-1, :-2]]


def plane_sweep(p_pad, k_pad, anchor, source, trans):
    coef = jnp.zeros_like(trans)
    flow = jnp.zeros_like(trans)
    for k_side, p_side in zip(flat_sides(k_pad), flat_sides(p_pad)):
        face = 0.5 * (trans + k_side)
        coef = coef + face
        flow = flow + face * p_side
    return (anchor + source + flow) / (1.0 + coef)


def well_source(wells, rates, row_start, rows, cols, width):
    row_ids = row_start + jnp.arange(rows, dtype=jnp.int32)
    col_ids = jnp.arange(cols, dtype=jnp.int32)
    flat = row_ids[:, None] * width + col_ids[None, :]
    hit = flat[:, :, None] == wells[None, None, :]
    return 4.0 * jnp.sum(jnp.where(hit, rates[None, None, :], jnp.float32(0.0)), axis=-1)


def cube_sides(padded):
    return [
        padded[2:, 1:-1, 1:-1],
        padded[:-2, 1:-1, 1:-1],
        padded[1:-1, 2:, 1:-1],
        padded[1:-1, :-2, 1:-1],
        padded[1:-1, 1:-1, 2:],
        padded[1:-1, 1:-1, :-2],
    ]


def on_device(displacement, damage, modulus, toughness, pressure, crack_mask, wells, rates):
    depth_cells, tile_cells, width = displacement.shape
    total_depth = depth_cells * lax.axis_size("depth")
    total_rows = tile_cells * lax.axis_size("tile")
    depth_start = lax.axis_index("depth") * depth_cells
    tile_start = lax.axis_index("tile") * tile_cells
    stiff = ((1.0 - damage) ** 2 + 0.001) * modulus
    mask_f = crack_mask.astype(jnp.float32)

    lo_z, hi_z = halo_swap(
        jnp.concatenate([displacement[:2], stiff[:2], damage[:1]]),
        jnp.concatenate([displacement[-2:], stiff[-2:], damage[-1:]]),
        "depth",
    )
    u_z = jnp.concatenate([lo_z[0:2], displacement, hi_z[0:2]])
    c_z = jnp.concatenate([lo_z[2:4], stiff, hi_z[2:4]])
    d_lo, d_hi = lo_z[4:5], hi_z[4:5]

    ext = depth_cells + 4

    def tile_face(rows, edge):
        return jnp.concatenate(
            [
                u_z[:, rows].reshape(-1, width),
                c_z[:, rows].reshape(-1, width),
                damage[:, edge],
                pressure[rows],
                mask_f[rows],
            ]
        )

    lo_x, hi_x = halo_swap(tile_face(slice(0, 2), 0), tile_face(slice(tile_cells - 2, tile_cells), tile_cells - 1), "tile")

    def unpack(face):
        at = 0
        u_f = face[at:at + ext * 2].reshape(ext, 2, width)
        at += ext * 2
        c_f = face[at:at + ext * 2].reshape(ext, 2, width)
        at += ext * 2
        d_f = face[at:at + depth_cells].reshape(depth_cells, 1, width)
        at += depth_cells
        p_f = face[at:at + 2]
        m_f = face[at + 2:at + 4]
        return u_f, c_f, d_f, p_f, m_f

    u_lo, c_lo, dx_lo, p_lo, m_lo = unpack(lo_x)
    u_hi, c_hi, dx_hi, p_hi, m_hi = unpack(hi_x)
    u_p = pad_last(jnp.concatenate([u_lo, u_z, u_hi], axis=1))
    c_p = pad_last(jnp.concatenate([c_lo, c_z, c_hi], axis=1))

    u_c = u_p[1:-1, 1:-1, 1:-1]
    c_c = c_p[1:-1, 1:-1, 1:-1]
    coef = jnp.zeros_like(c_c)
    flux = jnp.zeros_like(c_c)
    for c_side, u_side in zip(cube_sides(c_p), cube_sides(u_p)):
        face = 0.5 * (c_c + c_side)
        coef = coef + face
        flux = flux + face * (u_side - u_c)
    p_ext = jnp.concatenate([p_lo, pressure, p_hi])
    m_ext = jnp.concatenate([m_lo, mask_f, m_hi])
    load = 4.0 * m_ext[1:-1] * p_ext[1:-1]
    z_ids = depth_start - 1 + jnp.arange(depth_cells + 2, dtype=jnp.int32)
    x_ids = tile_start - 1 + jnp.arange(tile_cells + 2, dtype=jnp.int32)
    force = jnp.where((z_ids == total_depth // 2)[:, None, None], load[None, :, :], jnp.float32(0.0))
    moved = u_c + 0.8 * (force + flux) / coef
    inside = ((z_ids >= 0) & (z_ids < total_depth))[:, None, None] & ((x_ids >= 0) & (x_ids < total_rows))[None, :, None]
    moved = jnp.where(inside, moved, jnp.float32(0.0))

    m_pad = pad_last(moved)
    own = moved[1:-1, 1:-1]
    energy = jnp.zeros_like(own)
    for m_side in cube_sides(m_pad):
        energy = energy + (m_side - own) ** 2
    energy = 0.25 * modulus * energy

    d_zx = jnp.concatenate([d_lo, damage, d_hi])
    d_x = jnp.concatenate([dx_lo, damage, dx_hi], axis=1)
    d_y = pad_last(damage)
    beside_all = (
        d_zx[2:] + d_zx[:-2] + d_x[:, 2:] + d_x[:, :-2] + d_y[:, :, 2:] + d_y[:, :, :-2]
    )
    trial = (2.0 * energy + toughness * beside_all) / (7.0 * toughness + 2.0 * energy)
    new_damage = jnp.maximum(damage, trial)
    partial_open = 4.0 / total_depth * jnp.sum(new_damage * own * own, axis=0)
    aperture = 0.5 + butterfly_sum(partial_open, "depth")
    trans = mask_f * aperture**3

    t_lo, t_hi = halo_swap(trans[:2], trans[-2:], "tile")
    t_ext = jnp.concatenate([t_lo, trans, t_hi])
    rows_in = ((x_ids >= 0) & (x_ids < total_rows))[:, None]
    src_ext = well_source(wells, rates, tile_start - 1, tile_cells + 2, width, width)
    k_pad = pad_last(t_ext)
    level = plane_sweep(pad_last(p_ext), k_pad, p_ext[1:-1], src_ext, t_ext[1:-1])
    level = jnp.where(rows_in, level, jnp.float32(0.0))
    return plane_sweep(pad_last(level), k_pad[1:-1], pressure, src_ext[1:-1], trans)


def solution(mesh):
    return jax.shard_map(
        on_device,
        mesh=mesh,
        in_specs=(
            P("depth", "tile", None),
            P("depth", "tile", None),
            P("depth", "tile", None),
            P("depth", "tile", None),
            P("tile", None),
            P("tile", None),
            P(),
            P(),
        ),
        out_specs=P("tile", None),
        check_vma=False,
    )
```

```python
import functools

import jax
import jax.numpy as jnp
from jax import lax
from jax.experimental import pallas as pl
from jax.experimental.pallas import tpu as pltpu
from jax.sharding import PartitionSpec as P


def halo_swap(lo_face, hi_face, axis):
    count = lax.axis_size(axis)
    even = lax.axis_index(axis) % 2 == 0
    pairs_a = [(i, i ^ 1) for i in range(count)]
    pairs_b = [(i, i + 1) for i in range(1, count - 1, 2)] + [(i + 1, i) for i in range(1, count - 1, 2)]
    got_a = lax.ppermute(jnp.where(even, hi_face, lo_face), axis, pairs_a)
    got_b = lax.ppermute(jnp.where(even, lo_face, hi_face), axis, pairs_b)
    return jnp.where(even, got_b, got_a), jnp.where(even, got_a, got_b)


def butterfly_sum(part, axis):
    count = lax.axis_size(axis)
    order = [1 << k for k in range(1, count.bit_length() - 1)] + [1]
    for step in order:
        pairs = [(i, i ^ step) for i in range(lax.axis_size(axis))]
        part = part + lax.ppermute(part, axis, pairs)
    return part


def pad_last(stacked):
    widths = [(0, 0)] * (stacked.ndim - 1) + [(1, 1)]
    return jnp.pad(stacked, widths)


def flat_sides(padded):
    return [padded[2:, 1:-1], padded[:-2, 1:-1], padded[1:-1, 2:], padded[1:-1, :-2]]


def plane_sweep(p_pad, k_pad, anchor, source, trans):
    coef = jnp.zeros_like(trans)
    flow = jnp.zeros_like(trans)
    for k_side, p_side in zip(flat_sides(k_pad), flat_sides(p_pad)):
        face = 0.5 * (trans + k_side)
        coef = coef + face
        flow = flow + face * p_side
    return (anchor + source + flow) / (1.0 + coef)


def well_source(wells, rates, row_start, rows, cols, width):
    row_ids = row_start + jnp.arange(rows, dtype=jnp.int32)
    col_ids = jnp.arange(cols, dtype=jnp.int32)
    flat = row_ids[:, None] * width + col_ids[None, :]
    hit = flat[:, :, None] == wells[None, None, :]
    return 4.0 * jnp.sum(jnp.where(hit, rates[None, None, :], jnp.float32(0.0)), axis=-1)


def cube_sides(padded):
    return [
        padded[2:, 1:-1, 1:-1],
        padded[:-2, 1:-1, 1:-1],
        padded[1:-1, 2:, 1:-1],
        padded[1:-1, :-2, 1:-1],
        padded[1:-1, 1:-1, 2:],
        padded[1:-1, 1:-1, :-2],
    ]


X0 = 8


def stencil_kernel(total_depth, total_rows, ids_ref, u_ref, dmg_ref, mod_ref, tgh_ref, zlo_ref, zhi_ref, xlo_ref,
                   xhi_ref, load_ref, out_ref, u_s, c_s, d_s, m_s):
    depth_cells, tile_cells, width = u_ref.shape
    rows_all = u_s.shape[1]
    ext = depth_cells + 4
    own = slice(X0, X0 + tile_cells)
    zero = jnp.zeros((rows_all, width), jnp.float32)

    def clear(k, carry):
        u_s[k] = zero
        c_s[k] = zero
        return carry

    lax.fori_loop(0, ext, clear, 0)

    def clear_d(k, carry):
        d_s[k] = zero
        return carry

    lax.fori_loop(0, depth_cells + 2, clear_d, 0)

    def place(k, carry):
        dk = dmg_ref[k]
        u_s[k + 2, own] = u_ref[k]
        c_s[k + 2, own] = ((1.0 - dk) ** 2 + 0.001) * mod_ref[k]
        d_s[k + 1, own] = dk
        return carry

    lax.fori_loop(0, depth_cells, place, 0)
    u_s[0:2, own] = zlo_ref[0:2]
    c_s[0:2, own] = zlo_ref[2:4]
    d_s[0, own] = zlo_ref[4]
    u_s[ext - 2:ext, own] = zhi_ref[0:2]
    c_s[ext - 2:ext, own] = zhi_ref[2:4]
    d_s[depth_cells + 1, own] = zhi_ref[4]
    for z in range(ext):
        u_s[z, X0 - 2:X0] = xlo_ref[2 * z:2 * z + 2]
        c_s[z, X0 - 2:X0] = xlo_ref[2 * ext + 2 * z:2 * ext + 2 * z + 2]
        u_s[z, X0 + tile_cells:X0 + tile_cells + 2] = xhi_ref[2 * z:2 * z + 2]
        c_s[z, X0 + tile_cells:X0 + tile_cells + 2] = xhi_ref[2 * ext + 2 * z:2 * ext + 2 * z + 2]
    for z in range(depth_cells):
        d_s[z + 1, X0 - 1:X0] = xlo_ref[4 * ext + z:4 * ext + z + 1]
        d_s[z + 1, X0 + tile_cells:X0 + tile_cells + 1] = xhi_ref[4 * ext + z:4 * ext + z + 1]

    col = lax.broadcasted_iota(jnp.int32, (rows_all, width), 1)
    row = lax.broadcasted_iota(jnp.int32, (rows_all, width), 0)
    has_next = col < width - 1
    has_prev = col > 0
    depth_start = ids_ref[0]
    x_glob = ids_ref[1] + row - X0
    x_in = (x_glob >= 0) & (x_glob < total_rows)
    load = load_ref[...]

    def y_next(a):
        return jnp.where(has_next, pltpu.roll(a, width - 1, 1), 0.0)

    def y_prev(a):
        return jnp.where(has_prev, pltpu.roll(a, 1, 1), 0.0)

    def x_next(a):
        return pltpu.roll(a, rows_all - 1, 0)

    def x_prev(a):
        return pltpu.roll(a, 1, 0)

    def moved_body(k, carry):
        uc = u_s[k + 1]
        cc = c_s[k + 1]
        pairs = [
            (c_s[k + 2], u_s[k + 2]),
            (c_s[k], u_s[k]),
            (x_next(cc), x_next(uc)),
            (x_prev(cc), x_prev(uc)),
            (y_next(cc), y_next(uc)),
            (y_prev(cc), y_prev(uc)),
        ]
        coef = zero
        flux = zero
        for cn, un in pairs:
            face = 0.5 * (cc + cn)
            coef = coef + face
            flux = flux + face * (un - uc)
        z_glob = depth_start + k - 1
        force = jnp.where(z_glob == total_depth // 2, load, 0.0)
        moved = uc + 0.8 * (force + flux) / coef
        keep = x_in & (z_glob >= 0) & (z_glob < total_depth)
        m_s[k] = jnp.where(keep, moved, 0.0)
        return carry

    lax.fori_loop(0, depth_cells + 2, moved_body, 0)

    def energy_body(k, acc):
        mc = m_s[k + 1]
        energy = (
            (m_s[k + 2] - mc) ** 2 + (m_s[k] - mc) ** 2 + (x_next(mc) - mc) ** 2 + (x_prev(mc) - mc) ** 2
            + (y_next(mc) - mc) ** 2 + (y_prev(mc) - mc) ** 2
        )
        dc = d_s[k + 1]
        beside = d_s[k + 2] + d_s[k] + x_next(dc) + x_prev(dc) + y_next(dc) + y_prev(dc)
        energy = 0.25 * mod_ref[k] * energy[own]
        tough = tgh_ref[k]
        trial = (2.0 * energy + tough * beside[own]) / (7.0 * tough + 2.0 * energy)
        new_damage = jnp.maximum(dmg_ref[k], trial)
        mo = mc[own]
        return acc + new_damage * mo * mo

    acc = lax.fori_loop(0, depth_cells, energy_body, jnp.zeros((tile_cells, width), jnp.float32))
    out_ref[...] = (4.0 / total_depth) * acc


def stencil_partial(ids, u, dmg, mod, tgh, zlo, zhi, xlo, xhi, load32, total_depth, total_rows):
    depth_cells, tile_cells, width = u.shape
    rows_all = tile_cells + 2 * X0
    vmem = pl.BlockSpec(memory_space=pltpu.VMEM)
    return pl.pallas_call(
        functools.partial(stencil_kernel, total_depth, total_rows),
        out_shape=jax.ShapeDtypeStruct((tile_cells, width), jnp.float32),
        in_specs=[pl.BlockSpec(memory_space=pltpu.SMEM)] + [vmem] * 9,
        out_specs=vmem,
        scratch_shapes=[
            pltpu.VMEM((depth_cells + 4, rows_all, width), jnp.float32),
            pltpu.VMEM((depth_cells + 4, rows_all, width), jnp.float32),
            pltpu.VMEM((depth_cells + 2, rows_all, width), jnp.float32),
            pltpu.VMEM((depth_cells + 2, rows_all, width), jnp.float32),
        ],
    )(ids, u, dmg, mod, tgh, zlo, zhi, xlo, xhi, load32)


def on_device(displacement, damage, modulus, toughness, pressure, crack_mask, wells, rates):
    depth_cells, tile_cells, width = displacement.shape
    total_depth = depth_cells * lax.axis_size("depth")
    total_rows = tile_cells * lax.axis_size("tile")
    depth_start = lax.axis_index("depth") * depth_cells
    tile_start = lax.axis_index("tile") * tile_cells
    mask_f = crack_mask.astype(jnp.float32)

    def stiff_of(dmg, mod):
        return ((1.0 - dmg) ** 2 + 0.001) * mod

    lo_z, hi_z = halo_swap(
        jnp.concatenate([displacement[:2], stiff_of(damage[:2], modulus[:2]), damage[:1]]),
        jnp.concatenate([displacement[-2:], stiff_of(damage[-2:], modulus[-2:]), damage[-1:]]),
        "depth",
    )

    ext = depth_cells + 4

    def tile_face(rows, edge):
        return jnp.concatenate(
            [
                jnp.concatenate([lo_z[0:2, rows], displacement[:, rows], hi_z[0:2, rows]]).reshape(-1, width),
                jnp.concatenate(
                    [lo_z[2:4, rows], stiff_of(damage[:, rows], modulus[:, rows]), hi_z[2:4, rows]]
                ).reshape(-1, width),
                damage[:, edge],
                pressure[rows],
                mask_f[rows],
            ]
        )

    lo_x, hi_x = halo_swap(tile_face(slice(0, 2), 0), tile_face(slice(tile_cells - 2, tile_cells), tile_cells - 1), "tile")

    p_lo, m_lo = lo_x[-4:-2], lo_x[-2:]
    p_hi, m_hi = hi_x[-4:-2], hi_x[-2:]
    p_ext = jnp.concatenate([p_lo, pressure, p_hi])
    m_ext = jnp.concatenate([m_lo, mask_f, m_hi])
    load32 = jnp.pad(4.0 * m_ext[1:-1] * p_ext[1:-1], ((X0 - 1, X0 - 1), (0, 0)))
    x_ids = tile_start - 1 + jnp.arange(tile_cells + 2, dtype=jnp.int32)
    ids = jnp.stack([depth_start, tile_start]).astype(jnp.int32)
    partial_open = stencil_partial(
        ids, displacement, damage, modulus, toughness, lo_z, hi_z, lo_x, hi_x, load32, total_depth, total_rows
    )
    aperture = 0.5 + butterfly_sum(partial_open, "depth")
    trans = mask_f * aperture**3

    t_lo, t_hi = halo_swap(trans[:2], trans[-2:], "tile")
    t_ext = jnp.concatenate([t_lo, trans, t_hi])
    rows_in = ((x_ids >= 0) & (x_ids < total_rows))[:, None]
    src_ext = well_source(wells, rates, tile_start - 1, tile_cells + 2, width, width)
    k_pad = pad_last(t_ext)
    level = plane_sweep(pad_last(p_ext), k_pad, p_ext[1:-1], src_ext, t_ext[1:-1])
    level = jnp.where(rows_in, level, jnp.float32(0.0))
    return plane_sweep(pad_last(level), k_pad[1:-1], pressure, src_ext[1:-1], trans)


def solution(mesh):
    return jax.shard_map(
        on_device,
        mesh=mesh,
        in_specs=(
            P("depth", "tile", None),
            P("depth", "tile", None),
            P("depth", "tile", None),
            P("depth", "tile", None),
            P("tile", None),
            P("tile", None),
            P(),
            P(),
        ),
        out_specs=P("tile", None),
        check_vma=False,
    )
```

```python
import functools

import jax
import jax.numpy as jnp
from jax import lax
from jax.experimental import pallas as pl
from jax.experimental.pallas import tpu as pltpu
from jax.sharding import PartitionSpec as P


def halo_swap(lo_face, hi_face, axis):
    count = lax.axis_size(axis)
    even = lax.axis_index(axis) % 2 == 0
    pairs_a = [(i, i ^ 1) for i in range(count)]
    pairs_b = [(i, i + 1) for i in range(1, count - 1, 2)] + [(i + 1, i) for i in range(1, count - 1, 2)]
    got_a = lax.ppermute(jnp.where(even, hi_face, lo_face), axis, pairs_a)
    got_b = lax.ppermute(jnp.where(even, lo_face, hi_face), axis, pairs_b)
    return jnp.where(even, got_b, got_a), jnp.where(even, got_a, got_b)


def butterfly_sum(part, axis):
    count = lax.axis_size(axis)
    order = [1 << k for k in range(1, count.bit_length() - 1)] + [1]
    for step in order:
        pairs = [(i, i ^ step) for i in range(lax.axis_size(axis))]
        part = part + lax.ppermute(part, axis, pairs)
    return part


def pad_last(stacked):
    widths = [(0, 0)] * (stacked.ndim - 1) + [(1, 1)]
    return jnp.pad(stacked, widths)


def flat_sides(padded):
    return [padded[2:, 1:-1], padded[:-2, 1:-1], padded[1:-1, 2:], padded[1:-1, :-2]]


def plane_sweep(p_pad, k_pad, anchor, source, trans):
    coef = jnp.zeros_like(trans)
    flow = jnp.zeros_like(trans)
    for k_side, p_side in zip(flat_sides(k_pad), flat_sides(p_pad)):
        face = 0.5 * (trans + k_side)
        coef = coef + face
        flow = flow + face * p_side
    return (anchor + source + flow) / (1.0 + coef)


def well_source(wells, rates, row_start, rows, cols, width):
    row_ids = row_start + jnp.arange(rows, dtype=jnp.int32)
    col_ids = jnp.arange(cols, dtype=jnp.int32)
    flat = row_ids[:, None] * width + col_ids[None, :]
    hit = flat[:, :, None] == wells[None, None, :]
    return 4.0 * jnp.sum(jnp.where(hit, rates[None, None, :], jnp.float32(0.0)), axis=-1)


def cube_sides(padded):
    return [
        padded[2:, 1:-1, 1:-1],
        padded[:-2, 1:-1, 1:-1],
        padded[1:-1, 2:, 1:-1],
        padded[1:-1, :-2, 1:-1],
        padded[1:-1, 1:-1, 2:],
        padded[1:-1, 1:-1, :-2],
    ]


X0 = 8


def neighbours(rows_all, width):
    col = lax.broadcasted_iota(jnp.int32, (rows_all, width), 1)
    has_next = col < width - 1
    has_prev = col > 0

    def y_next(a):
        return jnp.where(has_next, pltpu.roll(a, width - 1, 1), 0.0)

    def y_prev(a):
        return jnp.where(has_prev, pltpu.roll(a, 1, 1), 0.0)

    def x_next(a):
        return pltpu.roll(a, rows_all - 1, 0)

    def x_prev(a):
        return pltpu.roll(a, 1, 0)

    return x_next, x_prev, y_next, y_prev


def moved_at(uc, cc, up, down, nb, z_glob, load, x_in, total_depth):
    x_next, x_prev, y_next, y_prev = nb
    pairs = [
        up,
        down,
        (x_next(cc), x_next(uc)),
        (x_prev(cc), x_prev(uc)),
        (y_next(cc), y_next(uc)),
        (y_prev(cc), y_prev(uc)),
    ]
    coef = jnp.zeros_like(uc)
    flux = jnp.zeros_like(uc)
    for cn, un in pairs:
        face = 0.5 * (cc + cn)
        coef = coef + face
        flux = flux + face * (un - uc)
    force = jnp.where(z_glob == total_depth // 2, load, 0.0)
    moved = uc + 0.8 * (force + flux) / coef
    keep = x_in & (z_glob >= 0) & (z_glob < total_depth)
    return jnp.where(keep, moved, 0.0)


def opening_at(mc, m_up, m_down, dc, d_up, d_down, nb, mod, tough, dmg, own):
    x_next, x_prev, y_next, y_prev = nb
    energy = (
        (m_up - mc) ** 2 + (m_down - mc) ** 2 + (x_next(mc) - mc) ** 2 + (x_prev(mc) - mc) ** 2
        + (y_next(mc) - mc) ** 2 + (y_prev(mc) - mc) ** 2
    )
    beside = d_up + d_down + x_next(dc) + x_prev(dc) + y_next(dc) + y_prev(dc)
    energy = 0.25 * mod * energy[own]
    trial = (2.0 * energy + tough * beside[own]) / (7.0 * tough + 2.0 * energy)
    new_damage = jnp.maximum(dmg, trial)
    mo = mc[own]
    return new_damage * mo * mo


def x_frame(ids_ref, rows_all, width, total_rows):
    row = lax.broadcasted_iota(jnp.int32, (rows_all, width), 0)
    x_glob = ids_ref[1] + row - X0
    return (x_glob >= 0) & (x_glob < total_rows)


def interior_kernel(total_depth, total_rows, ids_ref, u_ref, dmg_ref, mod_ref, tgh_ref, xlo_ref, xhi_ref, load_ref,
                    part_ref, edge_ref, u_s, c_s, d_s, m_s):
    depth_cells, tile_cells, width = u_ref.shape
    rows_all = u_s.shape[1]
    own = slice(X0, X0 + tile_cells)
    top = X0 + tile_cells
    zero = jnp.zeros((rows_all, width), jnp.float32)

    def place(k, carry):
        dk = dmg_ref[k]
        u_s[k] = zero
        c_s[k] = zero
        d_s[k] = zero
        u_s[k, own] = u_ref[k]
        c_s[k, own] = ((1.0 - dk) ** 2 + 0.001) * mod_ref[k]
        d_s[k, own] = dk
        return carry

    lax.fori_loop(0, depth_cells, place, 0)
    dz = 4 * depth_cells
    for z in range(depth_cells):
        u_s[z, X0 - 2:X0] = xlo_ref[2 * z:2 * z + 2]
        c_s[z, X0 - 2:X0] = xlo_ref[2 * depth_cells + 2 * z:2 * depth_cells + 2 * z + 2]
        d_s[z, X0 - 1:X0] = xlo_ref[dz + z:dz + z + 1]
        u_s[z, top:top + 2] = xhi_ref[2 * z:2 * z + 2]
        c_s[z, top:top + 2] = xhi_ref[2 * depth_cells + 2 * z:2 * depth_cells + 2 * z + 2]
        d_s[z, top:top + 1] = xhi_ref[dz + z:dz + z + 1]

    nb = neighbours(rows_all, width)
    x_in = x_frame(ids_ref, rows_all, width, total_rows)
    load = load_ref[...]
    depth_start = ids_ref[0]

    def moved_body(k, carry):
        m_s[k] = moved_at(
            u_s[k], c_s[k], (c_s[k + 1], u_s[k + 1]), (c_s[k - 1], u_s[k - 1]), nb, depth_start + k, load, x_in,
            total_depth,
        )
        return carry

    lax.fori_loop(1, depth_cells - 1, moved_body, 0)

    def open_body(k, acc):
        return acc + opening_at(
            m_s[k], m_s[k + 1], m_s[k - 1], d_s[k], d_s[k + 1], d_s[k - 1], nb, mod_ref[k], tgh_ref[k], dmg_ref[k], own
        )

    acc = lax.fori_loop(2, depth_cells - 2, open_body, jnp.zeros((tile_cells, width), jnp.float32))
    part_ref[...] = acc
    edge_ref[0] = m_s[1]
    edge_ref[1] = m_s[2]
    edge_ref[2] = m_s[depth_cells - 3]
    edge_ref[3] = m_s[depth_cells - 2]


def boundary_kernel(total_depth, total_rows, ids_ref, u_ref, dmg_ref, mod_ref, tgh_ref, xlo_ref, xhi_ref, zlo_ref,
                    zhi_ref, edge_ref, part_ref, load_ref, out_ref, u_s, c_s, d_s, m_s):
    depth_cells, tile_cells, width = u_ref.shape
    rows_all = u_s.shape[1]
    own = slice(X0, X0 + tile_cells)
    wide = slice(X0 - 1, X0 + tile_cells + 1)
    top = X0 + tile_cells
    zero = jnp.zeros((rows_all, width), jnp.float32)
    for j in range(8):
        u_s[j] = zero
        c_s[j] = zero
        d_s[j] = zero
    ext = tile_cells + 2
    for side, ref, adj, sec in ((0, zlo_ref, 1, 0), (4, zhi_ref, 6, 7)):
        u_s[adj, wide] = ref[0:ext]
        c_s[adj, wide] = ref[ext:2 * ext]
        u_s[sec, own] = ref[2 * ext:2 * ext + tile_cells]
        c_s[sec, own] = ref[2 * ext + tile_cells:2 * ext + 2 * tile_cells]
    d_s[0, own] = zlo_ref[2 * ext + 2 * tile_cells:2 * ext + 3 * tile_cells]
    d_s[7, own] = zhi_ref[2 * ext + 2 * tile_cells:2 * ext + 3 * tile_cells]
    dz = 4 * depth_cells
    for slot, z in ((2, 0), (3, 1), (4, depth_cells - 2), (5, depth_cells - 1)):
        dk = dmg_ref[z]
        u_s[slot, own] = u_ref[z]
        c_s[slot, own] = ((1.0 - dk) ** 2 + 0.001) * mod_ref[z]
        u_s[slot, X0 - 2:X0] = xlo_ref[2 * z:2 * z + 2]
        c_s[slot, X0 - 2:X0] = xlo_ref[2 * depth_cells + 2 * z:2 * depth_cells + 2 * z + 2]
        u_s[slot, top:top + 2] = xhi_ref[2 * z:2 * z + 2]
        c_s[slot, top:top + 2] = xhi_ref[2 * depth_cells + 2 * z:2 * depth_cells + 2 * z + 2]
    for slot, z in ((1, 0), (2, 1), (5, depth_cells - 2), (6, depth_cells - 1)):
        d_s[slot, own] = dmg_ref[z]
        d_s[slot, X0 - 1:X0] = xlo_ref[dz + z:dz + z + 1]
        d_s[slot, top:top + 1] = xhi_ref[dz + z:dz + z + 1]
    d_s[3, own] = dmg_ref[2]
    d_s[4, own] = dmg_ref[depth_cells - 3]
    m_s[2] = edge_ref[0]
    m_s[3] = edge_ref[1]
    m_s[4] = edge_ref[2]
    m_s[5] = edge_ref[3]

    nb = neighbours(rows_all, width)
    x_in = x_frame(ids_ref, rows_all, width, total_rows)
    load = load_ref[...]
    depth_start = ids_ref[0]
    for us, ms, z in ((1, 0, -1), (2, 1, 0), (5, 6, depth_cells - 1), (6, 7, depth_cells)):
        m_s[ms] = moved_at(
            u_s[us], c_s[us], (c_s[us + 1], u_s[us + 1]), (c_s[us - 1], u_s[us - 1]), nb, depth_start + z, load, x_in,
            total_depth,
        )
    acc = part_ref[...]
    for ms, z in ((1, 0), (2, 1), (5, depth_cells - 2), (6, depth_cells - 1)):
        acc = acc + opening_at(
            m_s[ms], m_s[ms + 1], m_s[ms - 1], d_s[ms], d_s[ms + 1], d_s[ms - 1], nb, mod_ref[z], tgh_ref[z],
            dmg_ref[z], own,
        )
    out_ref[...] = (4.0 / total_depth) * acc


def on_device(displacement, damage, modulus, toughness, pressure, crack_mask, wells, rates):
    depth_cells, tile_cells, width = displacement.shape
    total_depth = depth_cells * lax.axis_size("depth")
    total_rows = tile_cells * lax.axis_size("tile")
    depth_start = lax.axis_index("depth") * depth_cells
    tile_start = lax.axis_index("tile") * tile_cells
    mask_f = crack_mask.astype(jnp.float32)
    rows_all = tile_cells + 2 * X0

    def stiff_of(dmg, mod):
        return ((1.0 - dmg) ** 2 + 0.001) * mod

    def tile_face(rows, edge):
        return jnp.concatenate(
            [
                displacement[:, rows].reshape(-1, width),
                stiff_of(damage[:, rows], modulus[:, rows]).reshape(-1, width),
                damage[:, edge],
                pressure[rows],
                mask_f[rows],
            ]
        )

    lo_x, hi_x = halo_swap(tile_face(slice(0, 2), 0), tile_face(slice(tile_cells - 2, tile_cells), tile_cells - 1), "tile")
    dz = 4 * depth_cells
    p_ext = jnp.concatenate([lo_x[dz + depth_cells:dz + depth_cells + 2], pressure, hi_x[dz + depth_cells:dz + depth_cells + 2]])
    m_ext = jnp.concatenate([lo_x[dz + depth_cells + 2:], mask_f, hi_x[dz + depth_cells + 2:]])
    load_all = jnp.pad(4.0 * m_ext[1:-1] * p_ext[1:-1], ((X0 - 1, X0 - 1), (0, 0)))
    ids = jnp.stack([depth_start, tile_start]).astype(jnp.int32)

    def depth_face(adj, sec):
        u_adj = jnp.concatenate([lo_x[2 * adj + 1:2 * adj + 2], displacement[adj], hi_x[2 * adj:2 * adj + 1]])
        c0 = 2 * depth_cells
        c_adj = jnp.concatenate(
            [lo_x[c0 + 2 * adj + 1:c0 + 2 * adj + 2], stiff_of(damage[adj], modulus[adj]), hi_x[c0 + 2 * adj:c0 + 2 * adj + 1]]
        )
        return jnp.concatenate([u_adj, c_adj, displacement[sec], stiff_of(damage[sec], modulus[sec]), damage[adj]])

    lo_z, hi_z = halo_swap(depth_face(0, 1), depth_face(depth_cells - 1, depth_cells - 2), "depth")

    vmem = pl.BlockSpec(memory_space=pltpu.VMEM)
    smem = pl.BlockSpec(memory_space=pltpu.SMEM)
    f32 = jnp.float32
    part_in, edge = pl.pallas_call(
        functools.partial(interior_kernel, total_depth, total_rows),
        out_shape=(
            jax.ShapeDtypeStruct((tile_cells, width), f32),
            jax.ShapeDtypeStruct((4, rows_all, width), f32),
        ),
        in_specs=[smem] + [vmem] * 7,
        out_specs=(vmem, vmem),
        scratch_shapes=[pltpu.VMEM((depth_cells, rows_all, width), f32)] * 4,
    )(ids, displacement, damage, modulus, toughness, lo_x, hi_x, load_all)
    partial_open = pl.pallas_call(
        functools.partial(boundary_kernel, total_depth, total_rows),
        out_shape=jax.ShapeDtypeStruct((tile_cells, width), f32),
        in_specs=[smem] + [vmem] * 11,
        out_specs=vmem,
        scratch_shapes=[pltpu.VMEM((8, rows_all, width), f32)] * 4,
    )(ids, displacement, damage, modulus, toughness, lo_x, hi_x, lo_z, hi_z, edge, part_in, load_all)

    aperture = 0.5 + butterfly_sum(partial_open, "depth")
    trans = mask_f * aperture**3

    t_lo, t_hi = halo_swap(trans[:2], trans[-2:], "tile")
    t_ext = jnp.concatenate([t_lo, trans, t_hi])
    x_ids = tile_start - 1 + jnp.arange(tile_cells + 2, dtype=jnp.int32)
    rows_in = ((x_ids >= 0) & (x_ids < total_rows))[:, None]
    src_ext = well_source(wells, rates, tile_start - 1, tile_cells + 2, width, width)
    k_pad = pad_last(t_ext)
    level = plane_sweep(pad_last(p_ext), k_pad, p_ext[1:-1], src_ext, t_ext[1:-1])
    level = jnp.where(rows_in, level, jnp.float32(0.0))
    return plane_sweep(pad_last(level), k_pad[1:-1], pressure, src_ext[1:-1], trans)


def solution(mesh):
    return jax.shard_map(
        on_device,
        mesh=mesh,
        in_specs=(
            P("depth", "tile", None),
            P("depth", "tile", None),
            P("depth", "tile", None),
            P("depth", "tile", None),
            P("tile", None),
            P("tile", None),
            P(),
            P(),
        ),
        out_specs=P("tile", None),
        check_vma=False,
    )
```

```python
import functools

import jax
import jax.numpy as jnp
from jax import lax
from jax.experimental import pallas as pl
from jax.experimental.pallas import tpu as pltpu
from jax.sharding import PartitionSpec as P


def halo_swap(lo_face, hi_face, axis):
    count = lax.axis_size(axis)
    even = lax.axis_index(axis) % 2 == 0
    pairs_a = [(i, i ^ 1) for i in range(count)]
    pairs_b = [(i, i + 1) for i in range(1, count - 1, 2)] + [(i + 1, i) for i in range(1, count - 1, 2)]
    got_a = lax.ppermute(jnp.where(even, hi_face, lo_face), axis, pairs_a)
    got_b = lax.ppermute(jnp.where(even, lo_face, hi_face), axis, pairs_b)
    return jnp.where(even, got_b, got_a), jnp.where(even, got_a, got_b)


def butterfly_sum(part, axis):
    count = lax.axis_size(axis)
    order = [1 << k for k in range(1, count.bit_length() - 1)] + [1]
    for step in order:
        pairs = [(i, i ^ step) for i in range(lax.axis_size(axis))]
        part = part + lax.ppermute(part, axis, pairs)
    return part


def pad_last(stacked):
    widths = [(0, 0)] * (stacked.ndim - 1) + [(1, 1)]
    return jnp.pad(stacked, widths)


def flat_sides(padded):
    return [padded[2:, 1:-1], padded[:-2, 1:-1], padded[1:-1, 2:], padded[1:-1, :-2]]


def plane_sweep(p_pad, k_pad, anchor, source, trans):
    coef = jnp.zeros_like(trans)
    flow = jnp.zeros_like(trans)
    for k_side, p_side in zip(flat_sides(k_pad), flat_sides(p_pad)):
        face = 0.5 * (trans + k_side)
        coef = coef + face
        flow = flow + face * p_side
    return (anchor + source + flow) / (1.0 + coef)


def well_source(wells, rates, row_start, rows, cols, width):
    row_ids = row_start + jnp.arange(rows, dtype=jnp.int32)
    col_ids = jnp.arange(cols, dtype=jnp.int32)
    flat = row_ids[:, None] * width + col_ids[None, :]
    hit = flat[:, :, None] == wells[None, None, :]
    return 4.0 * jnp.sum(jnp.where(hit, rates[None, None, :], jnp.float32(0.0)), axis=-1)


def cube_sides(padded):
    return [
        padded[2:, 1:-1, 1:-1],
        padded[:-2, 1:-1, 1:-1],
        padded[1:-1, 2:, 1:-1],
        padded[1:-1, :-2, 1:-1],
        padded[1:-1, 1:-1, 2:],
        padded[1:-1, 1:-1, :-2],
    ]


X0 = 8


def neighbours(rows_all, width):
    col = lax.broadcasted_iota(jnp.int32, (rows_all, width), 1)
    has_next = col < width - 1
    has_prev = col > 0

    def y_next(a):
        return jnp.where(has_next, pltpu.roll(a, width - 1, 1), 0.0)

    def y_prev(a):
        return jnp.where(has_prev, pltpu.roll(a, 1, 1), 0.0)

    def x_next(a):
        return pltpu.roll(a, rows_all - 1, 0)

    def x_prev(a):
        return pltpu.roll(a, 1, 0)

    return x_next, x_prev, y_next, y_prev


def moved_at(uc, cc, up, down, nb, z_glob, load, x_in, total_depth):
    x_next, x_prev, y_next, y_prev = nb
    pairs = [
        up,
        down,
        (x_next(cc), x_next(uc)),
        (x_prev(cc), x_prev(uc)),
        (y_next(cc), y_next(uc)),
        (y_prev(cc), y_prev(uc)),
    ]
    coef = jnp.zeros_like(uc)
    flux = jnp.zeros_like(uc)
    for cn, un in pairs:
        face = 0.5 * (cc + cn)
        coef = coef + face
        flux = flux + face * (un - uc)
    force = jnp.where(z_glob == total_depth // 2, load, 0.0)
    moved = uc + 0.8 * (force + flux) / coef
    keep = x_in & (z_glob >= 0) & (z_glob < total_depth)
    return jnp.where(keep, moved, 0.0)


def opening_at(mc, m_up, m_down, dc, d_up, d_down, nb, mod, tough, dmg, own):
    x_next, x_prev, y_next, y_prev = nb
    energy = (
        (m_up - mc) ** 2 + (m_down - mc) ** 2 + (x_next(mc) - mc) ** 2 + (x_prev(mc) - mc) ** 2
        + (y_next(mc) - mc) ** 2 + (y_prev(mc) - mc) ** 2
    )
    beside = d_up + d_down + x_next(dc) + x_prev(dc) + y_next(dc) + y_prev(dc)
    energy = 0.25 * mod * energy[own]
    trial = (2.0 * energy + tough * beside[own]) / (7.0 * tough + 2.0 * energy)
    new_damage = jnp.maximum(dmg, trial)
    mo = mc[own]
    return new_damage * mo * mo


def x_frame(ids_ref, rows_all, width, total_rows):
    row = lax.broadcasted_iota(jnp.int32, (rows_all, width), 0)
    x_glob = ids_ref[1] + row - X0
    return (x_glob >= 0) & (x_glob < total_rows)


def interior_kernel(total_depth, total_rows, ids_ref, u_ref, dmg_ref, mod_ref, tgh_ref, xlo_ref, xhi_ref, load_ref,
                    part_ref, edge_ref, u_s, c_s, d_s, m_s):
    depth_cells, tile_cells, width = u_ref.shape
    rows_all = u_s.shape[1]
    own = slice(X0, X0 + tile_cells)
    top = X0 + tile_cells
    zero = jnp.zeros((rows_all, width), jnp.float32)

    def place(k, carry):
        dk = dmg_ref[k]
        u_s[k] = zero
        c_s[k] = zero
        d_s[k] = zero
        u_s[k, own] = u_ref[k]
        c_s[k, own] = ((1.0 - dk) ** 2 + 0.001) * mod_ref[k]
        d_s[k, own] = dk
        return carry

    lax.fori_loop(0, depth_cells, place, 0)
    dz = 4 * depth_cells
    for z in range(depth_cells):
        u_s[z, X0 - 2:X0] = xlo_ref[2 * z:2 * z + 2]
        c_s[z, X0 - 2:X0] = xlo_ref[2 * depth_cells + 2 * z:2 * depth_cells + 2 * z + 2]
        d_s[z, X0 - 1:X0] = xlo_ref[dz + z:dz + z + 1]
        u_s[z, top:top + 2] = xhi_ref[2 * z:2 * z + 2]
        c_s[z, top:top + 2] = xhi_ref[2 * depth_cells + 2 * z:2 * depth_cells + 2 * z + 2]
        d_s[z, top:top + 1] = xhi_ref[dz + z:dz + z + 1]

    nb = neighbours(rows_all, width)
    x_in = x_frame(ids_ref, rows_all, width, total_rows)
    load = load_ref[...]
    depth_start = ids_ref[0]

    def moved_body(k, carry):
        m_s[k] = moved_at(
            u_s[k], c_s[k], (c_s[k + 1], u_s[k + 1]), (c_s[k - 1], u_s[k - 1]), nb, depth_start + k, load, x_in,
            total_depth,
        )
        return carry

    lax.fori_loop(1, depth_cells - 1, moved_body, 0)

    def open_body(k, acc):
        return acc + opening_at(
            m_s[k], m_s[k + 1], m_s[k - 1], d_s[k], d_s[k + 1], d_s[k - 1], nb, mod_ref[k], tgh_ref[k], dmg_ref[k], own
        )

    acc = lax.fori_loop(2, depth_cells - 2, open_body, jnp.zeros((tile_cells, width), jnp.float32))
    part_ref[...] = acc
    edge_ref[0] = m_s[1]
    edge_ref[1] = m_s[2]
    edge_ref[2] = m_s[depth_cells - 3]
    edge_ref[3] = m_s[depth_cells - 2]


def boundary_kernel(total_depth, total_rows, ids_ref, u_ref, dmg_ref, mod_ref, tgh_ref, xlo_ref, xhi_ref, zlo_ref,
                    zhi_ref, edge_ref, part_ref, load_ref, out_ref, u_s, c_s, d_s, m_s):
    depth_cells, tile_cells, width = u_ref.shape
    rows_all = u_s.shape[1]
    own = slice(X0, X0 + tile_cells)
    wide = slice(X0 - 1, X0 + tile_cells + 1)
    top = X0 + tile_cells
    zero = jnp.zeros((rows_all, width), jnp.float32)
    for j in range(8):
        u_s[j] = zero
        c_s[j] = zero
        d_s[j] = zero
    ext = tile_cells + 2
    for side, ref, adj, sec in ((0, zlo_ref, 1, 0), (4, zhi_ref, 6, 7)):
        u_s[adj, wide] = ref[0:ext]
        c_s[adj, wide] = ref[ext:2 * ext]
        u_s[sec, own] = ref[2 * ext:2 * ext + tile_cells]
        c_s[sec, own] = ref[2 * ext + tile_cells:2 * ext + 2 * tile_cells]
    d_s[0, own] = zlo_ref[2 * ext + 2 * tile_cells:2 * ext + 3 * tile_cells]
    d_s[7, own] = zhi_ref[2 * ext + 2 * tile_cells:2 * ext + 3 * tile_cells]
    dz = 4 * depth_cells
    for slot, z in ((2, 0), (3, 1), (4, depth_cells - 2), (5, depth_cells - 1)):
        dk = dmg_ref[z]
        u_s[slot, own] = u_ref[z]
        c_s[slot, own] = ((1.0 - dk) ** 2 + 0.001) * mod_ref[z]
        u_s[slot, X0 - 2:X0] = xlo_ref[2 * z:2 * z + 2]
        c_s[slot, X0 - 2:X0] = xlo_ref[2 * depth_cells + 2 * z:2 * depth_cells + 2 * z + 2]
        u_s[slot, top:top + 2] = xhi_ref[2 * z:2 * z + 2]
        c_s[slot, top:top + 2] = xhi_ref[2 * depth_cells + 2 * z:2 * depth_cells + 2 * z + 2]
    for slot, z in ((1, 0), (2, 1), (5, depth_cells - 2), (6, depth_cells - 1)):
        d_s[slot, own] = dmg_ref[z]
        d_s[slot, X0 - 1:X0] = xlo_ref[dz + z:dz + z + 1]
        d_s[slot, top:top + 1] = xhi_ref[dz + z:dz + z + 1]
    d_s[3, own] = dmg_ref[2]
    d_s[4, own] = dmg_ref[depth_cells - 3]
    m_s[2] = edge_ref[0]
    m_s[3] = edge_ref[1]
    m_s[4] = edge_ref[2]
    m_s[5] = edge_ref[3]

    nb = neighbours(rows_all, width)
    x_in = x_frame(ids_ref, rows_all, width, total_rows)
    load = load_ref[...]
    depth_start = ids_ref[0]
    for us, ms, z in ((1, 0, -1), (2, 1, 0), (5, 6, depth_cells - 1), (6, 7, depth_cells)):
        m_s[ms] = moved_at(
            u_s[us], c_s[us], (c_s[us + 1], u_s[us + 1]), (c_s[us - 1], u_s[us - 1]), nb, depth_start + z, load, x_in,
            total_depth,
        )
    acc = part_ref[...]
    for ms, z in ((1, 0), (2, 1), (5, depth_cells - 2), (6, depth_cells - 1)):
        acc = acc + opening_at(
            m_s[ms], m_s[ms + 1], m_s[ms - 1], d_s[ms], d_s[ms + 1], d_s[ms - 1], nb, mod_ref[z], tgh_ref[z],
            dmg_ref[z], own,
        )
    out_ref[...] = (4.0 / total_depth) * acc


def on_device(displacement, damage, modulus, toughness, pressure, crack_mask, wells, rates):
    depth_cells, tile_cells, width = displacement.shape
    total_depth = depth_cells * lax.axis_size("depth")
    total_rows = tile_cells * lax.axis_size("tile")
    depth_start = lax.axis_index("depth") * depth_cells
    tile_start = lax.axis_index("tile") * tile_cells
    mask_f = crack_mask.astype(jnp.float32)
    rows_all = tile_cells + 2 * X0

    def stiff_of(dmg, mod):
        return ((1.0 - dmg) ** 2 + 0.001) * mod

    def corner_face(x):
        return jnp.stack(
            [
                displacement[0, x],
                stiff_of(damage[0, x], modulus[0, x]),
                displacement[depth_cells - 1, x],
                stiff_of(damage[depth_cells - 1, x], modulus[depth_cells - 1, x]),
            ]
        )

    lo_c, hi_c = halo_swap(corner_face(0), corner_face(tile_cells - 1), "tile")

    def depth_face(adj, sec, at):
        u_adj = jnp.concatenate([lo_c[at:at + 1], displacement[adj], hi_c[at:at + 1]])
        c_adj = jnp.concatenate([lo_c[at + 1:at + 2], stiff_of(damage[adj], modulus[adj]), hi_c[at + 1:at + 2]])
        return jnp.concatenate([u_adj, c_adj, displacement[sec], stiff_of(damage[sec], modulus[sec]), damage[adj]])

    lo_z, hi_z = halo_swap(depth_face(0, 1, 0), depth_face(depth_cells - 1, depth_cells - 2, 2), "depth")

    def tile_face(rows, edge):
        return jnp.concatenate(
            [
                displacement[:, rows].reshape(-1, width),
                stiff_of(damage[:, rows], modulus[:, rows]).reshape(-1, width),
                damage[:, edge],
                pressure[rows],
                mask_f[rows],
            ]
        )

    face_lo, face_hi, _ = lax.optimization_barrier(
        (tile_face(slice(0, 2), 0), tile_face(slice(tile_cells - 2, tile_cells), tile_cells - 1), lo_c)
    )
    lo_x, hi_x = halo_swap(face_lo, face_hi, "tile")
    dz = 4 * depth_cells
    p_ext = jnp.concatenate([lo_x[dz + depth_cells:dz + depth_cells + 2], pressure, hi_x[dz + depth_cells:dz + depth_cells + 2]])
    m_ext = jnp.concatenate([lo_x[dz + depth_cells + 2:], mask_f, hi_x[dz + depth_cells + 2:]])
    load_all = jnp.pad(4.0 * m_ext[1:-1] * p_ext[1:-1], ((X0 - 1, X0 - 1), (0, 0)))
    ids = jnp.stack([depth_start, tile_start]).astype(jnp.int32)

    vmem = pl.BlockSpec(memory_space=pltpu.VMEM)
    smem = pl.BlockSpec(memory_space=pltpu.SMEM)
    f32 = jnp.float32
    part_in, edge = pl.pallas_call(
        functools.partial(interior_kernel, total_depth, total_rows),
        out_shape=(
            jax.ShapeDtypeStruct((tile_cells, width), f32),
            jax.ShapeDtypeStruct((4, rows_all, width), f32),
        ),
        in_specs=[smem] + [vmem] * 7,
        out_specs=(vmem, vmem),
        scratch_shapes=[pltpu.VMEM((depth_cells, rows_all, width), f32)] * 4,
    )(ids, displacement, damage, modulus, toughness, lo_x, hi_x, load_all)
    partial_open = pl.pallas_call(
        functools.partial(boundary_kernel, total_depth, total_rows),
        out_shape=jax.ShapeDtypeStruct((tile_cells, width), f32),
        in_specs=[smem] + [vmem] * 11,
        out_specs=vmem,
        scratch_shapes=[pltpu.VMEM((8, rows_all, width), f32)] * 4,
    )(ids, displacement, damage, modulus, toughness, lo_x, hi_x, lo_z, hi_z, edge, part_in, load_all)

    aperture = 0.5 + butterfly_sum(partial_open, "depth")
    trans = mask_f * aperture**3

    t_lo, t_hi = halo_swap(trans[:2], trans[-2:], "tile")
    t_ext = jnp.concatenate([t_lo, trans, t_hi])
    x_ids = tile_start - 1 + jnp.arange(tile_cells + 2, dtype=jnp.int32)
    rows_in = ((x_ids >= 0) & (x_ids < total_rows))[:, None]
    src_ext = well_source(wells, rates, tile_start - 1, tile_cells + 2, width, width)
    k_pad = pad_last(t_ext)
    level = plane_sweep(pad_last(p_ext), k_pad, p_ext[1:-1], src_ext, t_ext[1:-1])
    level = jnp.where(rows_in, level, jnp.float32(0.0))
    return plane_sweep(pad_last(level), k_pad[1:-1], pressure, src_ext[1:-1], trans)


def solution(mesh):
    return jax.shard_map(
        on_device,
        mesh=mesh,
        in_specs=(
            P("depth", "tile", None),
            P("depth", "tile", None),
            P("depth", "tile", None),
            P("depth", "tile", None),
            P("tile", None),
            P("tile", None),
            P(),
            P(),
        ),
        out_specs=P("tile", None),
        check_vma=False,
    )
```

```python
import functools

import jax
import jax.numpy as jnp
from jax import lax
from jax.experimental import pallas as pl
from jax.experimental.pallas import tpu as pltpu
from jax.sharding import PartitionSpec as P


def halo_swap(lo_face, hi_face, axis):
    count = lax.axis_size(axis)
    even = lax.axis_index(axis) % 2 == 0
    pairs_a = [(i, i ^ 1) for i in range(count)]
    pairs_b = [(i, i + 1) for i in range(1, count - 1, 2)] + [(i + 1, i) for i in range(1, count - 1, 2)]
    got_a = lax.ppermute(jnp.where(even, hi_face, lo_face), axis, pairs_a)
    got_b = lax.ppermute(jnp.where(even, lo_face, hi_face), axis, pairs_b)
    return jnp.where(even, got_b, got_a), jnp.where(even, got_a, got_b)


def diagonal_swap(lo_face, hi_face, flip):
    tiles = lax.axis_size("tile")
    depths = lax.axis_size("depth")
    even = lax.axis_index("tile") % 2 == 0
    pairs_a = [(t * depths + d, (t ^ 1) * depths + (d ^ flip)) for t in range(tiles) for d in range(depths)]
    pairs_b = []
    for t in range(1, tiles - 1, 2):
        for d in range(depths):
            pairs_b.append((t * depths + d, (t + 1) * depths + (d ^ flip)))
            pairs_b.append(((t + 1) * depths + (d ^ flip), t * depths + d))
    got_a = lax.ppermute(jnp.where(even, hi_face, lo_face), ("tile", "depth"), pairs_a)
    got_b = lax.ppermute(jnp.where(even, lo_face, hi_face), ("tile", "depth"), pairs_b)
    return jnp.where(even, got_b, got_a), jnp.where(even, got_a, got_b)


def butterfly_sum(part, axis):
    count = lax.axis_size(axis)
    order = [1 << k for k in range(1, count.bit_length() - 1)] + [1]
    for step in order:
        pairs = [(i, i ^ step) for i in range(lax.axis_size(axis))]
        part = part + lax.ppermute(part, axis, pairs)
    return part


def pad_last(stacked):
    widths = [(0, 0)] * (stacked.ndim - 1) + [(1, 1)]
    return jnp.pad(stacked, widths)


def flat_sides(padded):
    return [padded[2:, 1:-1], padded[:-2, 1:-1], padded[1:-1, 2:], padded[1:-1, :-2]]


def plane_sweep(p_pad, k_pad, anchor, source, trans):
    coef = jnp.zeros_like(trans)
    flow = jnp.zeros_like(trans)
    for k_side, p_side in zip(flat_sides(k_pad), flat_sides(p_pad)):
        face = 0.5 * (trans + k_side)
        coef = coef + face
        flow = flow + face * p_side
    return (anchor + source + flow) / (1.0 + coef)


def well_source(wells, rates, row_start, rows, cols, width):
    row_ids = row_start + jnp.arange(rows, dtype=jnp.int32)
    col_ids = jnp.arange(cols, dtype=jnp.int32)
    flat = row_ids[:, None] * width + col_ids[None, :]
    hit = flat[:, :, None] == wells[None, None, :]
    return 4.0 * jnp.sum(jnp.where(hit, rates[None, None, :], jnp.float32(0.0)), axis=-1)


def cube_sides(padded):
    return [
        padded[2:, 1:-1, 1:-1],
        padded[:-2, 1:-1, 1:-1],
        padded[1:-1, 2:, 1:-1],
        padded[1:-1, :-2, 1:-1],
        padded[1:-1, 1:-1, 2:],
        padded[1:-1, 1:-1, :-2],
    ]


X0 = 8


def neighbours(rows_all, width):
    col = lax.broadcasted_iota(jnp.int32, (rows_all, width), 1)
    has_next = col < width - 1
    has_prev = col > 0

    def y_next(a):
        return jnp.where(has_next, pltpu.roll(a, width - 1, 1), 0.0)

    def y_prev(a):
        return jnp.where(has_prev, pltpu.roll(a, 1, 1), 0.0)

    def x_next(a):
        return pltpu.roll(a, rows_all - 1, 0)

    def x_prev(a):
        return pltpu.roll(a, 1, 0)

    return x_next, x_prev, y_next, y_prev


def moved_at(uc, cc, up, down, nb, z_glob, load, x_in, total_depth):
    x_next, x_prev, y_next, y_prev = nb
    pairs = [
        up,
        down,
        (x_next(cc), x_next(uc)),
        (x_prev(cc), x_prev(uc)),
        (y_next(cc), y_next(uc)),
        (y_prev(cc), y_prev(uc)),
    ]
    coef = jnp.zeros_like(uc)
    flux = jnp.zeros_like(uc)
    for cn, un in pairs:
        face = 0.5 * (cc + cn)
        coef = coef + face
        flux = flux + face * (un - uc)
    force = jnp.where(z_glob == total_depth // 2, load, 0.0)
    moved = uc + 0.8 * (force + flux) / coef
    keep = x_in & (z_glob >= 0) & (z_glob < total_depth)
    return jnp.where(keep, moved, 0.0)


def opening_at(mc, m_up, m_down, dc, d_up, d_down, nb, mod, tough, dmg, own):
    x_next, x_prev, y_next, y_prev = nb
    energy = (
        (m_up - mc) ** 2 + (m_down - mc) ** 2 + (x_next(mc) - mc) ** 2 + (x_prev(mc) - mc) ** 2
        + (y_next(mc) - mc) ** 2 + (y_prev(mc) - mc) ** 2
    )
    beside = d_up + d_down + x_next(dc) + x_prev(dc) + y_next(dc) + y_prev(dc)
    energy = 0.25 * mod * energy[own]
    trial = (2.0 * energy + tough * beside[own]) / (7.0 * tough + 2.0 * energy)
    new_damage = jnp.maximum(dmg, trial)
    mo = mc[own]
    return new_damage * mo * mo


def x_frame(ids_ref, rows_all, width, total_rows):
    row = lax.broadcasted_iota(jnp.int32, (rows_all, width), 0)
    x_glob = ids_ref[1] + row - X0
    return (x_glob >= 0) & (x_glob < total_rows)


def interior_kernel(total_depth, total_rows, ids_ref, u_ref, dmg_ref, mod_ref, tgh_ref, xlo_ref, xhi_ref, load_ref,
                    part_ref, edge_ref, u_s, c_s, d_s, m_s):
    depth_cells, tile_cells, width = u_ref.shape
    rows_all = u_s.shape[1]
    own = slice(X0, X0 + tile_cells)
    top = X0 + tile_cells
    zero = jnp.zeros((rows_all, width), jnp.float32)

    def place(k, carry):
        dk = dmg_ref[k]
        u_s[k] = zero
        c_s[k] = zero
        d_s[k] = zero
        u_s[k, own] = u_ref[k]
        c_s[k, own] = ((1.0 - dk) ** 2 + 0.001) * mod_ref[k]
        d_s[k, own] = dk
        return carry

    lax.fori_loop(0, depth_cells, place, 0)
    dz = 4 * depth_cells
    for z in range(depth_cells):
        u_s[z, X0 - 2:X0] = xlo_ref[2 * z:2 * z + 2]
        c_s[z, X0 - 2:X0] = xlo_ref[2 * depth_cells + 2 * z:2 * depth_cells + 2 * z + 2]
        d_s[z, X0 - 1:X0] = xlo_ref[dz + z:dz + z + 1]
        u_s[z, top:top + 2] = xhi_ref[2 * z:2 * z + 2]
        c_s[z, top:top + 2] = xhi_ref[2 * depth_cells + 2 * z:2 * depth_cells + 2 * z + 2]
        d_s[z, top:top + 1] = xhi_ref[dz + z:dz + z + 1]

    nb = neighbours(rows_all, width)
    x_in = x_frame(ids_ref, rows_all, width, total_rows)
    load = load_ref[...]
    depth_start = ids_ref[0]

    def moved_body(k, carry):
        m_s[k] = moved_at(
            u_s[k], c_s[k], (c_s[k + 1], u_s[k + 1]), (c_s[k - 1], u_s[k - 1]), nb, depth_start + k, load, x_in,
            total_depth,
        )
        return carry

    lax.fori_loop(1, depth_cells - 1, moved_body, 0)

    def open_body(k, acc):
        return acc + opening_at(
            m_s[k], m_s[k + 1], m_s[k - 1], d_s[k], d_s[k + 1], d_s[k - 1], nb, mod_ref[k], tgh_ref[k], dmg_ref[k], own
        )

    acc = lax.fori_loop(2, depth_cells - 2, open_body, jnp.zeros((tile_cells, width), jnp.float32))
    part_ref[...] = acc
    edge_ref[0] = m_s[1]
    edge_ref[1] = m_s[2]
    edge_ref[2] = m_s[depth_cells - 3]
    edge_ref[3] = m_s[depth_cells - 2]


def boundary_kernel(total_depth, total_rows, ids_ref, u_ref, dmg_ref, mod_ref, tgh_ref, xlo_ref, xhi_ref, zlo_ref,
                    zhi_ref, edge_ref, part_ref, load_ref, out_ref, u_s, c_s, d_s, m_s):
    depth_cells, tile_cells, width = u_ref.shape
    rows_all = u_s.shape[1]
    own = slice(X0, X0 + tile_cells)
    wide = slice(X0 - 1, X0 + tile_cells + 1)
    top = X0 + tile_cells
    zero = jnp.zeros((rows_all, width), jnp.float32)
    for j in range(8):
        u_s[j] = zero
        c_s[j] = zero
        d_s[j] = zero
    ext = tile_cells + 2
    for side, ref, adj, sec in ((0, zlo_ref, 1, 0), (4, zhi_ref, 6, 7)):
        u_s[adj, wide] = ref[0:ext]
        c_s[adj, wide] = ref[ext:2 * ext]
        u_s[sec, own] = ref[2 * ext:2 * ext + tile_cells]
        c_s[sec, own] = ref[2 * ext + tile_cells:2 * ext + 2 * tile_cells]
    d_s[0, own] = zlo_ref[2 * ext + 2 * tile_cells:2 * ext + 3 * tile_cells]
    d_s[7, own] = zhi_ref[2 * ext + 2 * tile_cells:2 * ext + 3 * tile_cells]
    dz = 4 * depth_cells
    for slot, z in ((2, 0), (3, 1), (4, depth_cells - 2), (5, depth_cells - 1)):
        dk = dmg_ref[z]
        u_s[slot, own] = u_ref[z]
        c_s[slot, own] = ((1.0 - dk) ** 2 + 0.001) * mod_ref[z]
        u_s[slot, X0 - 2:X0] = xlo_ref[2 * z:2 * z + 2]
        c_s[slot, X0 - 2:X0] = xlo_ref[2 * depth_cells + 2 * z:2 * depth_cells + 2 * z + 2]
        u_s[slot, top:top + 2] = xhi_ref[2 * z:2 * z + 2]
        c_s[slot, top:top + 2] = xhi_ref[2 * depth_cells + 2 * z:2 * depth_cells + 2 * z + 2]
    for slot, z in ((1, 0), (2, 1), (5, depth_cells - 2), (6, depth_cells - 1)):
        d_s[slot, own] = dmg_ref[z]
        d_s[slot, X0 - 1:X0] = xlo_ref[dz + z:dz + z + 1]
        d_s[slot, top:top + 1] = xhi_ref[dz + z:dz + z + 1]
    d_s[3, own] = dmg_ref[2]
    d_s[4, own] = dmg_ref[depth_cells - 3]
    m_s[2] = edge_ref[0]
    m_s[3] = edge_ref[1]
    m_s[4] = edge_ref[2]
    m_s[5] = edge_ref[3]

    nb = neighbours(rows_all, width)
    x_in = x_frame(ids_ref, rows_all, width, total_rows)
    load = load_ref[...]
    depth_start = ids_ref[0]
    for us, ms, z in ((1, 0, -1), (2, 1, 0), (5, 6, depth_cells - 1), (6, 7, depth_cells)):
        m_s[ms] = moved_at(
            u_s[us], c_s[us], (c_s[us + 1], u_s[us + 1]), (c_s[us - 1], u_s[us - 1]), nb, depth_start + z, load, x_in,
            total_depth,
        )
    acc = part_ref[...]
    for ms, z in ((1, 0), (2, 1), (5, depth_cells - 2), (6, depth_cells - 1)):
        acc = acc + opening_at(
            m_s[ms], m_s[ms + 1], m_s[ms - 1], d_s[ms], d_s[ms + 1], d_s[ms - 1], nb, mod_ref[z], tgh_ref[z],
            dmg_ref[z], own,
        )
    out_ref[...] = (4.0 / total_depth) * acc


def on_device(displacement, damage, modulus, toughness, pressure, crack_mask, wells, rates):
    depth_cells, tile_cells, width = displacement.shape
    total_depth = depth_cells * lax.axis_size("depth")
    total_rows = tile_cells * lax.axis_size("tile")
    depth_start = lax.axis_index("depth") * depth_cells
    tile_start = lax.axis_index("tile") * tile_cells
    mask_f = crack_mask.astype(jnp.float32)
    rows_all = tile_cells + 2 * X0

    def stiff_of(dmg, mod):
        return ((1.0 - dmg) ** 2 + 0.001) * mod

    def tile_face(rows, edge):
        return jnp.concatenate(
            [
                displacement[:, rows].reshape(-1, width),
                stiff_of(damage[:, rows], modulus[:, rows]).reshape(-1, width),
                damage[:, edge],
                pressure[rows],
                mask_f[rows],
            ]
        )

    lo_x, hi_x = halo_swap(tile_face(slice(0, 2), 0), tile_face(slice(tile_cells - 2, tile_cells), tile_cells - 1), "tile")
    dz = 4 * depth_cells
    p_ext = jnp.concatenate([lo_x[dz + depth_cells:dz + depth_cells + 2], pressure, hi_x[dz + depth_cells:dz + depth_cells + 2]])
    m_ext = jnp.concatenate([lo_x[dz + depth_cells + 2:], mask_f, hi_x[dz + depth_cells + 2:]])
    load_all = jnp.pad(4.0 * m_ext[1:-1] * p_ext[1:-1], ((X0 - 1, X0 - 1), (0, 0)))
    ids = jnp.stack([depth_start, tile_start]).astype(jnp.int32)

    def depth_face(adj, sec):
        u_adj = jnp.concatenate([lo_x[2 * adj + 1:2 * adj + 2], displacement[adj], hi_x[2 * adj:2 * adj + 1]])
        c0 = 2 * depth_cells
        c_adj = jnp.concatenate(
            [lo_x[c0 + 2 * adj + 1:c0 + 2 * adj + 2], stiff_of(damage[adj], modulus[adj]), hi_x[c0 + 2 * adj:c0 + 2 * adj + 1]]
        )
        return jnp.concatenate([u_adj, c_adj, displacement[sec], stiff_of(damage[sec], modulus[sec]), damage[adj]])

    lo_z, hi_z = halo_swap(depth_face(0, 1), depth_face(depth_cells - 1, depth_cells - 2), "depth")

    vmem = pl.BlockSpec(memory_space=pltpu.VMEM)
    smem = pl.BlockSpec(memory_space=pltpu.SMEM)
    f32 = jnp.float32
    part_in, edge = pl.pallas_call(
        functools.partial(interior_kernel, total_depth, total_rows),
        out_shape=(
            jax.ShapeDtypeStruct((tile_cells, width), f32),
            jax.ShapeDtypeStruct((4, rows_all, width), f32),
        ),
        in_specs=[smem] + [vmem] * 7,
        out_specs=(vmem, vmem),
        scratch_shapes=[pltpu.VMEM((depth_cells, rows_all, width), f32)] * 4,
    )(ids, displacement, damage, modulus, toughness, lo_x, hi_x, load_all)
    partial_open = pl.pallas_call(
        functools.partial(boundary_kernel, total_depth, total_rows),
        out_shape=jax.ShapeDtypeStruct((tile_cells, width), f32),
        in_specs=[smem] + [vmem] * 11,
        out_specs=vmem,
        scratch_shapes=[pltpu.VMEM((8, rows_all, width), f32)] * 4,
    )(ids, displacement, damage, modulus, toughness, lo_x, hi_x, lo_z, hi_z, edge, part_in, load_all)

    depths = lax.axis_size("depth")
    part_y = partial_open
    for step in [1 << k for k in range(1, depths.bit_length() - 1)]:
        part_y = part_y + lax.ppermute(part_y, "depth", [(i, i ^ step) for i in range(depths)])
    far = lax.ppermute(part_y, "depth", [(i, i ^ 1) for i in range(depths)])
    n_lo, n_hi = halo_swap(part_y[:2], part_y[-2:], "tile")
    g_lo, g_hi = diagonal_swap(part_y[:2], part_y[-2:], 1)
    open_ext = jnp.concatenate([n_lo + g_lo, part_y + far, n_hi + g_hi])
    x_ids = tile_start - 1 + jnp.arange(tile_cells + 2, dtype=jnp.int32)
    x_ids2 = tile_start - 2 + jnp.arange(tile_cells + 4, dtype=jnp.int32)
    rows_in2 = ((x_ids2 >= 0) & (x_ids2 < total_rows))[:, None]
    t_ext = jnp.where(rows_in2, m_ext * (0.5 + open_ext) ** 3, jnp.float32(0.0))
    trans = t_ext[2:-2]
    rows_in = ((x_ids >= 0) & (x_ids < total_rows))[:, None]
    src_ext = well_source(wells, rates, tile_start - 1, tile_cells + 2, width, width)
    k_pad = pad_last(t_ext)
    level = plane_sweep(pad_last(p_ext), k_pad, p_ext[1:-1], src_ext, t_ext[1:-1])
    level = jnp.where(rows_in, level, jnp.float32(0.0))
    return plane_sweep(pad_last(level), k_pad[1:-1], pressure, src_ext[1:-1], trans)


def solution(mesh):
    return jax.shard_map(
        on_device,
        mesh=mesh,
        in_specs=(
            P("depth", "tile", None),
            P("depth", "tile", None),
            P("depth", "tile", None),
            P("depth", "tile", None),
            P("tile", None),
            P("tile", None),
            P(),
            P(),
        ),
        out_specs=P("tile", None),
        check_vma=False,
    )
```

```python
import functools

import jax
import jax.numpy as jnp
from jax import lax
from jax.experimental import pallas as pl
from jax.experimental.pallas import tpu as pltpu
from jax.sharding import PartitionSpec as P


def halo_swap(lo_face, hi_face, axis):
    count = lax.axis_size(axis)
    even = lax.axis_index(axis) % 2 == 0
    pairs_a = [(i, i ^ 1) for i in range(count)]
    pairs_b = [(i, i + 1) for i in range(1, count - 1, 2)] + [(i + 1, i) for i in range(1, count - 1, 2)]
    got_a = lax.ppermute(jnp.where(even, hi_face, lo_face), axis, pairs_a)
    got_b = lax.ppermute(jnp.where(even, lo_face, hi_face), axis, pairs_b)
    return jnp.where(even, got_b, got_a), jnp.where(even, got_a, got_b)


def butterfly_sum(part, axis):
    count = lax.axis_size(axis)
    order = [1 << k for k in range(1, count.bit_length() - 1)] + [1]
    for step in order:
        pairs = [(i, i ^ step) for i in range(lax.axis_size(axis))]
        part = part + lax.ppermute(part, axis, pairs)
    return part


def pad_last(stacked):
    widths = [(0, 0)] * (stacked.ndim - 1) + [(1, 1)]
    return jnp.pad(stacked, widths)


def flat_sides(padded):
    return [padded[2:, 1:-1], padded[:-2, 1:-1], padded[1:-1, 2:], padded[1:-1, :-2]]


def plane_sweep(p_pad, k_pad, anchor, source, trans):
    coef = jnp.zeros_like(trans)
    flow = jnp.zeros_like(trans)
    for k_side, p_side in zip(flat_sides(k_pad), flat_sides(p_pad)):
        face = 0.5 * (trans + k_side)
        coef = coef + face
        flow = flow + face * p_side
    return (anchor + source + flow) / (1.0 + coef)


def well_source(wells, rates, row_start, rows, cols, width):
    row_ids = row_start + jnp.arange(rows, dtype=jnp.int32)
    col_ids = jnp.arange(cols, dtype=jnp.int32)
    flat = row_ids[:, None] * width + col_ids[None, :]
    hit = flat[:, :, None] == wells[None, None, :]
    return 4.0 * jnp.sum(jnp.where(hit, rates[None, None, :], jnp.float32(0.0)), axis=-1)


def cube_sides(padded):
    return [
        padded[2:, 1:-1, 1:-1],
        padded[:-2, 1:-1, 1:-1],
        padded[1:-1, 2:, 1:-1],
        padded[1:-1, :-2, 1:-1],
        padded[1:-1, 1:-1, 2:],
        padded[1:-1, 1:-1, :-2],
    ]


X0 = 8


def neighbours(rows_all, width):
    col = lax.broadcasted_iota(jnp.int32, (rows_all, width), 1)
    has_next = col < width - 1
    has_prev = col > 0

    def y_next(a):
        return jnp.where(has_next, pltpu.roll(a, width - 1, 1), 0.0)

    def y_prev(a):
        return jnp.where(has_prev, pltpu.roll(a, 1, 1), 0.0)

    def x_next(a):
        return pltpu.roll(a, rows_all - 1, 0)

    def x_prev(a):
        return pltpu.roll(a, 1, 0)

    return x_next, x_prev, y_next, y_prev


def moved_at(uc, cc, up, down, nb, z_glob, load, x_in, total_depth):
    x_next, x_prev, y_next, y_prev = nb
    pairs = [
        up,
        down,
        (x_next(cc), x_next(uc)),
        (x_prev(cc), x_prev(uc)),
        (y_next(cc), y_next(uc)),
        (y_prev(cc), y_prev(uc)),
    ]
    coef = jnp.zeros_like(uc)
    flux = jnp.zeros_like(uc)
    for cn, un in pairs:
        face = 0.5 * (cc + cn)
        coef = coef + face
        flux = flux + face * (un - uc)
    force = jnp.where(z_glob == total_depth // 2, load, 0.0)
    moved = uc + 0.8 * (force + flux) / coef
    keep = x_in & (z_glob >= 0) & (z_glob < total_depth)
    return jnp.where(keep, moved, 0.0)


def opening_at(mc, m_up, m_down, dc, d_up, d_down, nb, mod, tough, dmg, own):
    x_next, x_prev, y_next, y_prev = nb
    energy = (
        (m_up - mc) ** 2 + (m_down - mc) ** 2 + (x_next(mc) - mc) ** 2 + (x_prev(mc) - mc) ** 2
        + (y_next(mc) - mc) ** 2 + (y_prev(mc) - mc) ** 2
    )
    beside = d_up + d_down + x_next(dc) + x_prev(dc) + y_next(dc) + y_prev(dc)
    energy = 0.25 * mod * energy[own]
    trial = (2.0 * energy + tough * beside[own]) / (7.0 * tough + 2.0 * energy)
    new_damage = jnp.maximum(dmg, trial)
    mo = mc[own]
    return new_damage * mo * mo


def x_frame(ids_ref, rows_all, width, total_rows):
    row = lax.broadcasted_iota(jnp.int32, (rows_all, width), 0)
    x_glob = ids_ref[1] + row - X0
    return (x_glob >= 0) & (x_glob < total_rows)


def interior_kernel(total_depth, total_rows, ids_ref, u_ref, dmg_ref, mod_ref, tgh_ref, xlo_ref, xhi_ref, load_ref,
                    part_ref, edge_ref, u_s, c_s, d_s, m_s):
    depth_cells, tile_cells, width = u_ref.shape
    rows_all = u_s.shape[1]
    own = slice(X0, X0 + tile_cells)
    top = X0 + tile_cells
    zero = jnp.zeros((rows_all, width), jnp.float32)

    def place(k, carry):
        dk = dmg_ref[k]
        u_s[k] = zero
        c_s[k] = zero
        d_s[k] = zero
        u_s[k, own] = u_ref[k]
        c_s[k, own] = ((1.0 - dk) ** 2 + 0.001) * mod_ref[k]
        d_s[k, own] = dk
        return carry

    lax.fori_loop(0, depth_cells, place, 0)
    dz = 4 * depth_cells
    for z in range(depth_cells):
        u_s[z, X0 - 2:X0] = xlo_ref[2 * z:2 * z + 2]
        c_s[z, X0 - 2:X0] = xlo_ref[2 * depth_cells + 2 * z:2 * depth_cells + 2 * z + 2]
        d_s[z, X0 - 1:X0] = xlo_ref[dz + z:dz + z + 1]
        u_s[z, top:top + 2] = xhi_ref[2 * z:2 * z + 2]
        c_s[z, top:top + 2] = xhi_ref[2 * depth_cells + 2 * z:2 * depth_cells + 2 * z + 2]
        d_s[z, top:top + 1] = xhi_ref[dz + z:dz + z + 1]

    nb = neighbours(rows_all, width)
    x_in = x_frame(ids_ref, rows_all, width, total_rows)
    load = load_ref[...]
    depth_start = ids_ref[0]

    def moved_body(k, carry):
        m_s[k] = moved_at(
            u_s[k], c_s[k], (c_s[k + 1], u_s[k + 1]), (c_s[k - 1], u_s[k - 1]), nb, depth_start + k, load, x_in,
            total_depth,
        )
        return carry

    lax.fori_loop(1, depth_cells - 1, moved_body, 0)

    def open_body(k, acc):
        return acc + opening_at(
            m_s[k], m_s[k + 1], m_s[k - 1], d_s[k], d_s[k + 1], d_s[k - 1], nb, mod_ref[k], tgh_ref[k], dmg_ref[k], own
        )

    acc = lax.fori_loop(2, depth_cells - 2, open_body, jnp.zeros((tile_cells, width), jnp.float32))
    part_ref[...] = acc
    edge_ref[0] = m_s[1]
    edge_ref[1] = m_s[2]
    edge_ref[2] = m_s[depth_cells - 3]
    edge_ref[3] = m_s[depth_cells - 2]


def side_kernel(total_depth, total_rows, first, ids_ref, u_ref, dmg_ref, mod_ref, tgh_ref, xlo_ref, xhi_ref, halo_ref,
                edge_ref, load_ref, out_ref, u_s, c_s, d_s, m_s):
    depth_cells, tile_cells, width = u_ref.shape
    rows_all = u_s.shape[1]
    own = slice(X0, X0 + tile_cells)
    wide = slice(X0 - 1, X0 + tile_cells + 1)
    top = X0 + tile_cells
    ext = tile_cells + 2
    dz = 4 * depth_cells
    zero = jnp.zeros((rows_all, width), jnp.float32)
    odd = ids_ref[2]

    def run(is_top):
        for j in range(4):
            u_s[j] = zero
            c_s[j] = zero
            d_s[j] = zero
        adj, sec, d_halo = (2, 3, 3) if is_top else (1, 0, 0)
        u_s[adj, wide] = halo_ref[0:ext]
        c_s[adj, wide] = halo_ref[ext:2 * ext]
        u_s[sec, own] = halo_ref[2 * ext:2 * ext + tile_cells]
        c_s[sec, own] = halo_ref[2 * ext + tile_cells:2 * ext + 2 * tile_cells]
        d_s[d_halo, own] = halo_ref[2 * ext + 2 * tile_cells:2 * ext + 3 * tile_cells]
        base = depth_cells - 2 if is_top else 0
        u_slots = (0, 1) if is_top else (2, 3)
        for slot, z in zip(u_slots, (base, base + 1)):
            dk = dmg_ref[z]
            u_s[slot, own] = u_ref[z]
            c_s[slot, own] = ((1.0 - dk) ** 2 + 0.001) * mod_ref[z]
            u_s[slot, X0 - 2:X0] = xlo_ref[2 * z:2 * z + 2]
            c_s[slot, X0 - 2:X0] = xlo_ref[2 * depth_cells + 2 * z:2 * depth_cells + 2 * z + 2]
            u_s[slot, top:top + 2] = xhi_ref[2 * z:2 * z + 2]
            c_s[slot, top:top + 2] = xhi_ref[2 * depth_cells + 2 * z:2 * depth_cells + 2 * z + 2]
        for slot, z in zip((1, 2), (base, base + 1)):
            d_s[slot, own] = dmg_ref[z]
            d_s[slot, X0 - 1:X0] = xlo_ref[dz + z:dz + z + 1]
            d_s[slot, top:top + 1] = xhi_ref[dz + z:dz + z + 1]
        if is_top:
            d_s[0, own] = dmg_ref[depth_cells - 3]
            m_s[0] = edge_ref[2]
            m_s[1] = edge_ref[3]
            moves = ((1, 2, depth_cells - 1), (2, 3, depth_cells))
        else:
            d_s[3, own] = dmg_ref[2]
            m_s[2] = edge_ref[0]
            m_s[3] = edge_ref[1]
            moves = ((1, 0, -1), (2, 1, 0))
        nb = neighbours(rows_all, width)
        x_in = x_frame(ids_ref, rows_all, width, total_rows)
        load = load_ref[...]
        depth_start = ids_ref[0]
        for us, ms, z in moves:
            m_s[ms] = moved_at(
                u_s[us], c_s[us], (c_s[us + 1], u_s[us + 1]), (c_s[us - 1], u_s[us - 1]), nb, depth_start + z, load,
                x_in, total_depth,
            )
        acc = jnp.zeros((tile_cells, width), jnp.float32)
        for ms, z in zip((1, 2), (base, base + 1)):
            acc = acc + opening_at(
                m_s[ms], m_s[ms + 1], m_s[ms - 1], d_s[ms], d_s[ms + 1], d_s[ms - 1], nb, mod_ref[z], tgh_ref[z],
                dmg_ref[z], own,
            )
        out_ref[...] = acc

    @pl.when(odd == (0 if first else 1))
    def _():
        run(True)

    @pl.when(odd == (1 if first else 0))
    def _():
        run(False)


def on_device(displacement, damage, modulus, toughness, pressure, crack_mask, wells, rates):
    depth_cells, tile_cells, width = displacement.shape
    total_depth = depth_cells * lax.axis_size("depth")
    total_rows = tile_cells * lax.axis_size("tile")
    depth_start = lax.axis_index("depth") * depth_cells
    tile_start = lax.axis_index("tile") * tile_cells
    mask_f = crack_mask.astype(jnp.float32)
    rows_all = tile_cells + 2 * X0

    def stiff_of(dmg, mod):
        return ((1.0 - dmg) ** 2 + 0.001) * mod

    def tile_face(rows, edge):
        return jnp.concatenate(
            [
                displacement[:, rows].reshape(-1, width),
                stiff_of(damage[:, rows], modulus[:, rows]).reshape(-1, width),
                damage[:, edge],
                pressure[rows],
                mask_f[rows],
            ]
        )

    lo_x, hi_x = halo_swap(tile_face(slice(0, 2), 0), tile_face(slice(tile_cells - 2, tile_cells), tile_cells - 1), "tile")
    dz = 4 * depth_cells
    p_ext = jnp.concatenate([lo_x[dz + depth_cells:dz + depth_cells + 2], pressure, hi_x[dz + depth_cells:dz + depth_cells + 2]])
    m_ext = jnp.concatenate([lo_x[dz + depth_cells + 2:], mask_f, hi_x[dz + depth_cells + 2:]])
    load_all = jnp.pad(4.0 * m_ext[1:-1] * p_ext[1:-1], ((X0 - 1, X0 - 1), (0, 0)))
    ids = jnp.stack([depth_start, tile_start, lax.axis_index("depth") % 2]).astype(jnp.int32)

    def depth_face(adj, sec):
        u_adj = jnp.concatenate([lo_x[2 * adj + 1:2 * adj + 2], displacement[adj], hi_x[2 * adj:2 * adj + 1]])
        c0 = 2 * depth_cells
        c_adj = jnp.concatenate(
            [lo_x[c0 + 2 * adj + 1:c0 + 2 * adj + 2], stiff_of(damage[adj], modulus[adj]), hi_x[c0 + 2 * adj:c0 + 2 * adj + 1]]
        )
        return jnp.concatenate([u_adj, c_adj, displacement[sec], stiff_of(damage[sec], modulus[sec]), damage[adj]])

    depths = lax.axis_size("depth")
    even_z = lax.axis_index("depth") % 2 == 0
    lo_face, hi_face = depth_face(0, 1), depth_face(depth_cells - 1, depth_cells - 2)
    got_a = lax.ppermute(jnp.where(even_z, hi_face, lo_face), "depth", [(i, i ^ 1) for i in range(depths)])
    pairs_b = [(i, i + 1) for i in range(1, depths - 1, 2)] + [(i + 1, i) for i in range(1, depths - 1, 2)]
    got_b = lax.ppermute(jnp.where(even_z, lo_face, hi_face), "depth", pairs_b)

    vmem = pl.BlockSpec(memory_space=pltpu.VMEM)
    smem = pl.BlockSpec(memory_space=pltpu.SMEM)
    f32 = jnp.float32
    part_in, edge = pl.pallas_call(
        functools.partial(interior_kernel, total_depth, total_rows),
        out_shape=(
            jax.ShapeDtypeStruct((tile_cells, width), f32),
            jax.ShapeDtypeStruct((4, rows_all, width), f32),
        ),
        in_specs=[smem] + [vmem] * 7,
        out_specs=(vmem, vmem),
        scratch_shapes=[pltpu.VMEM((depth_cells, rows_all, width), f32)] * 4,
    )(ids, displacement, damage, modulus, toughness, lo_x, hi_x, load_all)
    sides = []
    for first, got in ((True, got_a), (False, got_b)):
        sides.append(pl.pallas_call(
            functools.partial(side_kernel, total_depth, total_rows, first),
            out_shape=jax.ShapeDtypeStruct((tile_cells, width), f32),
            in_specs=[smem] + [vmem] * 9,
            out_specs=vmem,
            scratch_shapes=[pltpu.VMEM((4, rows_all, width), f32)] * 4,
        )(ids, displacement, damage, modulus, toughness, lo_x, hi_x, got, edge, load_all))
    partial_open = (4.0 / total_depth) * ((part_in + sides[0]) + sides[1])
    aperture = 0.5 + butterfly_sum(partial_open, "depth")
    trans = mask_f * aperture**3

    t_lo, t_hi = halo_swap(trans[:2], trans[-2:], "tile")
    t_ext = jnp.concatenate([t_lo, trans, t_hi])
    x_ids = tile_start - 1 + jnp.arange(tile_cells + 2, dtype=jnp.int32)
    rows_in = ((x_ids >= 0) & (x_ids < total_rows))[:, None]
    src_ext = well_source(wells, rates, tile_start - 1, tile_cells + 2, width, width)
    k_pad = pad_last(t_ext)
    level = plane_sweep(pad_last(p_ext), k_pad, p_ext[1:-1], src_ext, t_ext[1:-1])
    level = jnp.where(rows_in, level, jnp.float32(0.0))
    return plane_sweep(pad_last(level), k_pad[1:-1], pressure, src_ext[1:-1], trans)


def solution(mesh):
    return jax.shard_map(
        on_device,
        mesh=mesh,
        in_specs=(
            P("depth", "tile", None),
            P("depth", "tile", None),
            P("depth", "tile", None),
            P("depth", "tile", None),
            P("tile", None),
            P("tile", None),
            P(),
            P(),
        ),
        out_specs=P("tile", None),
        check_vma=False,
    )
```

```python
import functools

import jax
import jax.numpy as jnp
from jax import lax
from jax.experimental import pallas as pl
from jax.experimental.pallas import tpu as pltpu
from jax.sharding import PartitionSpec as P


def halo_swap(lo_face, hi_face, axis):
    count = lax.axis_size(axis)
    even = lax.axis_index(axis) % 2 == 0
    pairs_a = [(i, i ^ 1) for i in range(count)]
    pairs_b = [(i, i + 1) for i in range(1, count - 1, 2)] + [(i + 1, i) for i in range(1, count - 1, 2)]
    got_a = lax.ppermute(jnp.where(even, hi_face, lo_face), axis, pairs_a)
    got_b = lax.ppermute(jnp.where(even, lo_face, hi_face), axis, pairs_b)
    return jnp.where(even, got_b, got_a), jnp.where(even, got_a, got_b)


def butterfly_sum(part, axis):
    count = lax.axis_size(axis)
    order = [1 << k for k in range(1, count.bit_length() - 1)] + [1]
    for step in order:
        pairs = [(i, i ^ step) for i in range(lax.axis_size(axis))]
        part = part + lax.ppermute(part, axis, pairs)
    return part


def pad_last(stacked):
    widths = [(0, 0)] * (stacked.ndim - 1) + [(1, 1)]
    return jnp.pad(stacked, widths)


def flat_sides(padded):
    return [padded[2:, 1:-1], padded[:-2, 1:-1], padded[1:-1, 2:], padded[1:-1, :-2]]


def plane_sweep(p_pad, k_pad, anchor, source, trans):
    coef = jnp.zeros_like(trans)
    flow = jnp.zeros_like(trans)
    for k_side, p_side in zip(flat_sides(k_pad), flat_sides(p_pad)):
        face = 0.5 * (trans + k_side)
        coef = coef + face
        flow = flow + face * p_side
    return (anchor + source + flow) / (1.0 + coef)


def well_source(wells, rates, row_start, rows, cols, width):
    row_ids = row_start + jnp.arange(rows, dtype=jnp.int32)
    col_ids = jnp.arange(cols, dtype=jnp.int32)
    flat = row_ids[:, None] * width + col_ids[None, :]
    hit = flat[:, :, None] == wells[None, None, :]
    return 4.0 * jnp.sum(jnp.where(hit, rates[None, None, :], jnp.float32(0.0)), axis=-1)


def cube_sides(padded):
    return [
        padded[2:, 1:-1, 1:-1],
        padded[:-2, 1:-1, 1:-1],
        padded[1:-1, 2:, 1:-1],
        padded[1:-1, :-2, 1:-1],
        padded[1:-1, 1:-1, 2:],
        padded[1:-1, 1:-1, :-2],
    ]


X0 = 8


def neighbours(rows_all, width):
    col = lax.broadcasted_iota(jnp.int32, (rows_all, width), 1)
    has_next = col < width - 1
    has_prev = col > 0

    def y_next(a):
        return jnp.where(has_next, pltpu.roll(a, width - 1, 1), 0.0)

    def y_prev(a):
        return jnp.where(has_prev, pltpu.roll(a, 1, 1), 0.0)

    def x_next(a):
        return pltpu.roll(a, rows_all - 1, 0)

    def x_prev(a):
        return pltpu.roll(a, 1, 0)

    return x_next, x_prev, y_next, y_prev


def moved_at(uc, cc, up, down, nb, z_glob, load, x_in, total_depth):
    x_next, x_prev, y_next, y_prev = nb
    pairs = [
        up,
        down,
        (x_next(cc), x_next(uc)),
        (x_prev(cc), x_prev(uc)),
        (y_next(cc), y_next(uc)),
        (y_prev(cc), y_prev(uc)),
    ]
    coef = jnp.zeros_like(uc)
    flux = jnp.zeros_like(uc)
    for cn, un in pairs:
        face = 0.5 * (cc + cn)
        coef = coef + face
        flux = flux + face * (un - uc)
    force = jnp.where(z_glob == total_depth // 2, load, 0.0)
    moved = uc + 0.8 * (force + flux) / coef
    keep = x_in & (z_glob >= 0) & (z_glob < total_depth)
    return jnp.where(keep, moved, 0.0)


def opening_at(mc, m_up, m_down, dc, d_up, d_down, nb, mod, tough, dmg, own):
    x_next, x_prev, y_next, y_prev = nb
    energy = (
        (m_up - mc) ** 2 + (m_down - mc) ** 2 + (x_next(mc) - mc) ** 2 + (x_prev(mc) - mc) ** 2
        + (y_next(mc) - mc) ** 2 + (y_prev(mc) - mc) ** 2
    )
    beside = d_up + d_down + x_next(dc) + x_prev(dc) + y_next(dc) + y_prev(dc)
    energy = 0.25 * mod * energy[own]
    trial = (2.0 * energy + tough * beside[own]) / (7.0 * tough + 2.0 * energy)
    new_damage = jnp.maximum(dmg, trial)
    mo = mc[own]
    return new_damage * mo * mo


def x_frame(ids_ref, rows_all, width, total_rows):
    row = lax.broadcasted_iota(jnp.int32, (rows_all, width), 0)
    x_glob = ids_ref[1] + row - X0
    return (x_glob >= 0) & (x_glob < total_rows)


def interior_kernel(total_depth, total_rows, ids_ref, u_ref, dmg_ref, mod_ref, tgh_ref, xlo_ref, xhi_ref, load_ref,
                    part_ref, edge_ref, u_s, c_s, d_s, m_s):
    depth_cells, tile_cells, width = u_ref.shape
    rows_all = u_s.shape[1]
    own = slice(X0, X0 + tile_cells)
    top = X0 + tile_cells
    zero = jnp.zeros((rows_all, width), jnp.float32)

    def place(k, carry):
        dk = dmg_ref[k]
        u_s[k] = zero
        c_s[k] = zero
        d_s[k] = zero
        u_s[k, own] = u_ref[k]
        c_s[k, own] = ((1.0 - dk) ** 2 + 0.001) * mod_ref[k]
        d_s[k, own] = dk
        return carry

    lax.fori_loop(0, depth_cells, place, 0)
    dz = 4 * depth_cells
    for z in range(depth_cells):
        u_s[z, X0 - 2:X0] = xlo_ref[2 * z:2 * z + 2]
        c_s[z, X0 - 2:X0] = xlo_ref[2 * depth_cells + 2 * z:2 * depth_cells + 2 * z + 2]
        d_s[z, X0 - 1:X0] = xlo_ref[dz + z:dz + z + 1]
        u_s[z, top:top + 2] = xhi_ref[2 * z:2 * z + 2]
        c_s[z, top:top + 2] = xhi_ref[2 * depth_cells + 2 * z:2 * depth_cells + 2 * z + 2]
        d_s[z, top:top + 1] = xhi_ref[dz + z:dz + z + 1]

    nb = neighbours(rows_all, width)
    x_in = x_frame(ids_ref, rows_all, width, total_rows)
    load = load_ref[...]
    depth_start = ids_ref[0]

    def moved_body(k, carry):
        m_s[k] = moved_at(
            u_s[k], c_s[k], (c_s[k + 1], u_s[k + 1]), (c_s[k - 1], u_s[k - 1]), nb, depth_start + k, load, x_in,
            total_depth,
        )
        return carry

    lax.fori_loop(1, depth_cells - 1, moved_body, 0)

    def open_body(k, acc):
        return acc + opening_at(
            m_s[k], m_s[k + 1], m_s[k - 1], d_s[k], d_s[k + 1], d_s[k - 1], nb, mod_ref[k], tgh_ref[k], dmg_ref[k], own
        )

    acc = lax.fori_loop(2, depth_cells - 2, open_body, jnp.zeros((tile_cells, width), jnp.float32))
    part_ref[...] = acc
    edge_ref[0] = m_s[1]
    edge_ref[1] = m_s[2]
    edge_ref[2] = m_s[depth_cells - 3]
    edge_ref[3] = m_s[depth_cells - 2]


def side_kernel(total_depth, total_rows, depth_cells, first, ids_ref, u_ref, dmg_ref, mod_ref, tgh_ref, xlo_ref, xhi_ref, halo_ref,
                edge_ref, load_ref, out_ref, u_s, c_s, d_s, m_s):
    _, tile_cells, width = u_ref.shape

    def loc(z):
        return z if z < 3 else z - depth_cells + 6

    rows_all = u_s.shape[1]
    own = slice(X0, X0 + tile_cells)
    wide = slice(X0 - 1, X0 + tile_cells + 1)
    top = X0 + tile_cells
    ext = tile_cells + 2
    dz = 4 * depth_cells
    zero = jnp.zeros((rows_all, width), jnp.float32)
    odd = ids_ref[2]

    def run(is_top):
        for j in range(4):
            u_s[j] = zero
            c_s[j] = zero
            d_s[j] = zero
        adj, sec, d_halo = (2, 3, 3) if is_top else (1, 0, 0)
        u_s[adj, wide] = halo_ref[0:ext]
        c_s[adj, wide] = halo_ref[ext:2 * ext]
        u_s[sec, own] = halo_ref[2 * ext:2 * ext + tile_cells]
        c_s[sec, own] = halo_ref[2 * ext + tile_cells:2 * ext + 2 * tile_cells]
        d_s[d_halo, own] = halo_ref[2 * ext + 2 * tile_cells:2 * ext + 3 * tile_cells]
        base = depth_cells - 2 if is_top else 0
        u_slots = (0, 1) if is_top else (2, 3)
        for slot, z in zip(u_slots, (base, base + 1)):
            dk = dmg_ref[loc(z)]
            u_s[slot, own] = u_ref[loc(z)]
            c_s[slot, own] = ((1.0 - dk) ** 2 + 0.001) * mod_ref[loc(z)]
            u_s[slot, X0 - 2:X0] = xlo_ref[2 * z:2 * z + 2]
            c_s[slot, X0 - 2:X0] = xlo_ref[2 * depth_cells + 2 * z:2 * depth_cells + 2 * z + 2]
            u_s[slot, top:top + 2] = xhi_ref[2 * z:2 * z + 2]
            c_s[slot, top:top + 2] = xhi_ref[2 * depth_cells + 2 * z:2 * depth_cells + 2 * z + 2]
        for slot, z in zip((1, 2), (base, base + 1)):
            d_s[slot, own] = dmg_ref[loc(z)]
            d_s[slot, X0 - 1:X0] = xlo_ref[dz + z:dz + z + 1]
            d_s[slot, top:top + 1] = xhi_ref[dz + z:dz + z + 1]
        if is_top:
            d_s[0, own] = dmg_ref[loc(depth_cells - 3)]
            m_s[0] = edge_ref[2]
            m_s[1] = edge_ref[3]
            moves = ((1, 2, depth_cells - 1), (2, 3, depth_cells))
        else:
            d_s[3, own] = dmg_ref[loc(2)]
            m_s[2] = edge_ref[0]
            m_s[3] = edge_ref[1]
            moves = ((1, 0, -1), (2, 1, 0))
        nb = neighbours(rows_all, width)
        x_in = x_frame(ids_ref, rows_all, width, total_rows)
        load = load_ref[...]
        depth_start = ids_ref[0]
        for us, ms, z in moves:
            m_s[ms] = moved_at(
                u_s[us], c_s[us], (c_s[us + 1], u_s[us + 1]), (c_s[us - 1], u_s[us - 1]), nb, depth_start + z, load,
                x_in, total_depth,
            )
        acc = jnp.zeros((tile_cells, width), jnp.float32)
        for ms, z in zip((1, 2), (base, base + 1)):
            acc = acc + opening_at(
                m_s[ms], m_s[ms + 1], m_s[ms - 1], d_s[ms], d_s[ms + 1], d_s[ms - 1], nb, mod_ref[loc(z)], tgh_ref[loc(z)],
                dmg_ref[loc(z)], own,
            )
        out_ref[...] = acc

    @pl.when(odd == (0 if first else 1))
    def _():
        run(True)

    @pl.when(odd == (1 if first else 0))
    def _():
        run(False)


def on_device(displacement, damage, modulus, toughness, pressure, crack_mask, wells, rates):
    depth_cells, tile_cells, width = displacement.shape
    total_depth = depth_cells * lax.axis_size("depth")
    total_rows = tile_cells * lax.axis_size("tile")
    depth_start = lax.axis_index("depth") * depth_cells
    tile_start = lax.axis_index("tile") * tile_cells
    mask_f = crack_mask.astype(jnp.float32)
    rows_all = tile_cells + 2 * X0

    def stiff_of(dmg, mod):
        return ((1.0 - dmg) ** 2 + 0.001) * mod

    def tile_face(rows, edge):
        return jnp.concatenate(
            [
                displacement[:, rows].reshape(-1, width),
                stiff_of(damage[:, rows], modulus[:, rows]).reshape(-1, width),
                damage[:, edge],
                pressure[rows],
                mask_f[rows],
            ]
        )

    lo_x, hi_x = halo_swap(tile_face(slice(0, 2), 0), tile_face(slice(tile_cells - 2, tile_cells), tile_cells - 1), "tile")
    dz = 4 * depth_cells
    p_ext = jnp.concatenate([lo_x[dz + depth_cells:dz + depth_cells + 2], pressure, hi_x[dz + depth_cells:dz + depth_cells + 2]])
    m_ext = jnp.concatenate([lo_x[dz + depth_cells + 2:], mask_f, hi_x[dz + depth_cells + 2:]])
    load_all = jnp.pad(4.0 * m_ext[1:-1] * p_ext[1:-1], ((X0 - 1, X0 - 1), (0, 0)))
    ids = jnp.stack([depth_start, tile_start, lax.axis_index("depth") % 2]).astype(jnp.int32)

    def depth_face(adj, sec):
        u_adj = jnp.concatenate([lo_x[2 * adj + 1:2 * adj + 2], displacement[adj], hi_x[2 * adj:2 * adj + 1]])
        c0 = 2 * depth_cells
        c_adj = jnp.concatenate(
            [lo_x[c0 + 2 * adj + 1:c0 + 2 * adj + 2], stiff_of(damage[adj], modulus[adj]), hi_x[c0 + 2 * adj:c0 + 2 * adj + 1]]
        )
        return jnp.concatenate([u_adj, c_adj, displacement[sec], stiff_of(damage[sec], modulus[sec]), damage[adj]])

    depths = lax.axis_size("depth")
    even_z = lax.axis_index("depth") % 2 == 0
    lo_face, hi_face = depth_face(0, 1), depth_face(depth_cells - 1, depth_cells - 2)
    got_a = lax.ppermute(jnp.where(even_z, hi_face, lo_face), "depth", [(i, i ^ 1) for i in range(depths)])
    pairs_b = [(i, i + 1) for i in range(1, depths - 1, 2)] + [(i + 1, i) for i in range(1, depths - 1, 2)]
    got_b = lax.ppermute(jnp.where(even_z, lo_face, hi_face), "depth", pairs_b)

    vmem = pl.BlockSpec(memory_space=pltpu.VMEM)
    smem = pl.BlockSpec(memory_space=pltpu.SMEM)
    f32 = jnp.float32
    part_in, edge = pl.pallas_call(
        functools.partial(interior_kernel, total_depth, total_rows),
        out_shape=(
            jax.ShapeDtypeStruct((tile_cells, width), f32),
            jax.ShapeDtypeStruct((4, rows_all, width), f32),
        ),
        in_specs=[smem] + [vmem] * 7,
        out_specs=(vmem, vmem),
        scratch_shapes=[pltpu.VMEM((depth_cells, rows_all, width), f32)] * 4,
    )(ids, displacement, damage, modulus, toughness, lo_x, hi_x, load_all)
    ends = [jnp.concatenate([a[:3], a[-3:]]) for a in (displacement, damage, modulus, toughness)]
    sides = []
    for first, got in ((True, got_a), (False, got_b)):
        sides.append(pl.pallas_call(
            functools.partial(side_kernel, total_depth, total_rows, depth_cells, first),
            out_shape=jax.ShapeDtypeStruct((tile_cells, width), f32),
            in_specs=[smem] + [vmem] * 9,
            out_specs=vmem,
            scratch_shapes=[pltpu.VMEM((4, rows_all, width), f32)] * 4,
        )(ids, *ends, lo_x, hi_x, got, edge, load_all))
    partial_open = (4.0 / total_depth) * ((part_in + sides[0]) + sides[1])
    aperture = 0.5 + butterfly_sum(partial_open, "depth")
    trans = mask_f * aperture**3

    t_lo, t_hi = halo_swap(trans[:2], trans[-2:], "tile")
    t_ext = jnp.concatenate([t_lo, trans, t_hi])
    x_ids = tile_start - 1 + jnp.arange(tile_cells + 2, dtype=jnp.int32)
    rows_in = ((x_ids >= 0) & (x_ids < total_rows))[:, None]
    src_ext = well_source(wells, rates, tile_start - 1, tile_cells + 2, width, width)
    k_pad = pad_last(t_ext)
    level = plane_sweep(pad_last(p_ext), k_pad, p_ext[1:-1], src_ext, t_ext[1:-1])
    level = jnp.where(rows_in, level, jnp.float32(0.0))
    return plane_sweep(pad_last(level), k_pad[1:-1], pressure, src_ext[1:-1], trans)


def solution(mesh):
    return jax.shard_map(
        on_device,
        mesh=mesh,
        in_specs=(
            P("depth", "tile", None),
            P("depth", "tile", None),
            P("depth", "tile", None),
            P("depth", "tile", None),
            P("tile", None),
            P("tile", None),
            P(),
            P(),
        ),
        out_specs=P("tile", None),
        check_vma=False,
    )
```

```python
import functools

import jax
import jax.numpy as jnp
from jax import lax
from jax.experimental import pallas as pl
from jax.experimental.pallas import tpu as pltpu
from jax.sharding import PartitionSpec as P


def halo_swap(lo_face, hi_face, axis):
    count = lax.axis_size(axis)
    even = lax.axis_index(axis) % 2 == 0
    pairs_a = [(i, i ^ 1) for i in range(count)]
    pairs_b = [(i, i + 1) for i in range(1, count - 1, 2)] + [(i + 1, i) for i in range(1, count - 1, 2)]
    got_a = lax.ppermute(jnp.where(even, hi_face, lo_face), axis, pairs_a)
    got_b = lax.ppermute(jnp.where(even, lo_face, hi_face), axis, pairs_b)
    return jnp.where(even, got_b, got_a), jnp.where(even, got_a, got_b)


def butterfly_sum(part, axis):
    count = lax.axis_size(axis)
    order = [1 << k for k in range(1, count.bit_length() - 1)] + [1]
    for step in order:
        pairs = [(i, i ^ step) for i in range(lax.axis_size(axis))]
        part = part + lax.ppermute(part, axis, pairs)
    return part


def pad_last(stacked):
    widths = [(0, 0)] * (stacked.ndim - 1) + [(1, 1)]
    return jnp.pad(stacked, widths)


def flat_sides(padded):
    return [padded[2:, 1:-1], padded[:-2, 1:-1], padded[1:-1, 2:], padded[1:-1, :-2]]


def plane_sweep(p_pad, k_pad, anchor, source, trans):
    coef = jnp.zeros_like(trans)
    flow = jnp.zeros_like(trans)
    for k_side, p_side in zip(flat_sides(k_pad), flat_sides(p_pad)):
        face = 0.5 * (trans + k_side)
        coef = coef + face
        flow = flow + face * p_side
    return (anchor + source + flow) / (1.0 + coef)


def well_source(wells, rates, row_start, rows, cols, width):
    row_ids = row_start + jnp.arange(rows, dtype=jnp.int32)
    col_ids = jnp.arange(cols, dtype=jnp.int32)
    flat = row_ids[:, None] * width + col_ids[None, :]
    hit = flat[:, :, None] == wells[None, None, :]
    return 4.0 * jnp.sum(jnp.where(hit, rates[None, None, :], jnp.float32(0.0)), axis=-1)


def cube_sides(padded):
    return [
        padded[2:, 1:-1, 1:-1],
        padded[:-2, 1:-1, 1:-1],
        padded[1:-1, 2:, 1:-1],
        padded[1:-1, :-2, 1:-1],
        padded[1:-1, 1:-1, 2:],
        padded[1:-1, 1:-1, :-2],
    ]


X0 = 8


def neighbours(rows_all, width):
    col = lax.broadcasted_iota(jnp.int32, (rows_all, width), 1)
    has_next = col < width - 1
    has_prev = col > 0

    def y_next(a):
        return jnp.where(has_next, pltpu.roll(a, width - 1, 1), 0.0)

    def y_prev(a):
        return jnp.where(has_prev, pltpu.roll(a, 1, 1), 0.0)

    def x_next(a):
        return pltpu.roll(a, rows_all - 1, 0)

    def x_prev(a):
        return pltpu.roll(a, 1, 0)

    return x_next, x_prev, y_next, y_prev


def moved_at(uc, cc, up, down, nb, z_glob, load, x_in, total_depth):
    x_next, x_prev, y_next, y_prev = nb
    pairs = [
        up,
        down,
        (x_next(cc), x_next(uc)),
        (x_prev(cc), x_prev(uc)),
        (y_next(cc), y_next(uc)),
        (y_prev(cc), y_prev(uc)),
    ]
    coef = jnp.zeros_like(uc)
    flux = jnp.zeros_like(uc)
    for cn, un in pairs:
        face = 0.5 * (cc + cn)
        coef = coef + face
        flux = flux + face * (un - uc)
    force = jnp.where(z_glob == total_depth // 2, load, 0.0)
    moved = uc + 0.8 * (force + flux) / coef
    keep = x_in & (z_glob >= 0) & (z_glob < total_depth)
    return jnp.where(keep, moved, 0.0)


def opening_at(mc, m_up, m_down, dc, d_up, d_down, nb, mod, tough, dmg, own):
    x_next, x_prev, y_next, y_prev = nb
    energy = (
        (m_up - mc) ** 2 + (m_down - mc) ** 2 + (x_next(mc) - mc) ** 2 + (x_prev(mc) - mc) ** 2
        + (y_next(mc) - mc) ** 2 + (y_prev(mc) - mc) ** 2
    )
    beside = d_up + d_down + x_next(dc) + x_prev(dc) + y_next(dc) + y_prev(dc)
    energy = 0.25 * mod * energy[own]
    trial = (2.0 * energy + tough * beside[own]) / (7.0 * tough + 2.0 * energy)
    new_damage = jnp.maximum(dmg, trial)
    mo = mc[own]
    return new_damage * mo * mo


def x_frame(ids_ref, rows_all, width, total_rows):
    row = lax.broadcasted_iota(jnp.int32, (rows_all, width), 0)
    x_glob = ids_ref[1] + row - X0
    return (x_glob >= 0) & (x_glob < total_rows)


def interior_kernel(total_depth, total_rows, ids_ref, u_ref, dmg_ref, mod_ref, tgh_ref, xlo_ref, xhi_ref, load_ref,
                    part_ref, edge_ref, u_s, c_s, d_s, m_s):
    depth_cells, tile_cells, width = u_ref.shape
    rows_all = u_s.shape[1]
    own = slice(X0, X0 + tile_cells)
    top = X0 + tile_cells
    zero = jnp.zeros((rows_all, width), jnp.float32)

    def place(k, carry):
        dk = dmg_ref[k]
        u_s[k] = zero
        c_s[k] = zero
        d_s[k] = zero
        u_s[k, own] = u_ref[k]
        c_s[k, own] = ((1.0 - dk) ** 2 + 0.001) * mod_ref[k]
        d_s[k, own] = dk
        return carry

    lax.fori_loop(0, depth_cells, place, 0)
    dz = 4 * depth_cells
    for z in range(depth_cells):
        u_s[z, X0 - 2:X0] = xlo_ref[2 * z:2 * z + 2]
        c_s[z, X0 - 2:X0] = xlo_ref[2 * depth_cells + 2 * z:2 * depth_cells + 2 * z + 2]
        d_s[z, X0 - 1:X0] = xlo_ref[dz + z:dz + z + 1]
        u_s[z, top:top + 2] = xhi_ref[2 * z:2 * z + 2]
        c_s[z, top:top + 2] = xhi_ref[2 * depth_cells + 2 * z:2 * depth_cells + 2 * z + 2]
        d_s[z, top:top + 1] = xhi_ref[dz + z:dz + z + 1]

    nb = neighbours(rows_all, width)
    x_in = x_frame(ids_ref, rows_all, width, total_rows)
    load = load_ref[...]
    depth_start = ids_ref[0]

    def moved_body(k, carry):
        m_s[k] = moved_at(
            u_s[k], c_s[k], (c_s[k + 1], u_s[k + 1]), (c_s[k - 1], u_s[k - 1]), nb, depth_start + k, load, x_in,
            total_depth,
        )
        return carry

    lax.fori_loop(1, depth_cells - 1, moved_body, 0)

    def open_body(k, acc):
        return acc + opening_at(
            m_s[k], m_s[k + 1], m_s[k - 1], d_s[k], d_s[k + 1], d_s[k - 1], nb, mod_ref[k], tgh_ref[k], dmg_ref[k], own
        )

    acc = lax.fori_loop(2, depth_cells - 2, open_body, jnp.zeros((tile_cells, width), jnp.float32))
    part_ref[...] = acc
    edge_ref[0] = m_s[1]
    edge_ref[1] = m_s[2]
    edge_ref[2] = m_s[depth_cells - 3]
    edge_ref[3] = m_s[depth_cells - 2]


def side_kernel(total_depth, total_rows, depth_cells, first, ids_ref, u_ref, dmg_ref, mod_ref, tgh_ref, xlo_ref, xhi_ref, halo_ref,
                edge_ref, load_ref, out_ref, u_s, c_s, d_s, m_s):
    _, tile_cells, width = u_ref.shape

    def loc(z):
        return z if z < 3 else z - depth_cells + 6

    rows_all = u_s.shape[1]
    own = slice(X0, X0 + tile_cells)
    wide = slice(X0 - 1, X0 + tile_cells + 1)
    top = X0 + tile_cells
    ext = tile_cells + 2
    dz = 4 * depth_cells
    zero = jnp.zeros((rows_all, width), jnp.float32)
    odd = ids_ref[2]

    def run(is_top):
        for j in range(4):
            u_s[j] = zero
            c_s[j] = zero
            d_s[j] = zero
        adj, sec, d_halo = (2, 3, 3) if is_top else (1, 0, 0)
        u_s[adj, wide] = halo_ref[0:ext]
        c_s[adj, wide] = halo_ref[ext:2 * ext]
        u_s[sec, own] = halo_ref[2 * ext:2 * ext + tile_cells]
        c_s[sec, own] = halo_ref[2 * ext + tile_cells:2 * ext + 2 * tile_cells]
        d_s[d_halo, own] = halo_ref[2 * ext + 2 * tile_cells:2 * ext + 3 * tile_cells]
        base = depth_cells - 2 if is_top else 0
        u_slots = (0, 1) if is_top else (2, 3)
        for slot, z in zip(u_slots, (base, base + 1)):
            dk = dmg_ref[loc(z)]
            u_s[slot, own] = u_ref[loc(z)]
            c_s[slot, own] = ((1.0 - dk) ** 2 + 0.001) * mod_ref[loc(z)]
            u_s[slot, X0 - 2:X0] = xlo_ref[2 * z:2 * z + 2]
            c_s[slot, X0 - 2:X0] = xlo_ref[2 * depth_cells + 2 * z:2 * depth_cells + 2 * z + 2]
            u_s[slot, top:top + 2] = xhi_ref[2 * z:2 * z + 2]
            c_s[slot, top:top + 2] = xhi_ref[2 * depth_cells + 2 * z:2 * depth_cells + 2 * z + 2]
        for slot, z in zip((1, 2), (base, base + 1)):
            d_s[slot, own] = dmg_ref[loc(z)]
            d_s[slot, X0 - 1:X0] = xlo_ref[dz + z:dz + z + 1]
            d_s[slot, top:top + 1] = xhi_ref[dz + z:dz + z + 1]
        if is_top:
            d_s[0, own] = dmg_ref[loc(depth_cells - 3)]
            m_s[0] = edge_ref[2]
            m_s[1] = edge_ref[3]
            moves = ((1, 2, depth_cells - 1), (2, 3, depth_cells))
        else:
            d_s[3, own] = dmg_ref[loc(2)]
            m_s[2] = edge_ref[0]
            m_s[3] = edge_ref[1]
            moves = ((1, 0, -1), (2, 1, 0))
        nb = neighbours(rows_all, width)
        x_in = x_frame(ids_ref, rows_all, width, total_rows)
        load = load_ref[...]
        depth_start = ids_ref[0]
        for us, ms, z in moves:
            m_s[ms] = moved_at(
                u_s[us], c_s[us], (c_s[us + 1], u_s[us + 1]), (c_s[us - 1], u_s[us - 1]), nb, depth_start + z, load,
                x_in, total_depth,
            )
        acc = jnp.zeros((tile_cells, width), jnp.float32)
        for ms, z in zip((1, 2), (base, base + 1)):
            acc = acc + opening_at(
                m_s[ms], m_s[ms + 1], m_s[ms - 1], d_s[ms], d_s[ms + 1], d_s[ms - 1], nb, mod_ref[loc(z)], tgh_ref[loc(z)],
                dmg_ref[loc(z)], own,
            )
        out_ref[...] = acc

    @pl.when(odd == (0 if first else 1))
    def _():
        run(True)

    @pl.when(odd == (1 if first else 0))
    def _():
        run(False)


def on_device(displacement, damage, modulus, toughness, pressure, crack_mask, wells, rates):
    depth_cells, tile_cells, width = displacement.shape
    total_depth = depth_cells * lax.axis_size("depth")
    total_rows = tile_cells * lax.axis_size("tile")
    depth_start = lax.axis_index("depth") * depth_cells
    tile_start = lax.axis_index("tile") * tile_cells
    mask_f = crack_mask.astype(jnp.float32)
    rows_all = tile_cells + 2 * X0

    def stiff_of(dmg, mod):
        return ((1.0 - dmg) ** 2 + 0.001) * mod

    def tile_face(rows, edge):
        return jnp.concatenate(
            [
                displacement[:, rows].reshape(-1, width),
                stiff_of(damage[:, rows], modulus[:, rows]).reshape(-1, width),
                damage[:, edge],
                pressure[rows],
                mask_f[rows],
            ]
        )

    lo_x, hi_x = halo_swap(tile_face(slice(0, 2), 0), tile_face(slice(tile_cells - 2, tile_cells), tile_cells - 1), "tile")
    dz = 4 * depth_cells
    p_ext = jnp.concatenate([lo_x[dz + depth_cells:dz + depth_cells + 2], pressure, hi_x[dz + depth_cells:dz + depth_cells + 2]])
    m_ext = jnp.concatenate([lo_x[dz + depth_cells + 2:], mask_f, hi_x[dz + depth_cells + 2:]])
    load_all = jnp.pad(4.0 * m_ext[1:-1] * p_ext[1:-1], ((X0 - 1, X0 - 1), (0, 0)))
    ids = jnp.stack([depth_start, tile_start, lax.axis_index("depth") % 2]).astype(jnp.int32)

    def depth_face(adj, sec):
        u_adj = jnp.concatenate([lo_x[2 * adj + 1:2 * adj + 2], displacement[adj], hi_x[2 * adj:2 * adj + 1]])
        c0 = 2 * depth_cells
        c_adj = jnp.concatenate(
            [lo_x[c0 + 2 * adj + 1:c0 + 2 * adj + 2], stiff_of(damage[adj], modulus[adj]), hi_x[c0 + 2 * adj:c0 + 2 * adj + 1]]
        )
        return jnp.concatenate([u_adj, c_adj, displacement[sec], stiff_of(damage[sec], modulus[sec]), damage[adj]])

    depths = lax.axis_size("depth")
    even_z = lax.axis_index("depth") % 2 == 0
    lo_face, hi_face = depth_face(0, 1), depth_face(depth_cells - 1, depth_cells - 2)
    got_a = lax.ppermute(jnp.where(even_z, hi_face, lo_face), "depth", [(i, i ^ 1) for i in range(depths)])
    pairs_b = [(i, i + 1) for i in range(1, depths - 1, 2)] + [(i + 1, i) for i in range(1, depths - 1, 2)]
    got_b = lax.ppermute(jnp.where(even_z, lo_face, hi_face), "depth", pairs_b)

    vmem = pl.BlockSpec(memory_space=pltpu.VMEM)
    smem = pl.BlockSpec(memory_space=pltpu.SMEM)
    f32 = jnp.float32
    part_in, edge = pl.pallas_call(
        functools.partial(interior_kernel, total_depth, total_rows),
        out_shape=(
            jax.ShapeDtypeStruct((tile_cells, width), f32),
            jax.ShapeDtypeStruct((4, rows_all, width), f32),
        ),
        in_specs=[smem] + [vmem] * 7,
        out_specs=(vmem, vmem),
        scratch_shapes=[pltpu.VMEM((depth_cells, rows_all, width), f32)] * 4,
    )(ids, displacement, damage, modulus, toughness, lo_x, hi_x, load_all)
    late = lax.optimization_barrier((displacement, damage, modulus, toughness, lo_x))[:4]
    ends = [jnp.concatenate([a[:3], a[-3:]]) for a in late]
    sides = []
    for first, got in ((True, got_a), (False, got_b)):
        sides.append(pl.pallas_call(
            functools.partial(side_kernel, total_depth, total_rows, depth_cells, first),
            out_shape=jax.ShapeDtypeStruct((tile_cells, width), f32),
            in_specs=[smem] + [vmem] * 9,
            out_specs=vmem,
            scratch_shapes=[pltpu.VMEM((4, rows_all, width), f32)] * 4,
        )(ids, *ends, lo_x, hi_x, got, edge, load_all))
    partial_open = (4.0 / total_depth) * ((part_in + sides[0]) + sides[1])
    aperture = 0.5 + butterfly_sum(partial_open, "depth")
    trans = mask_f * aperture**3

    t_lo, t_hi = halo_swap(trans[:2], trans[-2:], "tile")
    t_ext = jnp.concatenate([t_lo, trans, t_hi])
    x_ids = tile_start - 1 + jnp.arange(tile_cells + 2, dtype=jnp.int32)
    rows_in = ((x_ids >= 0) & (x_ids < total_rows))[:, None]
    src_ext = well_source(wells, rates, tile_start - 1, tile_cells + 2, width, width)
    k_pad = pad_last(t_ext)
    level = plane_sweep(pad_last(p_ext), k_pad, p_ext[1:-1], src_ext, t_ext[1:-1])
    level = jnp.where(rows_in, level, jnp.float32(0.0))
    return plane_sweep(pad_last(level), k_pad[1:-1], pressure, src_ext[1:-1], trans)


def solution(mesh):
    return jax.shard_map(
        on_device,
        mesh=mesh,
        in_specs=(
            P("depth", "tile", None),
            P("depth", "tile", None),
            P("depth", "tile", None),
            P("depth", "tile", None),
            P("tile", None),
            P("tile", None),
            P(),
            P(),
        ),
        out_specs=P("tile", None),
        check_vma=False,
    )
```

```python
import functools

import jax
import jax.numpy as jnp
from jax import lax
from jax.experimental import pallas as pl
from jax.experimental.pallas import tpu as pltpu
from jax.sharding import PartitionSpec as P


def halo_swap(lo_face, hi_face, axis):
    count = lax.axis_size(axis)
    even = lax.axis_index(axis) % 2 == 0
    pairs_a = [(i, i ^ 1) for i in range(count)]
    pairs_b = [(i, i + 1) for i in range(1, count - 1, 2)] + [(i + 1, i) for i in range(1, count - 1, 2)]
    got_a = lax.ppermute(jnp.where(even, hi_face, lo_face), axis, pairs_a)
    got_b = lax.ppermute(jnp.where(even, lo_face, hi_face), axis, pairs_b)
    return jnp.where(even, got_b, got_a), jnp.where(even, got_a, got_b)


def butterfly_sum(part, axis):
    count = lax.axis_size(axis)
    order = [1 << k for k in range(1, count.bit_length() - 1)] + [1]
    for step in order:
        pairs = [(i, i ^ step) for i in range(lax.axis_size(axis))]
        part = part + lax.ppermute(part, axis, pairs)
    return part


def pad_last(stacked):
    widths = [(0, 0)] * (stacked.ndim - 1) + [(1, 1)]
    return jnp.pad(stacked, widths)


def flat_sides(padded):
    return [padded[2:, 1:-1], padded[:-2, 1:-1], padded[1:-1, 2:], padded[1:-1, :-2]]


def plane_sweep(p_pad, k_pad, anchor, source, trans):
    coef = jnp.zeros_like(trans)
    flow = jnp.zeros_like(trans)
    for k_side, p_side in zip(flat_sides(k_pad), flat_sides(p_pad)):
        face = 0.5 * (trans + k_side)
        coef = coef + face
        flow = flow + face * p_side
    return (anchor + source + flow) / (1.0 + coef)


def well_source(wells, rates, row_start, rows, cols, width):
    row_ids = row_start + jnp.arange(rows, dtype=jnp.int32)
    col_ids = jnp.arange(cols, dtype=jnp.int32)
    flat = row_ids[:, None] * width + col_ids[None, :]
    hit = flat[:, :, None] == wells[None, None, :]
    return 4.0 * jnp.sum(jnp.where(hit, rates[None, None, :], jnp.float32(0.0)), axis=-1)


def cube_sides(padded):
    return [
        padded[2:, 1:-1, 1:-1],
        padded[:-2, 1:-1, 1:-1],
        padded[1:-1, 2:, 1:-1],
        padded[1:-1, :-2, 1:-1],
        padded[1:-1, 1:-1, 2:],
        padded[1:-1, 1:-1, :-2],
    ]


X0 = 8


def neighbours(rows_all, width):
    col = lax.broadcasted_iota(jnp.int32, (rows_all, width), 1)
    has_next = col < width - 1
    has_prev = col > 0

    def y_next(a):
        return jnp.where(has_next, pltpu.roll(a, width - 1, 1), 0.0)

    def y_prev(a):
        return jnp.where(has_prev, pltpu.roll(a, 1, 1), 0.0)

    def x_next(a):
        return pltpu.roll(a, rows_all - 1, 0)

    def x_prev(a):
        return pltpu.roll(a, 1, 0)

    return x_next, x_prev, y_next, y_prev


def moved_at(uc, cc, up, down, nb, z_glob, load, x_in, total_depth):
    x_next, x_prev, y_next, y_prev = nb
    pairs = [
        up,
        down,
        (x_next(cc), x_next(uc)),
        (x_prev(cc), x_prev(uc)),
        (y_next(cc), y_next(uc)),
        (y_prev(cc), y_prev(uc)),
    ]
    coef = jnp.zeros_like(uc)
    flux = jnp.zeros_like(uc)
    for cn, un in pairs:
        face = 0.5 * (cc + cn)
        coef = coef + face
        flux = flux + face * (un - uc)
    force = jnp.where(z_glob == total_depth // 2, load, 0.0)
    moved = uc + 0.8 * (force + flux) / coef
    keep = x_in & (z_glob >= 0) & (z_glob < total_depth)
    return jnp.where(keep, moved, 0.0)


def opening_at(mc, m_up, m_down, dc, d_up, d_down, nb, mod, tough, dmg, own):
    x_next, x_prev, y_next, y_prev = nb
    energy = (
        (m_up - mc) ** 2 + (m_down - mc) ** 2 + (x_next(mc) - mc) ** 2 + (x_prev(mc) - mc) ** 2
        + (y_next(mc) - mc) ** 2 + (y_prev(mc) - mc) ** 2
    )
    beside = d_up + d_down + x_next(dc) + x_prev(dc) + y_next(dc) + y_prev(dc)
    energy = 0.25 * mod * energy[own]
    trial = (2.0 * energy + tough * beside[own]) / (7.0 * tough + 2.0 * energy)
    new_damage = jnp.maximum(dmg, trial)
    mo = mc[own]
    return new_damage * mo * mo


def x_frame(ids_ref, rows_all, width, total_rows):
    row = lax.broadcasted_iota(jnp.int32, (rows_all, width), 0)
    x_glob = ids_ref[1] + row - X0
    return (x_glob >= 0) & (x_glob < total_rows)


def interior_kernel(total_depth, total_rows, ids_ref, u_ref, dmg_ref, mod_ref, tgh_ref, xlo_ref, xhi_ref, load_ref,
                    part_ref, edge_ref, u_s, c_s, d_s, m_s):
    depth_cells, tile_cells, width = u_ref.shape
    rows_all = u_s.shape[1]
    own = slice(X0, X0 + tile_cells)
    top = X0 + tile_cells
    zero = jnp.zeros((rows_all, width), jnp.float32)

    def place(k, carry):
        dk = dmg_ref[k]
        u_s[k] = zero
        c_s[k] = zero
        d_s[k] = zero
        u_s[k, own] = u_ref[k]
        c_s[k, own] = ((1.0 - dk) ** 2 + 0.001) * mod_ref[k]
        d_s[k, own] = dk
        return carry

    lax.fori_loop(0, depth_cells, place, 0)
    dz = 4 * depth_cells
    for z in range(depth_cells):
        u_s[z, X0 - 2:X0] = xlo_ref[2 * z:2 * z + 2]
        c_s[z, X0 - 2:X0] = xlo_ref[2 * depth_cells + 2 * z:2 * depth_cells + 2 * z + 2]
        d_s[z, X0 - 1:X0] = xlo_ref[dz + z:dz + z + 1]
        u_s[z, top:top + 2] = xhi_ref[2 * z:2 * z + 2]
        c_s[z, top:top + 2] = xhi_ref[2 * depth_cells + 2 * z:2 * depth_cells + 2 * z + 2]
        d_s[z, top:top + 1] = xhi_ref[dz + z:dz + z + 1]

    nb = neighbours(rows_all, width)
    x_in = x_frame(ids_ref, rows_all, width, total_rows)
    load = load_ref[...]
    depth_start = ids_ref[0]

    def moved_body(k, carry):
        m_s[k] = moved_at(
            u_s[k], c_s[k], (c_s[k + 1], u_s[k + 1]), (c_s[k - 1], u_s[k - 1]), nb, depth_start + k, load, x_in,
            total_depth,
        )
        return carry

    lax.fori_loop(1, depth_cells - 1, moved_body, 0)

    def open_body(k, acc):
        return acc + opening_at(
            m_s[k], m_s[k + 1], m_s[k - 1], d_s[k], d_s[k + 1], d_s[k - 1], nb, mod_ref[k], tgh_ref[k], dmg_ref[k], own
        )

    acc = lax.fori_loop(2, depth_cells - 2, open_body, jnp.zeros((tile_cells, width), jnp.float32))
    part_ref[...] = acc
    edge_ref[0] = m_s[1]
    edge_ref[1] = m_s[2]
    edge_ref[2] = m_s[depth_cells - 3]
    edge_ref[3] = m_s[depth_cells - 2]


class Ends:
    def __init__(self, lo, hi, depth_cells):
        self.lo, self.hi, self.depth_cells = lo, hi, depth_cells

    def __getitem__(self, z):
        return self.lo[z] if z < 4 else self.hi[z - self.depth_cells + 4]


def boundary_kernel(total_depth, total_rows, depth_cells, ids_ref, u_lo, u_hi, d_lo, d_hi, mod_lo, mod_hi, tgh_lo,
                    tgh_hi, xlo_ref, xhi_ref, zlo_ref, zhi_ref, edge_ref, part_ref, load_ref, out_ref, u_s, c_s, d_s,
                    m_s):
    u_ref = Ends(u_lo, u_hi, depth_cells)
    dmg_ref = Ends(d_lo, d_hi, depth_cells)
    mod_ref = Ends(mod_lo, mod_hi, depth_cells)
    tgh_ref = Ends(tgh_lo, tgh_hi, depth_cells)
    _, tile_cells, width = u_lo.shape
    rows_all = u_s.shape[1]
    own = slice(X0, X0 + tile_cells)
    wide = slice(X0 - 1, X0 + tile_cells + 1)
    top = X0 + tile_cells
    zero = jnp.zeros((rows_all, width), jnp.float32)
    for j in range(8):
        u_s[j] = zero
        c_s[j] = zero
        d_s[j] = zero
    ext = tile_cells + 2
    for side, ref, adj, sec in ((0, zlo_ref, 1, 0), (4, zhi_ref, 6, 7)):
        u_s[adj, wide] = ref[0:ext]
        c_s[adj, wide] = ref[ext:2 * ext]
        u_s[sec, own] = ref[2 * ext:2 * ext + tile_cells]
        c_s[sec, own] = ref[2 * ext + tile_cells:2 * ext + 2 * tile_cells]
    d_s[0, own] = zlo_ref[2 * ext + 2 * tile_cells:2 * ext + 3 * tile_cells]
    d_s[7, own] = zhi_ref[2 * ext + 2 * tile_cells:2 * ext + 3 * tile_cells]
    dz = 4 * depth_cells
    for slot, z in ((2, 0), (3, 1), (4, depth_cells - 2), (5, depth_cells - 1)):
        dk = dmg_ref[z]
        u_s[slot, own] = u_ref[z]
        c_s[slot, own] = ((1.0 - dk) ** 2 + 0.001) * mod_ref[z]
        u_s[slot, X0 - 2:X0] = xlo_ref[2 * z:2 * z + 2]
        c_s[slot, X0 - 2:X0] = xlo_ref[2 * depth_cells + 2 * z:2 * depth_cells + 2 * z + 2]
        u_s[slot, top:top + 2] = xhi_ref[2 * z:2 * z + 2]
        c_s[slot, top:top + 2] = xhi_ref[2 * depth_cells + 2 * z:2 * depth_cells + 2 * z + 2]
    for slot, z in ((1, 0), (2, 1), (5, depth_cells - 2), (6, depth_cells - 1)):
        d_s[slot, own] = dmg_ref[z]
        d_s[slot, X0 - 1:X0] = xlo_ref[dz + z:dz + z + 1]
        d_s[slot, top:top + 1] = xhi_ref[dz + z:dz + z + 1]
    d_s[3, own] = dmg_ref[2]
    d_s[4, own] = dmg_ref[depth_cells - 3]
    m_s[2] = edge_ref[0]
    m_s[3] = edge_ref[1]
    m_s[4] = edge_ref[2]
    m_s[5] = edge_ref[3]

    nb = neighbours(rows_all, width)
    x_in = x_frame(ids_ref, rows_all, width, total_rows)
    load = load_ref[...]
    depth_start = ids_ref[0]
    for us, ms, z in ((1, 0, -1), (2, 1, 0), (5, 6, depth_cells - 1), (6, 7, depth_cells)):
        m_s[ms] = moved_at(
            u_s[us], c_s[us], (c_s[us + 1], u_s[us + 1]), (c_s[us - 1], u_s[us - 1]), nb, depth_start + z, load, x_in,
            total_depth,
        )
    acc = part_ref[...]
    for ms, z in ((1, 0), (2, 1), (5, depth_cells - 2), (6, depth_cells - 1)):
        acc = acc + opening_at(
            m_s[ms], m_s[ms + 1], m_s[ms - 1], d_s[ms], d_s[ms + 1], d_s[ms - 1], nb, mod_ref[z], tgh_ref[z],
            dmg_ref[z], own,
        )
    out_ref[...] = (4.0 / total_depth) * acc


def on_device(displacement, damage, modulus, toughness, pressure, crack_mask, wells, rates):
    depth_cells, tile_cells, width = displacement.shape
    total_depth = depth_cells * lax.axis_size("depth")
    total_rows = tile_cells * lax.axis_size("tile")
    depth_start = lax.axis_index("depth") * depth_cells
    tile_start = lax.axis_index("tile") * tile_cells
    mask_f = crack_mask.astype(jnp.float32)
    rows_all = tile_cells + 2 * X0

    def stiff_of(dmg, mod):
        return ((1.0 - dmg) ** 2 + 0.001) * mod

    def tile_face(rows, edge):
        return jnp.concatenate(
            [
                displacement[:, rows].reshape(-1, width),
                stiff_of(damage[:, rows], modulus[:, rows]).reshape(-1, width),
                damage[:, edge],
                pressure[rows],
                mask_f[rows],
            ]
        )

    lo_x, hi_x = halo_swap(tile_face(slice(0, 2), 0), tile_face(slice(tile_cells - 2, tile_cells), tile_cells - 1), "tile")
    dz = 4 * depth_cells
    p_ext = jnp.concatenate([lo_x[dz + depth_cells:dz + depth_cells + 2], pressure, hi_x[dz + depth_cells:dz + depth_cells + 2]])
    m_ext = jnp.concatenate([lo_x[dz + depth_cells + 2:], mask_f, hi_x[dz + depth_cells + 2:]])
    load_all = jnp.pad(4.0 * m_ext[1:-1] * p_ext[1:-1], ((X0 - 1, X0 - 1), (0, 0)))
    ids = jnp.stack([depth_start, tile_start]).astype(jnp.int32)

    def depth_face(adj, sec):
        u_adj = jnp.concatenate([lo_x[2 * adj + 1:2 * adj + 2], displacement[adj], hi_x[2 * adj:2 * adj + 1]])
        c0 = 2 * depth_cells
        c_adj = jnp.concatenate(
            [lo_x[c0 + 2 * adj + 1:c0 + 2 * adj + 2], stiff_of(damage[adj], modulus[adj]), hi_x[c0 + 2 * adj:c0 + 2 * adj + 1]]
        )
        return jnp.concatenate([u_adj, c_adj, displacement[sec], stiff_of(damage[sec], modulus[sec]), damage[adj]])

    lo_z, hi_z = halo_swap(depth_face(0, 1), depth_face(depth_cells - 1, depth_cells - 2), "depth")

    vmem = pl.BlockSpec(memory_space=pltpu.VMEM)
    smem = pl.BlockSpec(memory_space=pltpu.SMEM)
    f32 = jnp.float32
    part_in, edge = pl.pallas_call(
        functools.partial(interior_kernel, total_depth, total_rows),
        out_shape=(
            jax.ShapeDtypeStruct((tile_cells, width), f32),
            jax.ShapeDtypeStruct((4, rows_all, width), f32),
        ),
        in_specs=[smem] + [vmem] * 7,
        out_specs=(vmem, vmem),
        scratch_shapes=[pltpu.VMEM((depth_cells, rows_all, width), f32)] * 4,
    )(ids, displacement, damage, modulus, toughness, lo_x, hi_x, load_all)
    end_lo = pl.BlockSpec((4, tile_cells, width), lambda i: (0, 0, 0))
    end_hi = pl.BlockSpec((4, tile_cells, width), lambda i: (depth_cells // 4 - 1, 0, 0))
    partial_open = pl.pallas_call(
        functools.partial(boundary_kernel, total_depth, total_rows, depth_cells),
        out_shape=jax.ShapeDtypeStruct((tile_cells, width), f32),
        grid=(1,),
        in_specs=[smem] + [end_lo, end_hi] * 4 + [vmem] * 7,
        out_specs=vmem,
        scratch_shapes=[pltpu.VMEM((8, rows_all, width), f32)] * 4,
    )(ids, displacement, displacement, damage, damage, modulus, modulus, toughness, toughness, lo_x, hi_x, lo_z, hi_z,
      edge, part_in, load_all)

    aperture = 0.5 + butterfly_sum(partial_open, "depth")
    trans = mask_f * aperture**3

    t_lo, t_hi = halo_swap(trans[:2], trans[-2:], "tile")
    t_ext = jnp.concatenate([t_lo, trans, t_hi])
    x_ids = tile_start - 1 + jnp.arange(tile_cells + 2, dtype=jnp.int32)
    rows_in = ((x_ids >= 0) & (x_ids < total_rows))[:, None]
    src_ext = well_source(wells, rates, tile_start - 1, tile_cells + 2, width, width)
    k_pad = pad_last(t_ext)
    level = plane_sweep(pad_last(p_ext), k_pad, p_ext[1:-1], src_ext, t_ext[1:-1])
    level = jnp.where(rows_in, level, jnp.float32(0.0))
    return plane_sweep(pad_last(level), k_pad[1:-1], pressure, src_ext[1:-1], trans)


def solution(mesh):
    return jax.shard_map(
        on_device,
        mesh=mesh,
        in_specs=(
            P("depth", "tile", None),
            P("depth", "tile", None),
            P("depth", "tile", None),
            P("depth", "tile", None),
            P("tile", None),
            P("tile", None),
            P(),
            P(),
        ),
        out_specs=P("tile", None),
        check_vma=False,
    )
```

```python
import functools

import jax
import jax.numpy as jnp
from jax import lax
from jax.experimental import pallas as pl
from jax.experimental.pallas import tpu as pltpu
from jax.sharding import PartitionSpec as P


def halo_swap(lo_face, hi_face, axis):
    count = lax.axis_size(axis)
    even = lax.axis_index(axis) % 2 == 0
    pairs_a = [(i, i ^ 1) for i in range(count)]
    pairs_b = [(i, i + 1) for i in range(1, count - 1, 2)] + [(i + 1, i) for i in range(1, count - 1, 2)]
    got_a = lax.ppermute(jnp.where(even, hi_face, lo_face), axis, pairs_a)
    got_b = lax.ppermute(jnp.where(even, lo_face, hi_face), axis, pairs_b)
    return jnp.where(even, got_b, got_a), jnp.where(even, got_a, got_b)


def butterfly_sum(part, axis):
    count = lax.axis_size(axis)
    order = [1 << k for k in range(1, count.bit_length() - 1)] + [1]
    for step in order:
        pairs = [(i, i ^ step) for i in range(lax.axis_size(axis))]
        part = part + lax.ppermute(part, axis, pairs)
    return part


def pad_last(stacked):
    widths = [(0, 0)] * (stacked.ndim - 1) + [(1, 1)]
    return jnp.pad(stacked, widths)


def flat_sides(padded):
    return [padded[2:, 1:-1], padded[:-2, 1:-1], padded[1:-1, 2:], padded[1:-1, :-2]]


def plane_sweep(p_pad, k_pad, anchor, source, trans):
    coef = jnp.zeros_like(trans)
    flow = jnp.zeros_like(trans)
    for k_side, p_side in zip(flat_sides(k_pad), flat_sides(p_pad)):
        face = 0.5 * (trans + k_side)
        coef = coef + face
        flow = flow + face * p_side
    return (anchor + source + flow) / (1.0 + coef)


def well_source(wells, rates, row_start, rows, cols, width):
    row_ids = row_start + jnp.arange(rows, dtype=jnp.int32)
    col_ids = jnp.arange(cols, dtype=jnp.int32)
    flat = row_ids[:, None] * width + col_ids[None, :]
    hit = flat[:, :, None] == wells[None, None, :]
    return 4.0 * jnp.sum(jnp.where(hit, rates[None, None, :], jnp.float32(0.0)), axis=-1)


def cube_sides(padded):
    return [
        padded[2:, 1:-1, 1:-1],
        padded[:-2, 1:-1, 1:-1],
        padded[1:-1, 2:, 1:-1],
        padded[1:-1, :-2, 1:-1],
        padded[1:-1, 1:-1, 2:],
        padded[1:-1, 1:-1, :-2],
    ]


X0 = 8


def neighbours(rows_all, width):
    col = lax.broadcasted_iota(jnp.int32, (rows_all, width), 1)
    has_next = col < width - 1
    has_prev = col > 0

    def y_next(a):
        return jnp.where(has_next, pltpu.roll(a, width - 1, 1), 0.0)

    def y_prev(a):
        return jnp.where(has_prev, pltpu.roll(a, 1, 1), 0.0)

    def x_next(a):
        return pltpu.roll(a, rows_all - 1, 0)

    def x_prev(a):
        return pltpu.roll(a, 1, 0)

    return x_next, x_prev, y_next, y_prev


def moved_at(uc, cc, up, down, nb, z_glob, load, x_in, total_depth):
    x_next, x_prev, y_next, y_prev = nb
    pairs = [
        up,
        down,
        (x_next(cc), x_next(uc)),
        (x_prev(cc), x_prev(uc)),
        (y_next(cc), y_next(uc)),
        (y_prev(cc), y_prev(uc)),
    ]
    coef = jnp.zeros_like(uc)
    flux = jnp.zeros_like(uc)
    for cn, un in pairs:
        face = 0.5 * (cc + cn)
        coef = coef + face
        flux = flux + face * (un - uc)
    force = jnp.where(z_glob == total_depth // 2, load, 0.0)
    moved = uc + 0.8 * (force + flux) / coef
    keep = x_in & (z_glob >= 0) & (z_glob < total_depth)
    return jnp.where(keep, moved, 0.0)


def opening_at(mc, m_up, m_down, dc, d_up, d_down, nb, mod, tough, dmg, own):
    x_next, x_prev, y_next, y_prev = nb
    energy = (
        (m_up - mc) ** 2 + (m_down - mc) ** 2 + (x_next(mc) - mc) ** 2 + (x_prev(mc) - mc) ** 2
        + (y_next(mc) - mc) ** 2 + (y_prev(mc) - mc) ** 2
    )
    beside = d_up + d_down + x_next(dc) + x_prev(dc) + y_next(dc) + y_prev(dc)
    energy = 0.25 * mod * energy[own]
    trial = (2.0 * energy + tough * beside[own]) / (7.0 * tough + 2.0 * energy)
    new_damage = jnp.maximum(dmg, trial)
    mo = mc[own]
    return new_damage * mo * mo


def x_frame(ids_ref, rows_all, width, total_rows):
    row = lax.broadcasted_iota(jnp.int32, (rows_all, width), 0)
    x_glob = ids_ref[1] + row - X0
    return (x_glob >= 0) & (x_glob < total_rows)


def interior_kernel(total_depth, total_rows, ids_ref, u_ref, dmg_ref, mod_ref, tgh_ref, xlo_ref, xhi_ref, load_ref,
                    part_ref, edge_ref, u_s, c_s, d_s, m_s):
    depth_cells, tile_cells, width = u_ref.shape
    rows_all = u_s.shape[1]
    own = slice(X0, X0 + tile_cells)
    top = X0 + tile_cells
    zero = jnp.zeros((rows_all, width), jnp.float32)

    def place(k, carry):
        dk = dmg_ref[k]
        u_s[k] = zero
        c_s[k] = zero
        d_s[k] = zero
        u_s[k, own] = u_ref[k]
        c_s[k, own] = ((1.0 - dk) ** 2 + 0.001) * mod_ref[k]
        d_s[k, own] = dk
        return carry

    lax.fori_loop(0, depth_cells, place, 0)
    dz = 4 * depth_cells
    for z in range(depth_cells):
        u_s[z, X0 - 2:X0] = xlo_ref[2 * z:2 * z + 2]
        c_s[z, X0 - 2:X0] = xlo_ref[2 * depth_cells + 2 * z:2 * depth_cells + 2 * z + 2]
        d_s[z, X0 - 1:X0] = xlo_ref[dz + z:dz + z + 1]
        u_s[z, top:top + 2] = xhi_ref[2 * z:2 * z + 2]
        c_s[z, top:top + 2] = xhi_ref[2 * depth_cells + 2 * z:2 * depth_cells + 2 * z + 2]
        d_s[z, top:top + 1] = xhi_ref[dz + z:dz + z + 1]

    nb = neighbours(rows_all, width)
    x_in = x_frame(ids_ref, rows_all, width, total_rows)
    load = load_ref[...]
    depth_start = ids_ref[0]

    def moved_body(k, carry):
        m_s[k] = moved_at(
            u_s[k], c_s[k], (c_s[k + 1], u_s[k + 1]), (c_s[k - 1], u_s[k - 1]), nb, depth_start + k, load, x_in,
            total_depth,
        )
        return carry

    lax.fori_loop(1, depth_cells - 1, moved_body, 0)

    def open_body(k, acc):
        return acc + opening_at(
            m_s[k], m_s[k + 1], m_s[k - 1], d_s[k], d_s[k + 1], d_s[k - 1], nb, mod_ref[k], tgh_ref[k], dmg_ref[k], own
        )

    acc = lax.fori_loop(2, depth_cells - 2, open_body, jnp.zeros((tile_cells, width), jnp.float32))
    part_ref[...] = acc
    edge_ref[0] = m_s[1]
    edge_ref[1] = m_s[2]
    edge_ref[2] = m_s[depth_cells - 3]
    edge_ref[3] = m_s[depth_cells - 2]


def face_kernel(u_lo, u_hi, d_lo, d_hi, m_lo, m_hi, p_ref, k_ref, lo_out, hi_out):
    depth_cells = u_lo.shape[0]
    tile_cells = p_ref.shape[0]
    dz = 4 * depth_cells
    for z in range(depth_cells):
        for out, u_b, d_b, m_b, rows, edge in ((lo_out, u_lo, d_lo, m_lo, slice(0, 2), 0), (hi_out, u_hi, d_hi, m_hi, slice(6, 8), 7)):
            out[2 * z:2 * z + 2] = u_b[z, rows]
            dk = d_b[z, rows]
            out[2 * depth_cells + 2 * z:2 * depth_cells + 2 * z + 2] = ((1.0 - dk) ** 2 + 0.001) * m_b[z, rows]
            out[dz + z:dz + z + 1] = d_b[z, edge:edge + 1]
    lo_out[dz + depth_cells:dz + depth_cells + 2] = p_ref[0:2]
    lo_out[dz + depth_cells + 2:dz + depth_cells + 4] = k_ref[0:2].astype(jnp.float32)
    hi_out[dz + depth_cells:dz + depth_cells + 2] = p_ref[tile_cells - 2:tile_cells]
    hi_out[dz + depth_cells + 2:dz + depth_cells + 4] = k_ref[tile_cells - 2:tile_cells].astype(jnp.float32)


class Ends:
    def __init__(self, lo, hi, depth_cells):
        self.lo, self.hi, self.depth_cells = lo, hi, depth_cells

    def __getitem__(self, z):
        return self.lo[z] if z < 4 else self.hi[z - self.depth_cells + 4]


def boundary_kernel(total_depth, total_rows, depth_cells, ids_ref, u_lo, u_hi, d_lo, d_hi, mod_lo, mod_hi, tgh_lo,
                    tgh_hi, xlo_ref, xhi_ref, zlo_ref, zhi_ref, edge_ref, part_ref, load_ref, out_ref, u_s, c_s, d_s,
                    m_s):
    u_ref = Ends(u_lo, u_hi, depth_cells)
    dmg_ref = Ends(d_lo, d_hi, depth_cells)
    mod_ref = Ends(mod_lo, mod_hi, depth_cells)
    tgh_ref = Ends(tgh_lo, tgh_hi, depth_cells)
    _, tile_cells, width = u_lo.shape
    rows_all = u_s.shape[1]
    own = slice(X0, X0 + tile_cells)
    wide = slice(X0 - 1, X0 + tile_cells + 1)
    top = X0 + tile_cells
    zero = jnp.zeros((rows_all, width), jnp.float32)
    for j in range(8):
        u_s[j] = zero
        c_s[j] = zero
        d_s[j] = zero
    ext = tile_cells + 2
    for side, ref, adj, sec in ((0, zlo_ref, 1, 0), (4, zhi_ref, 6, 7)):
        u_s[adj, wide] = ref[0:ext]
        c_s[adj, wide] = ref[ext:2 * ext]
        u_s[sec, own] = ref[2 * ext:2 * ext + tile_cells]
        c_s[sec, own] = ref[2 * ext + tile_cells:2 * ext + 2 * tile_cells]
    d_s[0, own] = zlo_ref[2 * ext + 2 * tile_cells:2 * ext + 3 * tile_cells]
    d_s[7, own] = zhi_ref[2 * ext + 2 * tile_cells:2 * ext + 3 * tile_cells]
    dz = 4 * depth_cells
    for slot, z in ((2, 0), (3, 1), (4, depth_cells - 2), (5, depth_cells - 1)):
        dk = dmg_ref[z]
        u_s[slot, own] = u_ref[z]
        c_s[slot, own] = ((1.0 - dk) ** 2 + 0.001) * mod_ref[z]
        u_s[slot, X0 - 2:X0] = xlo_ref[2 * z:2 * z + 2]
        c_s[slot, X0 - 2:X0] = xlo_ref[2 * depth_cells + 2 * z:2 * depth_cells + 2 * z + 2]
        u_s[slot, top:top + 2] = xhi_ref[2 * z:2 * z + 2]
        c_s[slot, top:top + 2] = xhi_ref[2 * depth_cells + 2 * z:2 * depth_cells + 2 * z + 2]
    for slot, z in ((1, 0), (2, 1), (5, depth_cells - 2), (6, depth_cells - 1)):
        d_s[slot, own] = dmg_ref[z]
        d_s[slot, X0 - 1:X0] = xlo_ref[dz + z:dz + z + 1]
        d_s[slot, top:top + 1] = xhi_ref[dz + z:dz + z + 1]
    d_s[3, own] = dmg_ref[2]
    d_s[4, own] = dmg_ref[depth_cells - 3]
    m_s[2] = edge_ref[0]
    m_s[3] = edge_ref[1]
    m_s[4] = edge_ref[2]
    m_s[5] = edge_ref[3]

    nb = neighbours(rows_all, width)
    x_in = x_frame(ids_ref, rows_all, width, total_rows)
    load = load_ref[...]
    depth_start = ids_ref[0]
    for us, ms, z in ((1, 0, -1), (2, 1, 0), (5, 6, depth_cells - 1), (6, 7, depth_cells)):
        m_s[ms] = moved_at(
            u_s[us], c_s[us], (c_s[us + 1], u_s[us + 1]), (c_s[us - 1], u_s[us - 1]), nb, depth_start + z, load, x_in,
            total_depth,
        )
    acc = part_ref[...]
    for ms, z in ((1, 0), (2, 1), (5, depth_cells - 2), (6, depth_cells - 1)):
        acc = acc + opening_at(
            m_s[ms], m_s[ms + 1], m_s[ms - 1], d_s[ms], d_s[ms + 1], d_s[ms - 1], nb, mod_ref[z], tgh_ref[z],
            dmg_ref[z], own,
        )
    out_ref[...] = (4.0 / total_depth) * acc


def on_device(displacement, damage, modulus, toughness, pressure, crack_mask, wells, rates):
    depth_cells, tile_cells, width = displacement.shape
    total_depth = depth_cells * lax.axis_size("depth")
    total_rows = tile_cells * lax.axis_size("tile")
    depth_start = lax.axis_index("depth") * depth_cells
    tile_start = lax.axis_index("tile") * tile_cells
    mask_f = crack_mask.astype(jnp.float32)
    rows_all = tile_cells + 2 * X0

    def stiff_of(dmg, mod):
        return ((1.0 - dmg) ** 2 + 0.001) * mod

    vmem = pl.BlockSpec(memory_space=pltpu.VMEM)
    smem = pl.BlockSpec(memory_space=pltpu.SMEM)
    f32 = jnp.float32
    rows_lo = pl.BlockSpec((depth_cells, 8, width), lambda i: (0, 0, 0))
    rows_hi = pl.BlockSpec((depth_cells, 8, width), lambda i: (0, tile_cells // 8 - 1, 0))
    face_rows = 5 * depth_cells + 4
    face_lo, face_hi = pl.pallas_call(
        face_kernel,
        out_shape=(jax.ShapeDtypeStruct((face_rows, width), f32),) * 2,
        grid=(1,),
        in_specs=[rows_lo, rows_hi] * 3 + [vmem, vmem],
        out_specs=(vmem, vmem),
    )(displacement, displacement, damage, damage, modulus, modulus, pressure, crack_mask)
    lo_x, hi_x = halo_swap(face_lo, face_hi, "tile")
    dz = 4 * depth_cells
    p_ext = jnp.concatenate([lo_x[dz + depth_cells:dz + depth_cells + 2], pressure, hi_x[dz + depth_cells:dz + depth_cells + 2]])
    m_ext = jnp.concatenate([lo_x[dz + depth_cells + 2:], mask_f, hi_x[dz + depth_cells + 2:]])
    load_all = jnp.pad(4.0 * m_ext[1:-1] * p_ext[1:-1], ((X0 - 1, X0 - 1), (0, 0)))
    ids = jnp.stack([depth_start, tile_start]).astype(jnp.int32)

    def depth_face(adj, sec):
        u_adj = jnp.concatenate([lo_x[2 * adj + 1:2 * adj + 2], displacement[adj], hi_x[2 * adj:2 * adj + 1]])
        c0 = 2 * depth_cells
        c_adj = jnp.concatenate(
            [lo_x[c0 + 2 * adj + 1:c0 + 2 * adj + 2], stiff_of(damage[adj], modulus[adj]), hi_x[c0 + 2 * adj:c0 + 2 * adj + 1]]
        )
        return jnp.concatenate([u_adj, c_adj, displacement[sec], stiff_of(damage[sec], modulus[sec]), damage[adj]])

    lo_z, hi_z = halo_swap(depth_face(0, 1), depth_face(depth_cells - 1, depth_cells - 2), "depth")

    vmem = pl.BlockSpec(memory_space=pltpu.VMEM)
    smem = pl.BlockSpec(memory_space=pltpu.SMEM)
    f32 = jnp.float32
    part_in, edge = pl.pallas_call(
        functools.partial(interior_kernel, total_depth, total_rows),
        out_shape=(
            jax.ShapeDtypeStruct((tile_cells, width), f32),
            jax.ShapeDtypeStruct((4, rows_all, width), f32),
        ),
        in_specs=[smem] + [vmem] * 7,
        out_specs=(vmem, vmem),
        scratch_shapes=[pltpu.VMEM((depth_cells, rows_all, width), f32)] * 4,
    )(ids, displacement, damage, modulus, toughness, lo_x, hi_x, load_all)
    end_lo = pl.BlockSpec((4, tile_cells, width), lambda i: (0, 0, 0))
    end_hi = pl.BlockSpec((4, tile_cells, width), lambda i: (depth_cells // 4 - 1, 0, 0))
    partial_open = pl.pallas_call(
        functools.partial(boundary_kernel, total_depth, total_rows, depth_cells),
        out_shape=jax.ShapeDtypeStruct((tile_cells, width), f32),
        grid=(1,),
        in_specs=[smem] + [end_lo, end_hi] * 4 + [vmem] * 7,
        out_specs=vmem,
        scratch_shapes=[pltpu.VMEM((8, rows_all, width), f32)] * 4,
    )(ids, displacement, displacement, damage, damage, modulus, modulus, toughness, toughness, lo_x, hi_x, lo_z, hi_z,
      edge, part_in, load_all)

    aperture = 0.5 + butterfly_sum(partial_open, "depth")
    trans = mask_f * aperture**3

    t_lo, t_hi = halo_swap(trans[:2], trans[-2:], "tile")
    t_ext = jnp.concatenate([t_lo, trans, t_hi])
    x_ids = tile_start - 1 + jnp.arange(tile_cells + 2, dtype=jnp.int32)
    rows_in = ((x_ids >= 0) & (x_ids < total_rows))[:, None]
    src_ext = well_source(wells, rates, tile_start - 1, tile_cells + 2, width, width)
    k_pad = pad_last(t_ext)
    level = plane_sweep(pad_last(p_ext), k_pad, p_ext[1:-1], src_ext, t_ext[1:-1])
    level = jnp.where(rows_in, level, jnp.float32(0.0))
    return plane_sweep(pad_last(level), k_pad[1:-1], pressure, src_ext[1:-1], trans)


def solution(mesh):
    return jax.shard_map(
        on_device,
        mesh=mesh,
        in_specs=(
            P("depth", "tile", None),
            P("depth", "tile", None),
            P("depth", "tile", None),
            P("depth", "tile", None),
            P("tile", None),
            P("tile", None),
            P(),
            P(),
        ),
        out_specs=P("tile", None),
        check_vma=False,
    )
```

```python
import functools

import jax
import jax.numpy as jnp
from jax import lax
from jax.experimental import pallas as pl
from jax.experimental.pallas import tpu as pltpu
from jax.sharding import PartitionSpec as P


def halo_swap(lo_face, hi_face, axis):
    count = lax.axis_size(axis)
    even = lax.axis_index(axis) % 2 == 0
    pairs_a = [(i, i ^ 1) for i in range(count)]
    pairs_b = [(i, i + 1) for i in range(1, count - 1, 2)] + [(i + 1, i) for i in range(1, count - 1, 2)]
    got_a = lax.ppermute(jnp.where(even, hi_face, lo_face), axis, pairs_a)
    got_b = lax.ppermute(jnp.where(even, lo_face, hi_face), axis, pairs_b)
    return jnp.where(even, got_b, got_a), jnp.where(even, got_a, got_b)


def butterfly_sum(part, axis):
    count = lax.axis_size(axis)
    order = [1 << k for k in range(1, count.bit_length() - 1)] + [1]
    for step in order:
        pairs = [(i, i ^ step) for i in range(lax.axis_size(axis))]
        part = part + lax.ppermute(part, axis, pairs)
    return part


def pad_last(stacked):
    widths = [(0, 0)] * (stacked.ndim - 1) + [(1, 1)]
    return jnp.pad(stacked, widths)


def flat_sides(padded):
    return [padded[2:, 1:-1], padded[:-2, 1:-1], padded[1:-1, 2:], padded[1:-1, :-2]]


def plane_sweep(p_pad, k_pad, anchor, source, trans):
    coef = jnp.zeros_like(trans)
    flow = jnp.zeros_like(trans)
    for k_side, p_side in zip(flat_sides(k_pad), flat_sides(p_pad)):
        face = 0.5 * (trans + k_side)
        coef = coef + face
        flow = flow + face * p_side
    return (anchor + source + flow) / (1.0 + coef)


def well_source(wells, rates, row_start, rows, cols, width):
    row_ids = row_start + jnp.arange(rows, dtype=jnp.int32)
    col_ids = jnp.arange(cols, dtype=jnp.int32)
    flat = row_ids[:, None] * width + col_ids[None, :]
    hit = flat[:, :, None] == wells[None, None, :]
    return 4.0 * jnp.sum(jnp.where(hit, rates[None, None, :], jnp.float32(0.0)), axis=-1)


def cube_sides(padded):
    return [
        padded[2:, 1:-1, 1:-1],
        padded[:-2, 1:-1, 1:-1],
        padded[1:-1, 2:, 1:-1],
        padded[1:-1, :-2, 1:-1],
        padded[1:-1, 1:-1, 2:],
        padded[1:-1, 1:-1, :-2],
    ]


X0 = 8


def neighbours(rows_all, width):
    col = lax.broadcasted_iota(jnp.int32, (rows_all, width), 1)
    has_next = col < width - 1
    has_prev = col > 0

    def y_next(a):
        return jnp.where(has_next, pltpu.roll(a, width - 1, 1), 0.0)

    def y_prev(a):
        return jnp.where(has_prev, pltpu.roll(a, 1, 1), 0.0)

    def x_next(a):
        return pltpu.roll(a, rows_all - 1, 0)

    def x_prev(a):
        return pltpu.roll(a, 1, 0)

    return x_next, x_prev, y_next, y_prev


def moved_at(uc, cc, up, down, nb, z_glob, load, x_in, total_depth):
    x_next, x_prev, y_next, y_prev = nb
    pairs = [
        up,
        down,
        (x_next(cc), x_next(uc)),
        (x_prev(cc), x_prev(uc)),
        (y_next(cc), y_next(uc)),
        (y_prev(cc), y_prev(uc)),
    ]
    coef = jnp.zeros_like(uc)
    flux = jnp.zeros_like(uc)
    for cn, un in pairs:
        face = 0.5 * (cc + cn)
        coef = coef + face
        flux = flux + face * (un - uc)
    force = jnp.where(z_glob == total_depth // 2, load, 0.0)
    moved = uc + 0.8 * (force + flux) / coef
    keep = x_in & (z_glob >= 0) & (z_glob < total_depth)
    return jnp.where(keep, moved, 0.0)


def opening_at(mc, m_up, m_down, dc, d_up, d_down, nb, mod, tough, dmg, own):
    x_next, x_prev, y_next, y_prev = nb
    energy = (
        (m_up - mc) ** 2 + (m_down - mc) ** 2 + (x_next(mc) - mc) ** 2 + (x_prev(mc) - mc) ** 2
        + (y_next(mc) - mc) ** 2 + (y_prev(mc) - mc) ** 2
    )
    beside = d_up + d_down + x_next(dc) + x_prev(dc) + y_next(dc) + y_prev(dc)
    energy = 0.25 * mod * energy[own]
    trial = (2.0 * energy + tough * beside[own]) / (7.0 * tough + 2.0 * energy)
    new_damage = jnp.maximum(dmg, trial)
    mo = mc[own]
    return new_damage * mo * mo


def x_frame(ids_ref, rows_all, width, total_rows):
    row = lax.broadcasted_iota(jnp.int32, (rows_all, width), 0)
    x_glob = ids_ref[1] + row - X0
    return (x_glob >= 0) & (x_glob < total_rows)


def interior_kernel(total_depth, total_rows, ids_ref, u_ref, dmg_ref, mod_ref, tgh_ref, xlo_ref, xhi_ref, load_ref,
                    part_ref, edge_ref, u_s, c_s, d_s, m_s):
    depth_cells, tile_cells, width = u_ref.shape
    rows_all = u_s.shape[1]
    own = slice(X0, X0 + tile_cells)
    top = X0 + tile_cells
    zero = jnp.zeros((rows_all, width), jnp.float32)

    def place(k, carry):
        dk = dmg_ref[k]
        u_s[k] = zero
        c_s[k] = zero
        d_s[k] = zero
        u_s[k, own] = u_ref[k]
        c_s[k, own] = ((1.0 - dk) ** 2 + 0.001) * mod_ref[k]
        d_s[k, own] = dk
        return carry

    lax.fori_loop(0, depth_cells, place, 0)
    dz = 4 * depth_cells
    for z in range(depth_cells):
        u_s[z, X0 - 2:X0] = xlo_ref[2 * z:2 * z + 2]
        c_s[z, X0 - 2:X0] = xlo_ref[2 * depth_cells + 2 * z:2 * depth_cells + 2 * z + 2]
        d_s[z, X0 - 1:X0] = xlo_ref[dz + z:dz + z + 1]
        u_s[z, top:top + 2] = xhi_ref[2 * z:2 * z + 2]
        c_s[z, top:top + 2] = xhi_ref[2 * depth_cells + 2 * z:2 * depth_cells + 2 * z + 2]
        d_s[z, top:top + 1] = xhi_ref[dz + z:dz + z + 1]

    nb = neighbours(rows_all, width)
    x_in = x_frame(ids_ref, rows_all, width, total_rows)
    load = load_ref[...]
    depth_start = ids_ref[0]

    def moved_body(k, carry):
        m_s[k] = moved_at(
            u_s[k], c_s[k], (c_s[k + 1], u_s[k + 1]), (c_s[k - 1], u_s[k - 1]), nb, depth_start + k, load, x_in,
            total_depth,
        )
        return carry

    lax.fori_loop(1, depth_cells - 1, moved_body, 0)

    def open_body(k, acc):
        return acc + opening_at(
            m_s[k], m_s[k + 1], m_s[k - 1], d_s[k], d_s[k + 1], d_s[k - 1], nb, mod_ref[k], tgh_ref[k], dmg_ref[k], own
        )

    acc = lax.fori_loop(2, depth_cells - 2, open_body, jnp.zeros((tile_cells, width), jnp.float32))
    part_ref[...] = acc
    edge_ref[0] = m_s[1]
    edge_ref[1] = m_s[2]
    edge_ref[2] = m_s[depth_cells - 3]
    edge_ref[3] = m_s[depth_cells - 2]


def face_kernel(par_ref, u_lo, u_hi, d_lo, d_hi, m_lo, m_hi, p_ref, k_ref, send_a, send_b):
    @pl.when(par_ref[0] == 0)
    def _():
        pack_faces(u_lo, u_hi, d_lo, d_hi, m_lo, m_hi, p_ref, k_ref, send_b, send_a)

    @pl.when(par_ref[0] == 1)
    def _():
        pack_faces(u_lo, u_hi, d_lo, d_hi, m_lo, m_hi, p_ref, k_ref, send_a, send_b)


def pack_faces(u_lo, u_hi, d_lo, d_hi, m_lo, m_hi, p_ref, k_ref, lo_out, hi_out):
    depth_cells = u_lo.shape[0]
    tile_cells = p_ref.shape[0]
    dz = 4 * depth_cells
    for z in range(depth_cells):
        for out, u_b, d_b, m_b, rows, edge in ((lo_out, u_lo, d_lo, m_lo, slice(0, 2), 0), (hi_out, u_hi, d_hi, m_hi, slice(6, 8), 7)):
            out[2 * z:2 * z + 2] = u_b[z, rows]
            dk = d_b[z, rows]
            out[2 * depth_cells + 2 * z:2 * depth_cells + 2 * z + 2] = ((1.0 - dk) ** 2 + 0.001) * m_b[z, rows]
            out[dz + z:dz + z + 1] = d_b[z, edge:edge + 1]
    lo_out[dz + depth_cells:dz + depth_cells + 2] = p_ref[0:2]
    lo_out[dz + depth_cells + 2:dz + depth_cells + 4] = k_ref[0:2].astype(jnp.float32)
    hi_out[dz + depth_cells:dz + depth_cells + 2] = p_ref[tile_cells - 2:tile_cells]
    hi_out[dz + depth_cells + 2:dz + depth_cells + 4] = k_ref[tile_cells - 2:tile_cells].astype(jnp.float32)


class Ends:
    def __init__(self, lo, hi, depth_cells):
        self.lo, self.hi, self.depth_cells = lo, hi, depth_cells

    def __getitem__(self, z):
        return self.lo[z] if z < 4 else self.hi[z - self.depth_cells + 4]


def boundary_kernel(total_depth, total_rows, depth_cells, ids_ref, u_lo, u_hi, d_lo, d_hi, mod_lo, mod_hi, tgh_lo,
                    tgh_hi, xlo_ref, xhi_ref, zlo_ref, zhi_ref, edge_ref, part_ref, load_ref, out_ref, u_s, c_s, d_s,
                    m_s):
    u_ref = Ends(u_lo, u_hi, depth_cells)
    dmg_ref = Ends(d_lo, d_hi, depth_cells)
    mod_ref = Ends(mod_lo, mod_hi, depth_cells)
    tgh_ref = Ends(tgh_lo, tgh_hi, depth_cells)
    _, tile_cells, width = u_lo.shape
    rows_all = u_s.shape[1]
    own = slice(X0, X0 + tile_cells)
    wide = slice(X0 - 1, X0 + tile_cells + 1)
    top = X0 + tile_cells
    zero = jnp.zeros((rows_all, width), jnp.float32)
    for j in range(8):
        u_s[j] = zero
        c_s[j] = zero
        d_s[j] = zero
    ext = tile_cells + 2
    for side, ref, adj, sec in ((0, zlo_ref, 1, 0), (4, zhi_ref, 6, 7)):
        u_s[adj, wide] = ref[0:ext]
        c_s[adj, wide] = ref[ext:2 * ext]
        u_s[sec, own] = ref[2 * ext:2 * ext + tile_cells]
        c_s[sec, own] = ref[2 * ext + tile_cells:2 * ext + 2 * tile_cells]
    d_s[0, own] = zlo_ref[2 * ext + 2 * tile_cells:2 * ext + 3 * tile_cells]
    d_s[7, own] = zhi_ref[2 * ext + 2 * tile_cells:2 * ext + 3 * tile_cells]
    dz = 4 * depth_cells
    for slot, z in ((2, 0), (3, 1), (4, depth_cells - 2), (5, depth_cells - 1)):
        dk = dmg_ref[z]
        u_s[slot, own] = u_ref[z]
        c_s[slot, own] = ((1.0 - dk) ** 2 + 0.001) * mod_ref[z]
        u_s[slot, X0 - 2:X0] = xlo_ref[2 * z:2 * z + 2]
        c_s[slot, X0 - 2:X0] = xlo_ref[2 * depth_cells + 2 * z:2 * depth_cells + 2 * z + 2]
        u_s[slot, top:top + 2] = xhi_ref[2 * z:2 * z + 2]
        c_s[slot, top:top + 2] = xhi_ref[2 * depth_cells + 2 * z:2 * depth_cells + 2 * z + 2]
    for slot, z in ((1, 0), (2, 1), (5, depth_cells - 2), (6, depth_cells - 1)):
        d_s[slot, own] = dmg_ref[z]
        d_s[slot, X0 - 1:X0] = xlo_ref[dz + z:dz + z + 1]
        d_s[slot, top:top + 1] = xhi_ref[dz + z:dz + z + 1]
    d_s[3, own] = dmg_ref[2]
    d_s[4, own] = dmg_ref[depth_cells - 3]
    m_s[2] = edge_ref[0]
    m_s[3] = edge_ref[1]
    m_s[4] = edge_ref[2]
    m_s[5] = edge_ref[3]

    nb = neighbours(rows_all, width)
    x_in = x_frame(ids_ref, rows_all, width, total_rows)
    load = load_ref[...]
    depth_start = ids_ref[0]
    for us, ms, z in ((1, 0, -1), (2, 1, 0), (5, 6, depth_cells - 1), (6, 7, depth_cells)):
        m_s[ms] = moved_at(
            u_s[us], c_s[us], (c_s[us + 1], u_s[us + 1]), (c_s[us - 1], u_s[us - 1]), nb, depth_start + z, load, x_in,
            total_depth,
        )
    acc = part_ref[...]
    for ms, z in ((1, 0), (2, 1), (5, depth_cells - 2), (6, depth_cells - 1)):
        acc = acc + opening_at(
            m_s[ms], m_s[ms + 1], m_s[ms - 1], d_s[ms], d_s[ms + 1], d_s[ms - 1], nb, mod_ref[z], tgh_ref[z],
            dmg_ref[z], own,
        )
    out_ref[...] = (4.0 / total_depth) * acc


def on_device(displacement, damage, modulus, toughness, pressure, crack_mask, wells, rates):
    depth_cells, tile_cells, width = displacement.shape
    total_depth = depth_cells * lax.axis_size("depth")
    total_rows = tile_cells * lax.axis_size("tile")
    depth_start = lax.axis_index("depth") * depth_cells
    tile_start = lax.axis_index("tile") * tile_cells
    mask_f = crack_mask.astype(jnp.float32)
    rows_all = tile_cells + 2 * X0

    def stiff_of(dmg, mod):
        return ((1.0 - dmg) ** 2 + 0.001) * mod

    vmem = pl.BlockSpec(memory_space=pltpu.VMEM)
    smem = pl.BlockSpec(memory_space=pltpu.SMEM)
    f32 = jnp.float32
    rows_lo = pl.BlockSpec((depth_cells, 8, width), lambda i: (0, 0, 0))
    rows_hi = pl.BlockSpec((depth_cells, 8, width), lambda i: (0, tile_cells // 8 - 1, 0))
    face_rows = 5 * depth_cells + 4
    parity = (lax.axis_index("tile") % 2).astype(jnp.int32).reshape(1)
    send_a, send_b = pl.pallas_call(
        face_kernel,
        out_shape=(jax.ShapeDtypeStruct((face_rows, width), f32),) * 2,
        grid=(1,),
        in_specs=[smem] + [rows_lo, rows_hi] * 3 + [vmem, vmem],
        out_specs=(vmem, vmem),
    )(parity, displacement, displacement, damage, damage, modulus, modulus, pressure, crack_mask)
    tiles = lax.axis_size("tile")
    even_x = lax.axis_index("tile") % 2 == 0
    got_a = lax.ppermute(send_a, "tile", [(i, i ^ 1) for i in range(tiles)])
    got_b = lax.ppermute(
        send_b, "tile", [(i, i + 1) for i in range(1, tiles - 1, 2)] + [(i + 1, i) for i in range(1, tiles - 1, 2)]
    )
    lo_x, hi_x = jnp.where(even_x, got_b, got_a), jnp.where(even_x, got_a, got_b)
    dz = 4 * depth_cells
    p_ext = jnp.concatenate([lo_x[dz + depth_cells:dz + depth_cells + 2], pressure, hi_x[dz + depth_cells:dz + depth_cells + 2]])
    m_ext = jnp.concatenate([lo_x[dz + depth_cells + 2:], mask_f, hi_x[dz + depth_cells + 2:]])
    load_all = jnp.pad(4.0 * m_ext[1:-1] * p_ext[1:-1], ((X0 - 1, X0 - 1), (0, 0)))
    ids = jnp.stack([depth_start, tile_start]).astype(jnp.int32)

    def depth_face(adj, sec):
        u_adj = jnp.concatenate([lo_x[2 * adj + 1:2 * adj + 2], displacement[adj], hi_x[2 * adj:2 * adj + 1]])
        c0 = 2 * depth_cells
        c_adj = jnp.concatenate(
            [lo_x[c0 + 2 * adj + 1:c0 + 2 * adj + 2], stiff_of(damage[adj], modulus[adj]), hi_x[c0 + 2 * adj:c0 + 2 * adj + 1]]
        )
        return jnp.concatenate([u_adj, c_adj, displacement[sec], stiff_of(damage[sec], modulus[sec]), damage[adj]])

    lo_z, hi_z = halo_swap(depth_face(0, 1), depth_face(depth_cells - 1, depth_cells - 2), "depth")

    vmem = pl.BlockSpec(memory_space=pltpu.VMEM)
    smem = pl.BlockSpec(memory_space=pltpu.SMEM)
    f32 = jnp.float32
    part_in, edge = pl.pallas_call(
        functools.partial(interior_kernel, total_depth, total_rows),
        out_shape=(
            jax.ShapeDtypeStruct((tile_cells, width), f32),
            jax.ShapeDtypeStruct((4, rows_all, width), f32),
        ),
        in_specs=[smem] + [vmem] * 7,
        out_specs=(vmem, vmem),
        scratch_shapes=[pltpu.VMEM((depth_cells, rows_all, width), f32)] * 4,
    )(ids, displacement, damage, modulus, toughness, lo_x, hi_x, load_all)
    end_lo = pl.BlockSpec((4, tile_cells, width), lambda i: (0, 0, 0))
    end_hi = pl.BlockSpec((4, tile_cells, width), lambda i: (depth_cells // 4 - 1, 0, 0))
    partial_open = pl.pallas_call(
        functools.partial(boundary_kernel, total_depth, total_rows, depth_cells),
        out_shape=jax.ShapeDtypeStruct((tile_cells, width), f32),
        grid=(1,),
        in_specs=[smem] + [end_lo, end_hi] * 4 + [vmem] * 7,
        out_specs=vmem,
        scratch_shapes=[pltpu.VMEM((8, rows_all, width), f32)] * 4,
    )(ids, displacement, displacement, damage, damage, modulus, modulus, toughness, toughness, lo_x, hi_x, lo_z, hi_z,
      edge, part_in, load_all)

    aperture = 0.5 + butterfly_sum(partial_open, "depth")
    trans = mask_f * aperture**3

    t_lo, t_hi = halo_swap(trans[:2], trans[-2:], "tile")
    t_ext = jnp.concatenate([t_lo, trans, t_hi])
    x_ids = tile_start - 1 + jnp.arange(tile_cells + 2, dtype=jnp.int32)
    rows_in = ((x_ids >= 0) & (x_ids < total_rows))[:, None]
    src_ext = well_source(wells, rates, tile_start - 1, tile_cells + 2, width, width)
    k_pad = pad_last(t_ext)
    level = plane_sweep(pad_last(p_ext), k_pad, p_ext[1:-1], src_ext, t_ext[1:-1])
    level = jnp.where(rows_in, level, jnp.float32(0.0))
    return plane_sweep(pad_last(level), k_pad[1:-1], pressure, src_ext[1:-1], trans)


def solution(mesh):
    return jax.shard_map(
        on_device,
        mesh=mesh,
        in_specs=(
            P("depth", "tile", None),
            P("depth", "tile", None),
            P("depth", "tile", None),
            P("depth", "tile", None),
            P("tile", None),
            P("tile", None),
            P(),
            P(),
        ),
        out_specs=P("tile", None),
        check_vma=False,
    )
```

```python
import functools

import jax
import jax.numpy as jnp
from jax import lax
from jax.experimental import pallas as pl
from jax.experimental.pallas import tpu as pltpu
from jax.sharding import PartitionSpec as P


def halo_swap(lo_face, hi_face, axis):
    count = lax.axis_size(axis)
    even = lax.axis_index(axis) % 2 == 0
    pairs_a = [(i, i ^ 1) for i in range(count)]
    pairs_b = [(i, i + 1) for i in range(1, count - 1, 2)] + [(i + 1, i) for i in range(1, count - 1, 2)]
    got_a = lax.ppermute(jnp.where(even, hi_face, lo_face), axis, pairs_a)
    got_b = lax.ppermute(jnp.where(even, lo_face, hi_face), axis, pairs_b)
    return jnp.where(even, got_b, got_a), jnp.where(even, got_a, got_b)


def butterfly_sum(part, axis):
    count = lax.axis_size(axis)
    order = [1 << k for k in range(1, count.bit_length() - 1)] + [1]
    for step in order:
        pairs = [(i, i ^ step) for i in range(lax.axis_size(axis))]
        part = part + lax.ppermute(part, axis, pairs)
    return part


def pad_last(stacked):
    widths = [(0, 0)] * (stacked.ndim - 1) + [(1, 1)]
    return jnp.pad(stacked, widths)


def flat_sides(padded):
    return [padded[2:, 1:-1], padded[:-2, 1:-1], padded[1:-1, 2:], padded[1:-1, :-2]]


def plane_sweep(p_pad, k_pad, anchor, source, trans):
    coef = jnp.zeros_like(trans)
    flow = jnp.zeros_like(trans)
    for k_side, p_side in zip(flat_sides(k_pad), flat_sides(p_pad)):
        face = 0.5 * (trans + k_side)
        coef = coef + face
        flow = flow + face * p_side
    return (anchor + source + flow) / (1.0 + coef)


def well_source(wells, rates, row_start, rows, cols, width):
    row_ids = row_start + jnp.arange(rows, dtype=jnp.int32)
    col_ids = jnp.arange(cols, dtype=jnp.int32)
    flat = row_ids[:, None] * width + col_ids[None, :]
    hit = flat[:, :, None] == wells[None, None, :]
    return 4.0 * jnp.sum(jnp.where(hit, rates[None, None, :], jnp.float32(0.0)), axis=-1)


def cube_sides(padded):
    return [
        padded[2:, 1:-1, 1:-1],
        padded[:-2, 1:-1, 1:-1],
        padded[1:-1, 2:, 1:-1],
        padded[1:-1, :-2, 1:-1],
        padded[1:-1, 1:-1, 2:],
        padded[1:-1, 1:-1, :-2],
    ]


X0 = 8


def neighbours(rows_all, width):
    col = lax.broadcasted_iota(jnp.int32, (rows_all, width), 1)
    has_next = col < width - 1
    has_prev = col > 0

    def y_next(a):
        return jnp.where(has_next, pltpu.roll(a, width - 1, 1), 0.0)

    def y_prev(a):
        return jnp.where(has_prev, pltpu.roll(a, 1, 1), 0.0)

    def x_next(a):
        return pltpu.roll(a, rows_all - 1, 0)

    def x_prev(a):
        return pltpu.roll(a, 1, 0)

    return x_next, x_prev, y_next, y_prev


def moved_at(uc, cc, up, down, nb, z_glob, load, x_in, total_depth):
    x_next, x_prev, y_next, y_prev = nb
    pairs = [
        up,
        down,
        (x_next(cc), x_next(uc)),
        (x_prev(cc), x_prev(uc)),
        (y_next(cc), y_next(uc)),
        (y_prev(cc), y_prev(uc)),
    ]
    coef = jnp.zeros_like(uc)
    flux = jnp.zeros_like(uc)
    for cn, un in pairs:
        face = 0.5 * (cc + cn)
        coef = coef + face
        flux = flux + face * (un - uc)
    force = jnp.where(z_glob == total_depth // 2, load, 0.0)
    moved = uc + 0.8 * (force + flux) / coef
    keep = x_in & (z_glob >= 0) & (z_glob < total_depth)
    return jnp.where(keep, moved, 0.0)


def opening_at(mc, m_up, m_down, dc, d_up, d_down, nb, mod, tough, dmg, own):
    x_next, x_prev, y_next, y_prev = nb
    energy = (
        (m_up - mc) ** 2 + (m_down - mc) ** 2 + (x_next(mc) - mc) ** 2 + (x_prev(mc) - mc) ** 2
        + (y_next(mc) - mc) ** 2 + (y_prev(mc) - mc) ** 2
    )
    beside = d_up + d_down + x_next(dc) + x_prev(dc) + y_next(dc) + y_prev(dc)
    energy = 0.25 * mod * energy[own]
    trial = (2.0 * energy + tough * beside[own]) / (7.0 * tough + 2.0 * energy)
    new_damage = jnp.maximum(dmg, trial)
    mo = mc[own]
    return new_damage * mo * mo


def x_frame(ids_ref, rows_all, width, total_rows):
    row = lax.broadcasted_iota(jnp.int32, (rows_all, width), 0)
    x_glob = ids_ref[1] + row - X0
    return (x_glob >= 0) & (x_glob < total_rows)


def interior_kernel(total_depth, total_rows, ids_ref, u_ref, dmg_ref, mod_ref, tgh_ref, xlo_ref, xhi_ref, load_ref,
                    part_ref, edge_ref, u_s, c_s, d_s, m_s):
    depth_cells, tile_cells, width = u_ref.shape
    rows_all = u_s.shape[1]
    own = slice(X0, X0 + tile_cells)
    top = X0 + tile_cells
    zero = jnp.zeros((rows_all, width), jnp.float32)

    def place(k, carry):
        dk = dmg_ref[k]
        u_s[k] = zero
        c_s[k] = zero
        d_s[k] = zero
        u_s[k, own] = u_ref[k]
        c_s[k, own] = ((1.0 - dk) ** 2 + 0.001) * mod_ref[k]
        d_s[k, own] = dk
        return carry

    lax.fori_loop(0, depth_cells, place, 0)
    dz = 4 * depth_cells
    for z in range(depth_cells):
        u_s[z, X0 - 2:X0] = xlo_ref[2 * z:2 * z + 2]
        c_s[z, X0 - 2:X0] = xlo_ref[2 * depth_cells + 2 * z:2 * depth_cells + 2 * z + 2]
        d_s[z, X0 - 1:X0] = xlo_ref[dz + z:dz + z + 1]
        u_s[z, top:top + 2] = xhi_ref[2 * z:2 * z + 2]
        c_s[z, top:top + 2] = xhi_ref[2 * depth_cells + 2 * z:2 * depth_cells + 2 * z + 2]
        d_s[z, top:top + 1] = xhi_ref[dz + z:dz + z + 1]

    nb = neighbours(rows_all, width)
    x_in = x_frame(ids_ref, rows_all, width, total_rows)
    load = load_ref[...]
    depth_start = ids_ref[0]

    def moved_body(k, carry):
        m_s[k] = moved_at(
            u_s[k], c_s[k], (c_s[k + 1], u_s[k + 1]), (c_s[k - 1], u_s[k - 1]), nb, depth_start + k, load, x_in,
            total_depth,
        )
        return carry

    lax.fori_loop(1, depth_cells - 1, moved_body, 0)

    def open_body(k, acc):
        return acc + opening_at(
            m_s[k], m_s[k + 1], m_s[k - 1], d_s[k], d_s[k + 1], d_s[k - 1], nb, mod_ref[k], tgh_ref[k], dmg_ref[k], own
        )

    acc = lax.fori_loop(2, depth_cells - 2, open_body, jnp.zeros((tile_cells, width), jnp.float32))
    part_ref[...] = acc
    edge_ref[0] = m_s[1]
    edge_ref[1] = m_s[2]
    edge_ref[2] = m_s[depth_cells - 3]
    edge_ref[3] = m_s[depth_cells - 2]


def face_kernel(par_ref, u_lo, u_hi, d_lo, d_hi, m_lo, m_hi, p_ref, k_ref, send_a, send_b):
    @pl.when(par_ref[0] == 0)
    def _():
        pack_faces(u_lo, u_hi, d_lo, d_hi, m_lo, m_hi, p_ref, k_ref, send_b, send_a)

    @pl.when(par_ref[0] == 1)
    def _():
        pack_faces(u_lo, u_hi, d_lo, d_hi, m_lo, m_hi, p_ref, k_ref, send_a, send_b)


def pack_faces(u_lo, u_hi, d_lo, d_hi, m_lo, m_hi, p_ref, k_ref, lo_out, hi_out):
    depth_cells = u_lo.shape[0]
    tile_cells = p_ref.shape[0]
    dz = 4 * depth_cells
    for z in range(depth_cells):
        for out, u_b, d_b, m_b, rows, edge in ((lo_out, u_lo, d_lo, m_lo, slice(0, 2), 0), (hi_out, u_hi, d_hi, m_hi, slice(6, 8), 7)):
            out[2 * z:2 * z + 2] = u_b[z, rows]
            dk = d_b[z, rows]
            out[2 * depth_cells + 2 * z:2 * depth_cells + 2 * z + 2] = ((1.0 - dk) ** 2 + 0.001) * m_b[z, rows]
            out[dz + z:dz + z + 1] = d_b[z, edge:edge + 1]
    lo_out[dz + depth_cells:dz + depth_cells + 2] = p_ref[0:2]
    lo_out[dz + depth_cells + 2:dz + depth_cells + 4] = k_ref[0:2].astype(jnp.float32)
    hi_out[dz + depth_cells:dz + depth_cells + 2] = p_ref[tile_cells - 2:tile_cells]
    hi_out[dz + depth_cells + 2:dz + depth_cells + 4] = k_ref[tile_cells - 2:tile_cells].astype(jnp.float32)


def depth_pack_kernel(depth_cells, par_ref, u_lo, u_hi, d_lo, d_hi, m_lo, m_hi, xlo_ref, xhi_ref, send_a, send_b):
    @pl.when(par_ref[0] == 0)
    def _():
        pack_depth(depth_cells, u_lo, d_lo, m_lo, xlo_ref, xhi_ref, send_b, 0, 1, 0)
        pack_depth(depth_cells, u_hi, d_hi, m_hi, xlo_ref, xhi_ref, send_a, 3, 2, depth_cells - 1)

    @pl.when(par_ref[0] == 1)
    def _():
        pack_depth(depth_cells, u_lo, d_lo, m_lo, xlo_ref, xhi_ref, send_a, 0, 1, 0)
        pack_depth(depth_cells, u_hi, d_hi, m_hi, xlo_ref, xhi_ref, send_b, 3, 2, depth_cells - 1)


def pack_depth(depth_cells, u_b, d_b, m_b, xlo_ref, xhi_ref, out, adj, sec, adj_z):
    tile_cells = u_b.shape[1]
    ext = tile_cells + 2
    c0 = 2 * depth_cells
    d_adj = d_b[adj]
    d_sec = d_b[sec]
    out[0:1] = xlo_ref[2 * adj_z + 1:2 * adj_z + 2]
    out[1:1 + tile_cells] = u_b[adj]
    out[1 + tile_cells:ext] = xhi_ref[2 * adj_z:2 * adj_z + 1]
    out[ext:ext + 1] = xlo_ref[c0 + 2 * adj_z + 1:c0 + 2 * adj_z + 2]
    out[ext + 1:ext + 1 + tile_cells] = ((1.0 - d_adj) ** 2 + 0.001) * m_b[adj]
    out[ext + 1 + tile_cells:2 * ext] = xhi_ref[c0 + 2 * adj_z:c0 + 2 * adj_z + 1]
    out[2 * ext:2 * ext + tile_cells] = u_b[sec]
    out[2 * ext + tile_cells:2 * ext + 2 * tile_cells] = ((1.0 - d_sec) ** 2 + 0.001) * m_b[sec]
    out[2 * ext + 2 * tile_cells:2 * ext + 3 * tile_cells] = d_adj


class Ends:
    def __init__(self, lo, hi, depth_cells):
        self.lo, self.hi, self.depth_cells = lo, hi, depth_cells

    def __getitem__(self, z):
        return self.lo[z] if z < 4 else self.hi[z - self.depth_cells + 4]


def boundary_kernel(total_depth, total_rows, depth_cells, ids_ref, u_lo, u_hi, d_lo, d_hi, mod_lo, mod_hi, tgh_lo,
                    tgh_hi, xlo_ref, xhi_ref, zlo_ref, zhi_ref, edge_ref, part_ref, load_ref, out_ref, u_s, c_s, d_s,
                    m_s):
    u_ref = Ends(u_lo, u_hi, depth_cells)
    dmg_ref = Ends(d_lo, d_hi, depth_cells)
    mod_ref = Ends(mod_lo, mod_hi, depth_cells)
    tgh_ref = Ends(tgh_lo, tgh_hi, depth_cells)
    _, tile_cells, width = u_lo.shape
    rows_all = u_s.shape[1]
    own = slice(X0, X0 + tile_cells)
    wide = slice(X0 - 1, X0 + tile_cells + 1)
    top = X0 + tile_cells
    zero = jnp.zeros((rows_all, width), jnp.float32)
    for j in range(8):
        u_s[j] = zero
        c_s[j] = zero
        d_s[j] = zero
    ext = tile_cells + 2
    for side, ref, adj, sec in ((0, zlo_ref, 1, 0), (4, zhi_ref, 6, 7)):
        u_s[adj, wide] = ref[0:ext]
        c_s[adj, wide] = ref[ext:2 * ext]
        u_s[sec, own] = ref[2 * ext:2 * ext + tile_cells]
        c_s[sec, own] = ref[2 * ext + tile_cells:2 * ext + 2 * tile_cells]
    d_s[0, own] = zlo_ref[2 * ext + 2 * tile_cells:2 * ext + 3 * tile_cells]
    d_s[7, own] = zhi_ref[2 * ext + 2 * tile_cells:2 * ext + 3 * tile_cells]
    dz = 4 * depth_cells
    for slot, z in ((2, 0), (3, 1), (4, depth_cells - 2), (5, depth_cells - 1)):
        dk = dmg_ref[z]
        u_s[slot, own] = u_ref[z]
        c_s[slot, own] = ((1.0 - dk) ** 2 + 0.001) * mod_ref[z]
        u_s[slot, X0 - 2:X0] = xlo_ref[2 * z:2 * z + 2]
        c_s[slot, X0 - 2:X0] = xlo_ref[2 * depth_cells + 2 * z:2 * depth_cells + 2 * z + 2]
        u_s[slot, top:top + 2] = xhi_ref[2 * z:2 * z + 2]
        c_s[slot, top:top + 2] = xhi_ref[2 * depth_cells + 2 * z:2 * depth_cells + 2 * z + 2]
    for slot, z in ((1, 0), (2, 1), (5, depth_cells - 2), (6, depth_cells - 1)):
        d_s[slot, own] = dmg_ref[z]
        d_s[slot, X0 - 1:X0] = xlo_ref[dz + z:dz + z + 1]
        d_s[slot, top:top + 1] = xhi_ref[dz + z:dz + z + 1]
    d_s[3, own] = dmg_ref[2]
    d_s[4, own] = dmg_ref[depth_cells - 3]
    m_s[2] = edge_ref[0]
    m_s[3] = edge_ref[1]
    m_s[4] = edge_ref[2]
    m_s[5] = edge_ref[3]

    nb = neighbours(rows_all, width)
    x_in = x_frame(ids_ref, rows_all, width, total_rows)
    load = load_ref[...]
    depth_start = ids_ref[0]
    for us, ms, z in ((1, 0, -1), (2, 1, 0), (5, 6, depth_cells - 1), (6, 7, depth_cells)):
        m_s[ms] = moved_at(
            u_s[us], c_s[us], (c_s[us + 1], u_s[us + 1]), (c_s[us - 1], u_s[us - 1]), nb, depth_start + z, load, x_in,
            total_depth,
        )
    acc = part_ref[...]
    for ms, z in ((1, 0), (2, 1), (5, depth_cells - 2), (6, depth_cells - 1)):
        acc = acc + opening_at(
            m_s[ms], m_s[ms + 1], m_s[ms - 1], d_s[ms], d_s[ms + 1], d_s[ms - 1], nb, mod_ref[z], tgh_ref[z],
            dmg_ref[z], own,
        )
    out_ref[...] = (4.0 / total_depth) * acc


def on_device(displacement, damage, modulus, toughness, pressure, crack_mask, wells, rates):
    depth_cells, tile_cells, width = displacement.shape
    total_depth = depth_cells * lax.axis_size("depth")
    total_rows = tile_cells * lax.axis_size("tile")
    depth_start = lax.axis_index("depth") * depth_cells
    tile_start = lax.axis_index("tile") * tile_cells
    mask_f = crack_mask.astype(jnp.float32)
    rows_all = tile_cells + 2 * X0

    def stiff_of(dmg, mod):
        return ((1.0 - dmg) ** 2 + 0.001) * mod

    vmem = pl.BlockSpec(memory_space=pltpu.VMEM)
    smem = pl.BlockSpec(memory_space=pltpu.SMEM)
    f32 = jnp.float32
    rows_lo = pl.BlockSpec((depth_cells, 8, width), lambda i: (0, 0, 0))
    rows_hi = pl.BlockSpec((depth_cells, 8, width), lambda i: (0, tile_cells // 8 - 1, 0))
    face_rows = 5 * depth_cells + 4
    parity = (lax.axis_index("tile") % 2).astype(jnp.int32).reshape(1)
    send_a, send_b = pl.pallas_call(
        face_kernel,
        out_shape=(jax.ShapeDtypeStruct((face_rows, width), f32),) * 2,
        grid=(1,),
        in_specs=[smem] + [rows_lo, rows_hi] * 3 + [vmem, vmem],
        out_specs=(vmem, vmem),
    )(parity, displacement, displacement, damage, damage, modulus, modulus, pressure, crack_mask)
    tiles = lax.axis_size("tile")
    even_x = lax.axis_index("tile") % 2 == 0
    got_a = lax.ppermute(send_a, "tile", [(i, i ^ 1) for i in range(tiles)])
    got_b = lax.ppermute(
        send_b, "tile", [(i, i + 1) for i in range(1, tiles - 1, 2)] + [(i + 1, i) for i in range(1, tiles - 1, 2)]
    )
    lo_x, hi_x = jnp.where(even_x, got_b, got_a), jnp.where(even_x, got_a, got_b)
    dz = 4 * depth_cells
    p_ext = jnp.concatenate([lo_x[dz + depth_cells:dz + depth_cells + 2], pressure, hi_x[dz + depth_cells:dz + depth_cells + 2]])
    m_ext = jnp.concatenate([lo_x[dz + depth_cells + 2:], mask_f, hi_x[dz + depth_cells + 2:]])
    load_all = jnp.pad(4.0 * m_ext[1:-1] * p_ext[1:-1], ((X0 - 1, X0 - 1), (0, 0)))
    ids = jnp.stack([depth_start, tile_start]).astype(jnp.int32)

    layers_lo = pl.BlockSpec((4, tile_cells, width), lambda i: (0, 0, 0))
    layers_hi = pl.BlockSpec((4, tile_cells, width), lambda i: (depth_cells // 4 - 1, 0, 0))
    depths = lax.axis_size("depth")
    parity_z = (lax.axis_index("depth") % 2).astype(jnp.int32).reshape(1)
    zsend_a, zsend_b = pl.pallas_call(
        functools.partial(depth_pack_kernel, depth_cells),
        out_shape=(jax.ShapeDtypeStruct((2 * (tile_cells + 2) + 3 * tile_cells, width), f32),) * 2,
        grid=(1,),
        in_specs=[smem] + [layers_lo, layers_hi] * 3 + [vmem, vmem],
        out_specs=(vmem, vmem),
    )(parity_z, displacement, displacement, damage, damage, modulus, modulus, lo_x, hi_x)
    even_z = lax.axis_index("depth") % 2 == 0
    zgot_a = lax.ppermute(zsend_a, "depth", [(i, i ^ 1) for i in range(depths)])
    zgot_b = lax.ppermute(
        zsend_b, "depth", [(i, i + 1) for i in range(1, depths - 1, 2)] + [(i + 1, i) for i in range(1, depths - 1, 2)]
    )
    lo_z, hi_z = jnp.where(even_z, zgot_b, zgot_a), jnp.where(even_z, zgot_a, zgot_b)

    vmem = pl.BlockSpec(memory_space=pltpu.VMEM)
    smem = pl.BlockSpec(memory_space=pltpu.SMEM)
    f32 = jnp.float32
    part_in, edge = pl.pallas_call(
        functools.partial(interior_kernel, total_depth, total_rows),
        out_shape=(
            jax.ShapeDtypeStruct((tile_cells, width), f32),
            jax.ShapeDtypeStruct((4, rows_all, width), f32),
        ),
        in_specs=[smem] + [vmem] * 7,
        out_specs=(vmem, vmem),
        scratch_shapes=[pltpu.VMEM((depth_cells, rows_all, width), f32)] * 4,
    )(ids, displacement, damage, modulus, toughness, lo_x, hi_x, load_all)
    end_lo = pl.BlockSpec((4, tile_cells, width), lambda i: (0, 0, 0))
    end_hi = pl.BlockSpec((4, tile_cells, width), lambda i: (depth_cells // 4 - 1, 0, 0))
    partial_open = pl.pallas_call(
        functools.partial(boundary_kernel, total_depth, total_rows, depth_cells),
        out_shape=jax.ShapeDtypeStruct((tile_cells, width), f32),
        grid=(1,),
        in_specs=[smem] + [end_lo, end_hi] * 4 + [vmem] * 7,
        out_specs=vmem,
        scratch_shapes=[pltpu.VMEM((8, rows_all, width), f32)] * 4,
    )(ids, displacement, displacement, damage, damage, modulus, modulus, toughness, toughness, lo_x, hi_x, lo_z, hi_z,
      edge, part_in, load_all)

    aperture = 0.5 + butterfly_sum(partial_open, "depth")
    trans = mask_f * aperture**3

    t_lo, t_hi = halo_swap(trans[:2], trans[-2:], "tile")
    t_ext = jnp.concatenate([t_lo, trans, t_hi])
    x_ids = tile_start - 1 + jnp.arange(tile_cells + 2, dtype=jnp.int32)
    rows_in = ((x_ids >= 0) & (x_ids < total_rows))[:, None]
    src_ext = well_source(wells, rates, tile_start - 1, tile_cells + 2, width, width)
    k_pad = pad_last(t_ext)
    level = plane_sweep(pad_last(p_ext), k_pad, p_ext[1:-1], src_ext, t_ext[1:-1])
    level = jnp.where(rows_in, level, jnp.float32(0.0))
    return plane_sweep(pad_last(level), k_pad[1:-1], pressure, src_ext[1:-1], trans)


def solution(mesh):
    return jax.shard_map(
        on_device,
        mesh=mesh,
        in_specs=(
            P("depth", "tile", None),
            P("depth", "tile", None),
            P("depth", "tile", None),
            P("depth", "tile", None),
            P("tile", None),
            P("tile", None),
            P(),
            P(),
        ),
        out_specs=P("tile", None),
        check_vma=False,
    )
```

```python
import functools

import jax
import jax.numpy as jnp
from jax import lax
from jax.experimental import pallas as pl
from jax.experimental.pallas import tpu as pltpu
from jax.sharding import PartitionSpec as P


def halo_swap(lo_face, hi_face, axis):
    count = lax.axis_size(axis)
    even = lax.axis_index(axis) % 2 == 0
    pairs_a = [(i, i ^ 1) for i in range(count)]
    pairs_b = [(i, i + 1) for i in range(1, count - 1, 2)] + [(i + 1, i) for i in range(1, count - 1, 2)]
    got_a = lax.ppermute(jnp.where(even, hi_face, lo_face), axis, pairs_a)
    got_b = lax.ppermute(jnp.where(even, lo_face, hi_face), axis, pairs_b)
    return jnp.where(even, got_b, got_a), jnp.where(even, got_a, got_b)


def butterfly_sum(part, axis):
    count = lax.axis_size(axis)
    order = [1 << k for k in range(1, count.bit_length() - 1)] + [1]
    for step in order:
        pairs = [(i, i ^ step) for i in range(lax.axis_size(axis))]
        part = part + lax.ppermute(part, axis, pairs)
    return part


def pad_last(stacked):
    widths = [(0, 0)] * (stacked.ndim - 1) + [(1, 1)]
    return jnp.pad(stacked, widths)


def flat_sides(padded):
    return [padded[2:, 1:-1], padded[:-2, 1:-1], padded[1:-1, 2:], padded[1:-1, :-2]]


def plane_sweep(p_pad, k_pad, anchor, source, trans):
    coef = jnp.zeros_like(trans)
    flow = jnp.zeros_like(trans)
    for k_side, p_side in zip(flat_sides(k_pad), flat_sides(p_pad)):
        face = 0.5 * (trans + k_side)
        coef = coef + face
        flow = flow + face * p_side
    return (anchor + source + flow) / (1.0 + coef)


def well_source(wells, rates, row_start, rows, cols, width):
    row_ids = row_start + jnp.arange(rows, dtype=jnp.int32)
    col_ids = jnp.arange(cols, dtype=jnp.int32)
    flat = row_ids[:, None] * width + col_ids[None, :]
    hit = flat[:, :, None] == wells[None, None, :]
    return 4.0 * jnp.sum(jnp.where(hit, rates[None, None, :], jnp.float32(0.0)), axis=-1)


def cube_sides(padded):
    return [
        padded[2:, 1:-1, 1:-1],
        padded[:-2, 1:-1, 1:-1],
        padded[1:-1, 2:, 1:-1],
        padded[1:-1, :-2, 1:-1],
        padded[1:-1, 1:-1, 2:],
        padded[1:-1, 1:-1, :-2],
    ]


X0 = 8


def neighbours(rows_all, width):
    col = lax.broadcasted_iota(jnp.int32, (rows_all, width), 1)
    has_next = col < width - 1
    has_prev = col > 0

    def y_next(a):
        return jnp.where(has_next, pltpu.roll(a, width - 1, 1), 0.0)

    def y_prev(a):
        return jnp.where(has_prev, pltpu.roll(a, 1, 1), 0.0)

    def x_next(a):
        return pltpu.roll(a, rows_all - 1, 0)

    def x_prev(a):
        return pltpu.roll(a, 1, 0)

    return x_next, x_prev, y_next, y_prev


def moved_at(uc, cc, up, down, nb, z_glob, load, x_in, total_depth):
    x_next, x_prev, y_next, y_prev = nb
    pairs = [
        up,
        down,
        (x_next(cc), x_next(uc)),
        (x_prev(cc), x_prev(uc)),
        (y_next(cc), y_next(uc)),
        (y_prev(cc), y_prev(uc)),
    ]
    coef = jnp.zeros_like(uc)
    flux = jnp.zeros_like(uc)
    for cn, un in pairs:
        face = 0.5 * (cc + cn)
        coef = coef + face
        flux = flux + face * (un - uc)
    force = jnp.where(z_glob == total_depth // 2, load, 0.0)
    moved = uc + 0.8 * (force + flux) / coef
    keep = x_in & (z_glob >= 0) & (z_glob < total_depth)
    return jnp.where(keep, moved, 0.0)


def opening_at(mc, m_up, m_down, dc, d_up, d_down, nb, mod, tough, dmg, own):
    x_next, x_prev, y_next, y_prev = nb
    energy = (
        (m_up - mc) ** 2 + (m_down - mc) ** 2 + (x_next(mc) - mc) ** 2 + (x_prev(mc) - mc) ** 2
        + (y_next(mc) - mc) ** 2 + (y_prev(mc) - mc) ** 2
    )
    beside = d_up + d_down + x_next(dc) + x_prev(dc) + y_next(dc) + y_prev(dc)
    energy = 0.25 * mod * energy[own]
    trial = (2.0 * energy + tough * beside[own]) / (7.0 * tough + 2.0 * energy)
    new_damage = jnp.maximum(dmg, trial)
    mo = mc[own]
    return new_damage * mo * mo


def x_frame(ids_ref, rows_all, width, total_rows):
    row = lax.broadcasted_iota(jnp.int32, (rows_all, width), 0)
    x_glob = ids_ref[1] + row - X0
    return (x_glob >= 0) & (x_glob < total_rows)


def interior_kernel(total_depth, total_rows, ids_ref, u_ref, dmg_ref, mod_ref, tgh_ref, xlo_ref, xhi_ref, load_ref,
                    part_ref, edge_ref, u_s, c_s, d_s, m_s):
    depth_cells, tile_cells, width = u_ref.shape
    rows_all = u_s.shape[1]
    own = slice(X0, X0 + tile_cells)
    top = X0 + tile_cells
    zero = jnp.zeros((rows_all, width), jnp.float32)

    def place(k, carry):
        dk = dmg_ref[k]
        u_s[k] = zero
        c_s[k] = zero
        d_s[k] = zero
        u_s[k, own] = u_ref[k]
        c_s[k, own] = ((1.0 - dk) ** 2 + 0.001) * mod_ref[k]
        d_s[k, own] = dk
        return carry

    lax.fori_loop(0, depth_cells, place, 0)
    dz = 4 * depth_cells
    for z in range(depth_cells):
        u_s[z, X0 - 2:X0] = xlo_ref[2 * z:2 * z + 2]
        c_s[z, X0 - 2:X0] = xlo_ref[2 * depth_cells + 2 * z:2 * depth_cells + 2 * z + 2]
        d_s[z, X0 - 1:X0] = xlo_ref[dz + z:dz + z + 1]
        u_s[z, top:top + 2] = xhi_ref[2 * z:2 * z + 2]
        c_s[z, top:top + 2] = xhi_ref[2 * depth_cells + 2 * z:2 * depth_cells + 2 * z + 2]
        d_s[z, top:top + 1] = xhi_ref[dz + z:dz + z + 1]

    nb = neighbours(rows_all, width)
    x_in = x_frame(ids_ref, rows_all, width, total_rows)
    load = load_ref[...]
    depth_start = ids_ref[0]

    def moved_body(k, carry):
        m_s[k] = moved_at(
            u_s[k], c_s[k], (c_s[k + 1], u_s[k + 1]), (c_s[k - 1], u_s[k - 1]), nb, depth_start + k, load, x_in,
            total_depth,
        )
        return carry

    lax.fori_loop(1, depth_cells - 1, moved_body, 0)

    def open_body(k, acc):
        return acc + opening_at(
            m_s[k], m_s[k + 1], m_s[k - 1], d_s[k], d_s[k + 1], d_s[k - 1], nb, mod_ref[k], tgh_ref[k], dmg_ref[k], own
        )

    acc = lax.fori_loop(2, depth_cells - 2, open_body, jnp.zeros((tile_cells, width), jnp.float32))
    part_ref[...] = acc
    edge_ref[0] = m_s[1]
    edge_ref[1] = m_s[2]
    edge_ref[2] = m_s[depth_cells - 3]
    edge_ref[3] = m_s[depth_cells - 2]


def face_kernel(par_ref, u_lo, u_hi, d_lo, d_hi, m_lo, m_hi, p_ref, k_ref, send_a, send_b):
    @pl.when(par_ref[0] == 0)
    def _():
        pack_faces(u_lo, u_hi, d_lo, d_hi, m_lo, m_hi, p_ref, k_ref, send_b, send_a)

    @pl.when(par_ref[0] == 1)
    def _():
        pack_faces(u_lo, u_hi, d_lo, d_hi, m_lo, m_hi, p_ref, k_ref, send_a, send_b)


def pack_faces(u_lo, u_hi, d_lo, d_hi, m_lo, m_hi, p_ref, k_ref, lo_out, hi_out):
    depth_cells = u_lo.shape[0]
    tile_cells = p_ref.shape[0]
    dz = 4 * depth_cells
    for z in range(depth_cells):
        for out, u_b, d_b, m_b, rows, edge in ((lo_out, u_lo, d_lo, m_lo, slice(0, 2), 0), (hi_out, u_hi, d_hi, m_hi, slice(6, 8), 7)):
            out[2 * z:2 * z + 2] = u_b[z, rows]
            dk = d_b[z, rows]
            out[2 * depth_cells + 2 * z:2 * depth_cells + 2 * z + 2] = ((1.0 - dk) ** 2 + 0.001) * m_b[z, rows]
            out[dz + z:dz + z + 1] = d_b[z, edge:edge + 1]
    lo_out[dz + depth_cells:dz + depth_cells + 2] = p_ref[0:2]
    lo_out[dz + depth_cells + 2:dz + depth_cells + 4] = k_ref[0:2].astype(jnp.float32)
    hi_out[dz + depth_cells:dz + depth_cells + 2] = p_ref[tile_cells - 2:tile_cells]
    hi_out[dz + depth_cells + 2:dz + depth_cells + 4] = k_ref[tile_cells - 2:tile_cells].astype(jnp.float32)


class Ends:
    def __init__(self, lo, hi, depth_cells):
        self.lo, self.hi, self.depth_cells = lo, hi, depth_cells

    def __getitem__(self, z):
        return self.lo[z] if z < 4 else self.hi[z - self.depth_cells + 4]


def boundary_kernel(total_depth, total_rows, depth_cells, ids_ref, u_lo, u_hi, d_lo, d_hi, mod_lo, mod_hi, tgh_lo,
                    tgh_hi, xlo_ref, xhi_ref, zlo_ref, zhi_ref, edge_ref, part_ref, load_ref, out_ref, u_s, c_s, d_s,
                    m_s):
    u_ref = Ends(u_lo, u_hi, depth_cells)
    dmg_ref = Ends(d_lo, d_hi, depth_cells)
    mod_ref = Ends(mod_lo, mod_hi, depth_cells)
    tgh_ref = Ends(tgh_lo, tgh_hi, depth_cells)
    _, tile_cells, width = u_lo.shape
    rows_all = u_s.shape[1]
    own = slice(X0, X0 + tile_cells)
    wide = slice(X0 - 1, X0 + tile_cells + 1)
    top = X0 + tile_cells
    zero = jnp.zeros((rows_all, width), jnp.float32)
    for j in range(8):
        u_s[j] = zero
        c_s[j] = zero
        d_s[j] = zero
    ext = tile_cells + 2
    def place_halo(lo_ref, hi_ref):
        for ref, adj, sec in ((lo_ref, 1, 0), (hi_ref, 6, 7)):
            u_s[adj, wide] = ref[0:ext]
            c_s[adj, wide] = ref[ext:2 * ext]
            u_s[sec, own] = ref[2 * ext:2 * ext + tile_cells]
            c_s[sec, own] = ref[2 * ext + tile_cells:2 * ext + 2 * tile_cells]
        d_s[0, own] = lo_ref[2 * ext + 2 * tile_cells:2 * ext + 3 * tile_cells]
        d_s[7, own] = hi_ref[2 * ext + 2 * tile_cells:2 * ext + 3 * tile_cells]

    @pl.when(ids_ref[2] == 0)
    def _():
        place_halo(zhi_ref, zlo_ref)

    @pl.when(ids_ref[2] == 1)
    def _():
        place_halo(zlo_ref, zhi_ref)

    dz = 4 * depth_cells
    for slot, z in ((2, 0), (3, 1), (4, depth_cells - 2), (5, depth_cells - 1)):
        dk = dmg_ref[z]
        u_s[slot, own] = u_ref[z]
        c_s[slot, own] = ((1.0 - dk) ** 2 + 0.001) * mod_ref[z]
        u_s[slot, X0 - 2:X0] = xlo_ref[2 * z:2 * z + 2]
        c_s[slot, X0 - 2:X0] = xlo_ref[2 * depth_cells + 2 * z:2 * depth_cells + 2 * z + 2]
        u_s[slot, top:top + 2] = xhi_ref[2 * z:2 * z + 2]
        c_s[slot, top:top + 2] = xhi_ref[2 * depth_cells + 2 * z:2 * depth_cells + 2 * z + 2]
    for slot, z in ((1, 0), (2, 1), (5, depth_cells - 2), (6, depth_cells - 1)):
        d_s[slot, own] = dmg_ref[z]
        d_s[slot, X0 - 1:X0] = xlo_ref[dz + z:dz + z + 1]
        d_s[slot, top:top + 1] = xhi_ref[dz + z:dz + z + 1]
    d_s[3, own] = dmg_ref[2]
    d_s[4, own] = dmg_ref[depth_cells - 3]
    m_s[2] = edge_ref[0]
    m_s[3] = edge_ref[1]
    m_s[4] = edge_ref[2]
    m_s[5] = edge_ref[3]

    nb = neighbours(rows_all, width)
    x_in = x_frame(ids_ref, rows_all, width, total_rows)
    load = load_ref[...]
    depth_start = ids_ref[0]
    for us, ms, z in ((1, 0, -1), (2, 1, 0), (5, 6, depth_cells - 1), (6, 7, depth_cells)):
        m_s[ms] = moved_at(
            u_s[us], c_s[us], (c_s[us + 1], u_s[us + 1]), (c_s[us - 1], u_s[us - 1]), nb, depth_start + z, load, x_in,
            total_depth,
        )
    acc = part_ref[...]
    for ms, z in ((1, 0), (2, 1), (5, depth_cells - 2), (6, depth_cells - 1)):
        acc = acc + opening_at(
            m_s[ms], m_s[ms + 1], m_s[ms - 1], d_s[ms], d_s[ms + 1], d_s[ms - 1], nb, mod_ref[z], tgh_ref[z],
            dmg_ref[z], own,
        )
    out_ref[...] = (4.0 / total_depth) * acc


def on_device(displacement, damage, modulus, toughness, pressure, crack_mask, wells, rates):
    depth_cells, tile_cells, width = displacement.shape
    total_depth = depth_cells * lax.axis_size("depth")
    total_rows = tile_cells * lax.axis_size("tile")
    depth_start = lax.axis_index("depth") * depth_cells
    tile_start = lax.axis_index("tile") * tile_cells
    mask_f = crack_mask.astype(jnp.float32)
    rows_all = tile_cells + 2 * X0

    def stiff_of(dmg, mod):
        return ((1.0 - dmg) ** 2 + 0.001) * mod

    vmem = pl.BlockSpec(memory_space=pltpu.VMEM)
    smem = pl.BlockSpec(memory_space=pltpu.SMEM)
    f32 = jnp.float32
    rows_lo = pl.BlockSpec((depth_cells, 8, width), lambda i: (0, 0, 0))
    rows_hi = pl.BlockSpec((depth_cells, 8, width), lambda i: (0, tile_cells // 8 - 1, 0))
    face_rows = 5 * depth_cells + 4
    parity = (lax.axis_index("tile") % 2).astype(jnp.int32).reshape(1)
    send_a, send_b = pl.pallas_call(
        face_kernel,
        out_shape=(jax.ShapeDtypeStruct((face_rows, width), f32),) * 2,
        grid=(1,),
        in_specs=[smem] + [rows_lo, rows_hi] * 3 + [vmem, vmem],
        out_specs=(vmem, vmem),
    )(parity, displacement, displacement, damage, damage, modulus, modulus, pressure, crack_mask)
    tiles = lax.axis_size("tile")
    even_x = lax.axis_index("tile") % 2 == 0
    got_a = lax.ppermute(send_a, "tile", [(i, i ^ 1) for i in range(tiles)])
    got_b = lax.ppermute(
        send_b, "tile", [(i, i + 1) for i in range(1, tiles - 1, 2)] + [(i + 1, i) for i in range(1, tiles - 1, 2)]
    )
    lo_x, hi_x = jnp.where(even_x, got_b, got_a), jnp.where(even_x, got_a, got_b)
    dz = 4 * depth_cells
    p_ext = jnp.concatenate([lo_x[dz + depth_cells:dz + depth_cells + 2], pressure, hi_x[dz + depth_cells:dz + depth_cells + 2]])
    m_ext = jnp.concatenate([lo_x[dz + depth_cells + 2:], mask_f, hi_x[dz + depth_cells + 2:]])
    load_all = jnp.pad(4.0 * m_ext[1:-1] * p_ext[1:-1], ((X0 - 1, X0 - 1), (0, 0)))
    ids = jnp.stack([depth_start, tile_start, lax.axis_index("depth") % 2]).astype(jnp.int32)

    def depth_face(adj, sec):
        u_adj = jnp.concatenate([lo_x[2 * adj + 1:2 * adj + 2], displacement[adj], hi_x[2 * adj:2 * adj + 1]])
        c0 = 2 * depth_cells
        c_adj = jnp.concatenate(
            [lo_x[c0 + 2 * adj + 1:c0 + 2 * adj + 2], stiff_of(damage[adj], modulus[adj]), hi_x[c0 + 2 * adj:c0 + 2 * adj + 1]]
        )
        return jnp.concatenate([u_adj, c_adj, displacement[sec], stiff_of(damage[sec], modulus[sec]), damage[adj]])

    depths = lax.axis_size("depth")
    even_z = lax.axis_index("depth") % 2 == 0
    z_lo_face, z_hi_face = depth_face(0, 1), depth_face(depth_cells - 1, depth_cells - 2)
    zgot_a = lax.ppermute(jnp.where(even_z, z_hi_face, z_lo_face), "depth", [(i, i ^ 1) for i in range(depths)])
    zgot_b = lax.ppermute(
        jnp.where(even_z, z_lo_face, z_hi_face), "depth",
        [(i, i + 1) for i in range(1, depths - 1, 2)] + [(i + 1, i) for i in range(1, depths - 1, 2)],
    )

    vmem = pl.BlockSpec(memory_space=pltpu.VMEM)
    smem = pl.BlockSpec(memory_space=pltpu.SMEM)
    f32 = jnp.float32
    part_in, edge = pl.pallas_call(
        functools.partial(interior_kernel, total_depth, total_rows),
        out_shape=(
            jax.ShapeDtypeStruct((tile_cells, width), f32),
            jax.ShapeDtypeStruct((4, rows_all, width), f32),
        ),
        in_specs=[smem] + [vmem] * 7,
        out_specs=(vmem, vmem),
        scratch_shapes=[pltpu.VMEM((depth_cells, rows_all, width), f32)] * 4,
    )(ids, displacement, damage, modulus, toughness, lo_x, hi_x, load_all)
    end_lo = pl.BlockSpec((4, tile_cells, width), lambda i: (0, 0, 0))
    end_hi = pl.BlockSpec((4, tile_cells, width), lambda i: (depth_cells // 4 - 1, 0, 0))
    partial_open = pl.pallas_call(
        functools.partial(boundary_kernel, total_depth, total_rows, depth_cells),
        out_shape=jax.ShapeDtypeStruct((tile_cells, width), f32),
        grid=(1,),
        in_specs=[smem] + [end_lo, end_hi] * 4 + [vmem] * 7,
        out_specs=vmem,
        scratch_shapes=[pltpu.VMEM((8, rows_all, width), f32)] * 4,
    )(ids, displacement, displacement, damage, damage, modulus, modulus, toughness, toughness, lo_x, hi_x, zgot_a, zgot_b,
      edge, part_in, load_all)

    aperture = 0.5 + butterfly_sum(partial_open, "depth")
    trans = mask_f * aperture**3

    t_lo, t_hi = halo_swap(trans[:2], trans[-2:], "tile")
    t_ext = jnp.concatenate([t_lo, trans, t_hi])
    x_ids = tile_start - 1 + jnp.arange(tile_cells + 2, dtype=jnp.int32)
    rows_in = ((x_ids >= 0) & (x_ids < total_rows))[:, None]
    src_ext = well_source(wells, rates, tile_start - 1, tile_cells + 2, width, width)
    k_pad = pad_last(t_ext)
    level = plane_sweep(pad_last(p_ext), k_pad, p_ext[1:-1], src_ext, t_ext[1:-1])
    level = jnp.where(rows_in, level, jnp.float32(0.0))
    return plane_sweep(pad_last(level), k_pad[1:-1], pressure, src_ext[1:-1], trans)


def solution(mesh):
    return jax.shard_map(
        on_device,
        mesh=mesh,
        in_specs=(
            P("depth", "tile", None),
            P("depth", "tile", None),
            P("depth", "tile", None),
            P("depth", "tile", None),
            P("tile", None),
            P("tile", None),
            P(),
            P(),
        ),
        out_specs=P("tile", None),
        check_vma=False,
    )
```
